32 devices in a mesh: pert: 8 (over y, x, core), gx: 4 (over z).
Axes of the slice: x: 2, y: 2, z: 4, core: 2. Of those that a mesh axis runs over, the one named last changes fastest.
Arguments:
- pert_field: float32 [8, 3, 1024, 8, 1024], P('pert', None, 'gx'), may hold values from -6 to 6
- base_store: bfloat16 [8, 3, 1024, 8, 1024], P('pert', None, 'gx'), may hold values from -6 to 6
- section_owner: int32 [1], replicated, may hold values from 0 to 7
- pert_ids: int32 [8], P('pert'), may hold values from 0 to 63
- member_visc: float32 [64], replicated, may hold values from 0.05 to 0.5
Outputs:
- section_field: float32 [8, 3, 1024, 2, 1024], P('pert', None, 'gx')
The draws below stay inside these ranges and needn't reach their ends.
All inputs are finite; a program needn't handle non-finite values.
Results may differ from the reference program's by a relative error of at most 0.0003.
Values may be sent and summed in bfloat16 or wider, within the bound.
No kernel may reach another device: no remote copies, remote signals or barrier semaphores. Data moves between devices by JAX's collectives and lax.ppermute only.
A program may use at most 320 MiB of HBM per device.

```python
import math
import jax
import jax.numpy as jnp
from jax import lax

NX = 1024
NY = 1024
NZ = 2
MEMBERS = 64
PERT = 8
LEVELS = 8
NZW = 8


def set_ends(values, stream_key, least, largest):
    index_at = [jax.random.randint(jax.random.fold_in(stream_key, axis), (), 0, length) for axis, length in enumerate(values.shape)]
    widest = values.shape.index(max(values.shape))
    next_to = index_at[:widest] + [(index_at[widest] + 1) % values.shape[widest]] + index_at[widest + 1:]
    return values.at[tuple(index_at)].set(least).at[tuple(next_to)].set(largest)


def levels(rng, shape, split, smallest, top_value):
    level = 1.0
    for position, blocks in split:
        steps = jax.random.uniform(jax.random.fold_in(jax.random.fold_in(rng, 6), position), (blocks,), jnp.float32, smallest / len(split), top_value / len(split))
        level = level * jnp.repeat(jnp.exp(steps), shape[position] // blocks).reshape((-1,) + (1,) * (len(shape) - 1 - position))
    return level


def centred(stream_key, dims, scale, bound, shards=(), kind=jnp.bfloat16):
    result = jax.random.normal(stream_key, dims, jnp.float32) * scale
    if len(shards) > 0:
        result = levels(stream_key, dims, shards, -0.22, 0.18) * result
    return jnp.clip(result, min=-bound, max=bound).astype(kind)


def setup_inputs(seed: int = 0) -> dict:
    seeds = jax.random.split(jax.random.key(seed), 6)
    return {
        "pert_field": centred(seeds[0], (PERT, 3, NX, NZW, NY), 1.0, 6.0, ((0, 8), (2, 4)), jnp.float32),
        "base_store": centred(seeds[1], (LEVELS, 3, NX, NZW, NY), 1.0, 6.0, ((0, 8), (2, 4))),
        "section_owner": jax.random.randint(seeds[2], (1,), 0, LEVELS).astype(jnp.int32),
        "pert_ids": set_ends(jax.random.randint(seeds[3], (PERT,), 0, MEMBERS), jax.random.fold_in(seeds[3], 1), 0, MEMBERS - 1).astype(jnp.int32),
        "member_visc": jnp.clip(jnp.exp(jax.random.uniform(seeds[4], (MEMBERS,), jnp.float32, math.log(0.05), math.log(0.5))), 0.05, 0.5),
    }


first_weights = (0.75, -0.15, 1.0 / 60.0)
second_weights = (1.5, -0.15, 1.0 / 90.0)
centre_second = -49.0 / 18.0
section_step = 0.25


def first_across(values, axis_number):
    summed = jnp.zeros_like(values)
    for offset_cells, weight in zip((1, 2, 3), first_weights):
        summed = summed + weight * (jnp.roll(values, -offset_cells, axis_number) - jnp.roll(values, offset_cells, axis_number))
    return summed


def second_across(values, axis_number):
    summed = centre_second * values
    for offset_cells, weight in zip((1, 2, 3), second_weights):
        summed = summed + weight * (jnp.roll(values, -offset_cells, axis_number) + jnp.roll(values, offset_cells, axis_number))
    return summed


def first_depth(values):
    summed = jnp.zeros_like(values[:, :, 3:3 + NZ])
    for offset_cells, weight in zip((1, 2, 3), first_weights):
        summed = summed + weight * (values[:, :, 3 + offset_cells:3 + offset_cells + NZ] - values[:, :, 3 - offset_cells:3 - offset_cells + NZ])
    return summed


def second_depth(values):
    summed = centre_second * values[:, :, 3:3 + NZ]
    for offset_cells, weight in zip((1, 2, 3), second_weights):
        summed = summed + weight * (values[:, :, 3 + offset_cells:3 + offset_cells + NZ] + values[:, :, 3 - offset_cells:3 - offset_cells + NZ])
    return summed


def compact_along(values):
    compact_rhs = (7.0 / 9.0) * (jnp.roll(values, -1, 1) - jnp.roll(values, 1, 1))
    compact_rhs = compact_rhs + (1.0 / 36.0) * (jnp.roll(values, -2, 1) - jnp.roll(values, 2, 1))
    wave_number = jnp.arange(NX).astype(jnp.float32)
    symbol = 1.0 + (2.0 / 3.0) * jnp.cos(2.0 * jnp.pi * wave_number / NX)
    spectrum = jnp.fft.fft(compact_rhs, axis=1) / symbol[None, :, None, None]
    return jnp.real(jnp.fft.ifft(spectrum, axis=1)).astype(jnp.float32)


def reference(pert_field, base_store, section_owner, pert_ids, member_visc):
    base_field = lax.dynamic_index_in_dim(base_store, section_owner[0], 0, keepdims=False).astype(jnp.float32)
    base_interior = base_field[:, :, 3:3 + NZ]
    base_along = compact_along(base_interior)
    base_across = first_across(base_interior, 3)
    base_depth = first_depth(base_field)

    def one_member(inputs):
        state_field, member = inputs
        viscosity = member_visc[member]
        interior = state_field[:, :, 3:3 + NZ]
        pert_along = compact_along(interior)
        pert_across = first_across(interior, 3)
        pert_depth = first_depth(state_field)
        laplacian = second_across(interior, 1) + second_across(interior, 3) + second_depth(state_field)
        advection = base_interior[0] * pert_along + base_interior[1] * pert_across + base_interior[2] * pert_depth
        stretching = interior[0] * base_along + interior[1] * base_across + interior[2] * base_depth
        return interior + section_step * (-advection - stretching + viscosity * laplacian)

    return lax.map(one_member, (pert_field, pert_ids))
```

```python
import functools

import jax
import jax.numpy as jnp
import numpy as np
from jax import lax
from jax.experimental import pallas as pl
from jax.experimental.pallas import tpu as pltpu
from jax.sharding import PartitionSpec as P

section_step = 0.25
reach = 16
code_scale = 4096.0
phases = 2
streams = ((0, 3), (1, 2))


def compact_kernel(length):
    wave = 2.0 * np.pi * np.arange(length) / length
    symbol = 14.0 / 9.0 * np.sin(wave) + 1.0 / 18.0 * np.sin(2.0 * wave)
    symbol = 1j * symbol / (1.0 + 2.0 / 3.0 * np.cos(wave))
    return np.real(np.fft.ifft(symbol))


def along_matrices(rows, length):
    kernel = compact_kernel(length)
    first = np.zeros((rows, rows + 2 * reach))
    second = np.zeros((rows, rows + 2 * reach))
    for i in range(rows):
        for k in range(-reach, reach + 1):
            first[i, i + reach + k] = kernel[-k % length]
        for k, weight in ((0, -980.0), (1, 270.0), (2, -27.0), (3, 2.0)):
            second[i, i + reach + k] = weight
            second[i, i + reach - k] = weight
    high = first.astype(jnp.bfloat16)
    low = (first - high.astype(np.float64)).astype(jnp.bfloat16)
    return high, low, second.astype(jnp.bfloat16)


first_taps = ((1, 45.0), (2, -9.0), (3, 1.0))
second_taps = ((0, -490.0), (1, 270.0), (2, -27.0), (3, 2.0))


def depth_matrix(rows, planes, fields):
    matrix = np.zeros((len(fields) * rows, rows * planes))
    for f, taps in enumerate(fields):
        for i in range(rows):
            for z, weight in taps:
                matrix[f * rows + i, i * planes + z] += weight
    return matrix.astype(jnp.bfloat16)


def first_at(z):
    return [(z + k, w) for k, w in first_taps] + [(z - k, -w) for k, w in first_taps]


def second_at(z):
    taps = [(z + k, w) for k, w in second_taps]
    return taps + [(z - k, w) for k, w in second_taps if k > 0]


def product(a, b):
    return jnp.dot(a, b, preferred_element_type=jnp.float32)


def split(values):
    high = values.astype(jnp.bfloat16)
    return high, (values - high.astype(jnp.float32)).astype(jnp.bfloat16)


def shifted_pairs(values):
    width = values.shape[-1]
    return [
        (pltpu.roll(values, width - k, 1), pltpu.roll(values, k, 1)) for k in (1, 2, 3)
    ]


def first_across(pairs):
    (u1, d1), (u2, d2), (u3, d3) = pairs
    return 0.75 * (u1 - d1) - 0.15 * (u2 - d2) + (1.0 / 60.0) * (u3 - d3)


def pack_kernel(weights, tile, coded):
    rows = coded.shape[2]
    mixed = product(weights[...], tile[0])
    for f in range(4):
        scale = code_scale if f < 2 else code_scale / 60.0
        part = jnp.round(mixed[f * rows : (f + 1) * rows] * scale)
        coded[0, f] = part.astype(jnp.int32).astype(jnp.int16)


def pack(tile, planes, x_rows):
    comps, deep, width = tile.shape
    slab = deep // planes
    ghost = [[t for t in first_at(z) if t[0] not in (3, 4)] for z in (3, 4)]
    weights = depth_matrix(x_rows, planes, [[(3, 1.0)], [(4, 1.0)]] + ghost)
    return pl.pallas_call(
        pack_kernel,
        out_shape=jax.ShapeDtypeStruct((comps, 4, slab, width), jnp.int16),
        grid=(comps, slab // x_rows),
        in_specs=[
            pl.BlockSpec(weights.shape, lambda c, i: (0, 0)),
            pl.BlockSpec((1, x_rows * planes, width), lambda c, i: (c, i, 0)),
        ],
        out_specs=pl.BlockSpec((1, 4, x_rows, width), lambda c, i: (c, 0, i, 0)),
        cost_estimate=pl.CostEstimate(
            flops=0, bytes_accessed=4 * comps * deep * width, transcendentals=0
        ),
    )(jnp.asarray(weights), tile)


def unpack_kernel(viscosity, weights, field, inner, depth, partial):
    rows = inner.shape[2]
    high, low = split(field[0])
    mixed = product(weights[...], high) + product(weights[...], low)
    gain = viscosity[0] * (section_step / 180.0)
    for p in range(2):
        value = mixed[p * rows : (p + 1) * rows]
        inner[0, p] = value
        depth[0, p] = mixed[(2 + p) * rows : (3 + p) * rows] * (1.0 / 60.0)
        partial[0, p] = value + gain * mixed[(4 + p) * rows : (5 + p) * rows]


def unpack(field, viscosity, planes, x_rows):
    comps, deep, width = field.shape
    slab = deep // planes
    fields = [[(3, 1.0)], [(4, 1.0)], first_at(3), first_at(4), second_at(3), second_at(4)]
    weights = depth_matrix(x_rows, planes, fields)
    shape = jax.ShapeDtypeStruct((comps, 2, slab, width), jnp.float32)
    spec = pl.BlockSpec((1, 2, x_rows, width), lambda c, i: (c, 0, i, 0))
    return pl.pallas_call(
        unpack_kernel,
        out_shape=(shape,) * 3,
        grid=(comps, slab // x_rows),
        in_specs=[
            pl.BlockSpec(memory_space=pltpu.SMEM),
            pl.BlockSpec(weights.shape, lambda c, i: (0, 0)),
            pl.BlockSpec((1, x_rows * planes, width), lambda c, i: (c, i, 0)),
        ],
        out_specs=(spec,) * 3,
        cost_estimate=pl.CostEstimate(
            flops=0, bytes_accessed=7 * comps * deep * width, transcendentals=0
        ),
    )(viscosity, jnp.asarray(weights), field)


def along_kernel(
    viscosity, m_top, m_low, inner, before, after, partial, along, across, sums, high_s, low_s, curve_s
):
    slab = inner.shape[2]
    rows = m_low.shape[0]

    def place(start, values):
        high, low = split(values)
        high_s[pl.ds(start, values.shape[0]), :] = high
        low_s[pl.ds(start, values.shape[0]), :] = low

    place(0, before[0, 0])
    place(reach + slab, after[0, 0])

    def fill(i, carry):
        start = pl.multiple_of(i * 32, 32)
        high, low = split(inner[0, 0, pl.ds(start, 32), :])
        at = pl.multiple_of(start + reach, 16)
        high_s[pl.ds(at, 32), :] = high
        low_s[pl.ds(at, 32), :] = low
        return carry

    lax.fori_loop(0, slab // 32, fill, 0)
    for b in range(slab // rows):
        window = pl.ds(b * rows, rows + 2 * reach)
        high, low = high_s[window, :], low_s[window, :]
        both = product(m_top[...], high) + product(m_top[...], low)
        along[0, 0, b * rows : (b + 1) * rows] = both[:rows] + product(m_low[...], high)
        curve_s[b * rows : (b + 1) * rows] = both[rows:]
    gain = viscosity[0] * section_step
    gain_along = viscosity[0] * (section_step / 180.0)

    def body(i, carry):
        at = pl.ds(pl.multiple_of(i * 16, 16), 16)
        pairs = shifted_pairs(inner[0, 0, at, :])
        across[0, 0, at, :] = first_across(pairs)
        (u1, d1), (u2, d2), (u3, d3) = pairs
        curve = 1.5 * (u1 + d1) - 0.15 * (u2 + d2) + (1.0 / 90.0) * (u3 + d3)
        sums[0, 0, at, :] = partial[0, 0, at, :] + gain * curve + gain_along * curve_s[at, :]
        return carry

    lax.fori_loop(0, slab // 16, body, 0)


def along_across(inner, before, after, partial, viscosity, length):
    comps, pair, slab, width = inner.shape
    rows = min(slab, 128)
    high, low, second = along_matrices(rows, length)
    top = np.concatenate([high, second], 0)
    shape = jax.ShapeDtypeStruct(inner.shape, jnp.float32)
    spec = pl.BlockSpec((1, 1, slab, width), lambda c, p: (c, p, 0, 0))
    rim = pl.BlockSpec((1, 1, reach, width), lambda c, p: (c, p, 0, 0))
    return pl.pallas_call(
        along_kernel,
        out_shape=(shape,) * 3,
        grid=(comps, pair),
        in_specs=[
            pl.BlockSpec(memory_space=pltpu.SMEM),
            pl.BlockSpec(top.shape, lambda c, p: (0, 0)),
            pl.BlockSpec(low.shape, lambda c, p: (0, 0)),
            spec,
            rim,
            rim,
            spec,
        ],
        out_specs=(spec,) * 3,
        scratch_shapes=[
            pltpu.VMEM((slab + 2 * reach, width), jnp.bfloat16),
            pltpu.VMEM((slab + 2 * reach, width), jnp.bfloat16),
            pltpu.VMEM((slab, width), jnp.float32),
        ],
        cost_estimate=pl.CostEstimate(
            flops=0, bytes_accessed=5 * 4 * inner.size, transcendentals=0
        ),
    )(viscosity, jnp.asarray(top), jnp.asarray(low), inner, before, after, partial)


def final_kernel(
    m_both, base, ghost, before, after, inner, along, across, depth, sums, out, base_s, slope_s
):
    step = pl.program_id(0)
    rows = inner.shape[2]
    slab = base.shape[2]
    inverse = 1.0 / code_scale

    def decoded(values):
        return values.astype(jnp.int32).astype(jnp.float32) * inverse

    @pl.when(step == 0)
    def _():
        for c in range(3):
            for p in range(2):
                base_s[c, p, 0:reach] = decoded(before[c, p]).astype(jnp.bfloat16)
                base_s[c, p, reach + slab :] = decoded(after[c, p]).astype(jnp.bfloat16)

                def fill(i, carry):
                    start = pl.multiple_of(i * 16, 16)
                    to = pl.multiple_of(start + reach, 16)
                    values = decoded(base[c, p, pl.ds(start, 16), :])
                    base_s[c, p, pl.ds(to, 16), :] = values.astype(jnp.bfloat16)
                    return carry

                lax.fori_loop(0, slab // 16, fill, 0)

    origin = pl.multiple_of(step * rows, 32)
    for c in range(3):
        for p in range(2):
            both = product(m_both[...], base_s[c, p, pl.ds(origin, rows + 2 * reach), :])
            slope_s[c, p] = both[:rows] + both[rows:]

    def body(i, carry):
        start = pl.multiple_of(i * 16, 16)
        at = pl.ds(start, 16)
        inside = pl.ds(pl.multiple_of(origin + reach + start, 16), 16)
        flow = [
            [base_s[c, p, inside, :].astype(jnp.float32) for p in range(2)] for c in range(3)
        ]
        for p in range(2):
            move = [inner[c, p, at, :] for c in range(3)]
            for c in range(3):
                dz = decoded(ghost[c, p, at, :])
                if p == 0:
                    dz = dz + 0.75 * flow[c][1]
                else:
                    dz = dz - 0.75 * flow[c][0]
                dy = first_across(shifted_pairs(flow[c][p]))
                total = flow[0][p] * along[c, p, at, :] + flow[1][p] * across[c, p, at, :]
                total = total + flow[2][p] * depth[c, p, at, :]
                total = total + move[0] * slope_s[c, p, at, :] + move[1] * dy + move[2] * dz
                out[0, c, at, p, :] = sums[c, p, at, :] - section_step * total
        return carry

    lax.fori_loop(0, rows // 16, body, 0)


def final(base, ghost, before, after, inner, along, across, depth, sums, length):
    comps, pair, slab, width = inner.shape
    rows = 32
    high, low, _ = along_matrices(rows, length)
    both = np.concatenate([high, low], 0)
    whole = pl.BlockSpec(base.shape, lambda i: (0, 0, 0, 0))
    rim = pl.BlockSpec(before.shape, lambda i: (0, 0, 0, 0))
    spec = pl.BlockSpec((comps, pair, rows, width), lambda i: (0, 0, i, 0))
    return pl.pallas_call(
        final_kernel,
        out_shape=jax.ShapeDtypeStruct((1, comps, slab, pair, width), jnp.float32),
        grid=(slab // rows,),
        in_specs=[pl.BlockSpec(both.shape, lambda i: (0, 0)), whole, spec, rim, rim] + [spec] * 5,
        out_specs=pl.BlockSpec((1, comps, rows, pair, width), lambda i: (0, 0, i, 0, 0)),
        scratch_shapes=[
            pltpu.VMEM((comps, pair, slab + 2 * reach, width), jnp.bfloat16),
            pltpu.VMEM((comps, pair, rows, width), jnp.float32),
        ],
        cost_estimate=pl.CostEstimate(
            flops=0, bytes_accessed=7 * 4 * inner.size, transcendentals=0
        ),
    )(jnp.asarray(both), base, ghost, before, after, inner, along, across, depth, sums)


def rims(array, axis_number):
    size = lax.axis_size("gx")
    length = array.shape[axis_number]
    up = [(i, (i + 1) % size) for i in range(size)]
    down = [(j, i) for i, j in up]
    last = lax.slice_in_dim(array, length - reach, length, axis=axis_number)
    first = lax.slice_in_dim(array, 0, reach, axis=axis_number)
    return lax.ppermute(last, "gx", up), lax.ppermute(first, "gx", down)


def swap(array, bit):
    return lax.ppermute(array, "pert", [(i, i ^ bit) for i in range(lax.axis_size("pert"))])


def spread(coded, root):
    me = lax.axis_index("pert")
    if lax.axis_size("pert") != 8:
        kept = jnp.where(me == root, coded, 0).astype(jnp.float32)
        return lax.psum(kept, "pert").astype(jnp.int16)
    comps, _, slab, width = coded.shape
    quarter = slab // 4
    core = me % 2
    is_root = me == root
    place = (me // 2) ^ (root // 2)
    at_a, at_b, at_c = place == 0, place == 1, place == 2

    def cut(which, fields):
        parts = [coded[:, f, q * quarter : (q + 1) * quarter] for f in fields for q in streams[which]]
        return jnp.stack(parts, 0)

    halves = [[cut(u, (0, 1)), cut(u, (2, 3))] for u in range(2)]
    mine = [jnp.where(core == 0, h[0], h[1]) for h in halves]
    theirs = [swap(jnp.where(core == 0, h[1], h[0]), 1) for h in halves]
    source = [jnp.where(is_root, mine[u], theirs[u]) for u in range(2)]
    sent_x = [[], []]
    sent_y = [[], []]
    for s in range(phases + 1):
        for u in range(2):
            k = min(s, phases - 1)
            one, two = source[u][k], source[u][phases + k]
            if s == phases:
                one, two = two, one
            if s > 0:
                one = jnp.where(at_a, one, sent_y[u][s - 1])
                two = jnp.where(at_a, two, sent_x[u][s - 1])
            sent_x[u].append(swap(one, 2))
            sent_y[u].append(swap(two, 4))
    pieces = {}
    for u in range(2):
        X, Y, S = sent_x[u], sent_y[u], source[u]
        parts = []
        for h in range(2):
            P1, P2 = (X, Y) if h == 0 else (Y, X)
            near, far = (at_b, at_c) if h == 0 else (at_c, at_b)
            for k in range(phases):
                late = P1[k + 2] if k + 2 <= phases else P2[phases]
                value = jnp.where(near, P1[k], jnp.where(far, late, P2[k + 1]))
                parts.append(jnp.where(at_a, S[h * phases + k], value))
        held = jnp.stack(parts, 0)
        other = swap(held, 1)
        flow = jnp.where(core == 0, held, other)
        ghost = jnp.where(core == 0, other, held)
        for h in range(2):
            for k, q in enumerate(streams[u]):
                pieces[h, q] = flow[h * phases + k]
                pieces[2 + h, q] = ghost[h * phases + k]
    return jnp.stack(
        [jnp.concatenate([pieces[f, q] for q in range(4)], 1) for f in range(4)], 1
    )


def per_device(pert_field, base_store, section_owner, pert_ids, member_visc):
    _, comps, slab, planes, width = pert_field.shape
    length = slab * lax.axis_size("gx")
    member_pick = pert_ids[0] == jnp.arange(member_visc.shape[0], dtype=jnp.int32)
    viscosity = jnp.sum(jnp.where(member_pick, member_visc, 0.0))[None]
    levels_here = base_store.shape[0]
    owner_slot = section_owner[0] % levels_here
    owner_root = section_owner[0] // levels_here
    tiles = base_store.reshape(levels_here, comps, slab * planes, width)
    tile = tiles[0] if levels_here == 1 else lax.dynamic_index_in_dim(tiles, owner_slot, 0, False)
    coded = pack(tile, planes, 32)
    field = pert_field.reshape(comps, slab * planes, width)
    inner, depth, partial = unpack(field, viscosity, planes, 32)
    before, after = rims(inner, 2)
    along, across, sums = along_across(inner, before, after, partial, viscosity, length)
    arrived = spread(coded, owner_root)
    base, ghost = arrived[:, :2], arrived[:, 2:]
    base_before, base_after = rims(base, 2)
    return final(
        base, ghost, base_before, base_after, inner, along, across, depth, sums, length
    )


def solution(mesh):
    placed = (
        P("pert", None, "gx", None, None),
        P("pert", None, "gx", None, None),
        P(),
        P("pert"),
        P(),
    )
    return jax.shard_map(
        per_device,
        mesh=mesh,
        in_specs=placed,
        out_specs=P("pert", None, "gx", None, None),
        check_vma=False,
    )
```

```python
import functools

import jax
import jax.numpy as jnp
import numpy as np
from jax import lax
from jax.experimental import pallas as pl
from jax.experimental.pallas import tpu as pltpu
from jax.sharding import PartitionSpec as P

section_step = 0.25
reach = 16
code_scale = 4096.0
phases = 2
streams = ((0, 3), (1, 2))


def compact_kernel(length):
    wave = 2.0 * np.pi * np.arange(length) / length
    symbol = 14.0 / 9.0 * np.sin(wave) + 1.0 / 18.0 * np.sin(2.0 * wave)
    symbol = 1j * symbol / (1.0 + 2.0 / 3.0 * np.cos(wave))
    return np.real(np.fft.ifft(symbol))


def along_matrices(rows, length):
    kernel = compact_kernel(length)
    first = np.zeros((rows, rows + 2 * reach))
    second = np.zeros((rows, rows + 2 * reach))
    for i in range(rows):
        for k in range(-reach, reach + 1):
            first[i, i + reach + k] = kernel[-k % length]
        for k, weight in ((0, -980.0), (1, 270.0), (2, -27.0), (3, 2.0)):
            second[i, i + reach + k] = weight
            second[i, i + reach - k] = weight
    high = first.astype(jnp.bfloat16)
    low = (first - high.astype(np.float64)).astype(jnp.bfloat16)
    return high, low, second.astype(jnp.bfloat16)


first_taps = ((1, 45.0), (2, -9.0), (3, 1.0))
second_taps = ((0, -490.0), (1, 270.0), (2, -27.0), (3, 2.0))


def depth_matrix(rows, planes, fields):
    matrix = np.zeros((len(fields) * rows, rows * planes))
    for f, taps in enumerate(fields):
        for i in range(rows):
            for z, weight in taps:
                matrix[f * rows + i, i * planes + z] += weight
    return matrix.astype(jnp.bfloat16)


def first_at(z):
    return [(z + k, w) for k, w in first_taps] + [(z - k, -w) for k, w in first_taps]


def second_at(z):
    taps = [(z + k, w) for k, w in second_taps]
    return taps + [(z - k, w) for k, w in second_taps if k > 0]


def product(a, b):
    return jnp.dot(a, b, preferred_element_type=jnp.float32)


def split(values):
    high = values.astype(jnp.bfloat16)
    return high, (values - high.astype(jnp.float32)).astype(jnp.bfloat16)


def shifted_pairs(values):
    width = values.shape[-1]
    return [
        (pltpu.roll(values, width - k, 1), pltpu.roll(values, k, 1)) for k in (1, 2, 3)
    ]


def first_across(pairs):
    (u1, d1), (u2, d2), (u3, d3) = pairs
    return 0.75 * (u1 - d1) - 0.15 * (u2 - d2) + (1.0 / 60.0) * (u3 - d3)


def pack_kernel(core, weights, tile, mine, theirs):
    rows = weights.shape[0] // 4
    blocks = mine.shape[3] // rows

    def store(kept, sent):
        for b in range(blocks):
            depth = weights.shape[1]
            mixed = product(weights[...], tile[0, b * depth : (b + 1) * depth])
            for f in range(4):
                scale = code_scale if f < 2 else code_scale / 60.0
                part = jnp.round(mixed[f * rows : (f + 1) * rows] * scale)
                target = kept if f < 2 else sent
                code = part.astype(jnp.int32).astype(jnp.int16)
                target[f % 2, 0, 0, b * rows : (b + 1) * rows] = code

    @pl.when(core[0] == 0)
    def _():
        store(mine, theirs)

    @pl.when(core[0] != 0)
    def _():
        store(theirs, mine)


def pack(tile, planes, core, which):
    comps, deep, width = tile.shape
    quarter = deep // planes // 4
    x_rows = min(quarter, 32)
    ghost = [[t for t in first_at(z) if t[0] not in (3, 4)] for z in (3, 4)]
    weights = depth_matrix(x_rows, planes, [[(3, 1.0)], [(4, 1.0)]] + ghost)
    first, second = streams[which]
    shape = jax.ShapeDtypeStruct((2, 2, comps, quarter, width), jnp.int16)
    spec = pl.BlockSpec((2, 1, 1, quarter, width), lambda k, c: (0, k, c, 0, 0))
    return pl.pallas_call(
        pack_kernel,
        out_shape=(shape,) * 2,
        grid=(2, comps),
        in_specs=[
            pl.BlockSpec(memory_space=pltpu.SMEM),
            pl.BlockSpec(weights.shape, lambda k, c: (0, 0)),
            pl.BlockSpec(
                (1, quarter * planes, width), lambda k, c: (c, first + k * (second - first), 0)
            ),
        ],
        out_specs=(spec,) * 2,
        cost_estimate=pl.CostEstimate(
            flops=0, bytes_accessed=2 * comps * deep * width, transcendentals=0
        ),
    )(core, jnp.asarray(weights), tile)


def field_kernel(
    viscosity, m_top, m_low, field, before, after, inner, depth, along, across, sums, high_s, low_s, curve_s
):
    slab, width = inner.shape[2:]
    rows = m_low.shape[0]
    planes = field.shape[1] // slab
    lanes = field.shape[2]
    column = pl.program_id(1)
    gain = viscosity[0] * section_step
    side = pl.ds(pl.multiple_of(column * lanes, lanes), lanes)

    def unpack(i, carry):
        start = pl.multiple_of(i * 8, 8)
        plane = [field[0, pl.ds(start * planes + z, 8, planes), :] for z in range(planes)]
        at = (pl.ds(start, 8), side)
        for p in range(2):
            z = 3 + p
            centre = plane[z]
            u1, u2, u3 = plane[z + 1], plane[z + 2], plane[z + 3]
            d1, d2, d3 = plane[z - 1], plane[z - 2], plane[z - 3]
            slope = 0.75 * (u1 - d1) - 0.15 * (u2 - d2) + (1.0 / 60.0) * (u3 - d3)
            curve = 1.5 * (u1 + d1) - 0.15 * (u2 + d2) + (1.0 / 90.0) * (u3 + d3)
            inner[(0, p) + at] = centre
            depth[(0, p) + at] = slope
            sums[(0, p) + at] = centre + gain * (curve - (49.0 / 18.0) * centre)
        return carry

    lax.fori_loop(0, slab // 8, unpack, 0, unroll=4)

    @pl.when(column == pl.num_programs(1) - 1)
    def _():
        field_rest(
            gain, m_top, m_low, before, after, inner, along, across, sums, high_s, low_s, curve_s
        )


def field_rest(
    gain, m_top, m_low, before, after, inner, along, across, sums, high_s, low_s, curve_s
):
    slab = inner.shape[2]
    rows = m_low.shape[0]
    for p in range(2):
        for start, rim in ((0, before), (reach + slab, after)):
            high, low = split(rim[0, :, p])
            high_s[start : start + reach, :] = high
            low_s[start : start + reach, :] = low

        def fill(i, carry):
            start = pl.multiple_of(i * 16, 16)
            high, low = split(inner[0, p, pl.ds(start, 16), :])
            at = pl.ds(pl.multiple_of(start + reach, 16), 16)
            high_s[at, :] = high
            low_s[at, :] = low
            return carry

        lax.fori_loop(0, slab // 16, fill, 0)
        for b in range(slab // rows):
            window = pl.ds(b * rows, rows + 2 * reach)
            high, low = high_s[window, :], low_s[window, :]
            both = product(m_top[...], high) + product(m_top[...], low)
            along[0, p, b * rows : (b + 1) * rows] = both[:rows] + product(m_low[...], high)
            curve_s[b * rows : (b + 1) * rows] = both[rows:]

        def body(i, carry):
            at = pl.ds(pl.multiple_of(i * 8, 8), 8)
            pairs = shifted_pairs(inner[0, p, at, :])
            across[0, p, at, :] = first_across(pairs)
            (u1, d1), (u2, d2), (u3, d3) = pairs
            curve = 1.5 * (u1 + d1) - 0.15 * (u2 + d2) + (1.0 / 90.0) * (u3 + d3)
            curve = curve + (1.0 / 180.0) * curve_s[at, :]
            sums[0, p, at, :] = sums[0, p, at, :] + gain * curve
            return carry

        lax.fori_loop(0, slab // 8, body, 0)


def field_terms(field, before, after, viscosity, length):
    comps, slab, planes, width = field.shape
    lanes = 128
    flat = field.reshape(comps, slab * planes, width)
    rows = min(slab, 128)
    high, low, second = along_matrices(rows, length)
    top = np.concatenate([high, second], 0)
    shape = jax.ShapeDtypeStruct((comps, 2, slab, width), jnp.float32)
    spec = pl.BlockSpec((1, 2, slab, width), lambda c, t: (c, 0, 0, 0))
    rim = pl.BlockSpec((1, reach, 2, width), lambda c, t: (c, 0, 0, 0))
    return pl.pallas_call(
        field_kernel,
        out_shape=(shape,) * 5,
        grid=(comps, width // lanes),
        in_specs=[
            pl.BlockSpec(memory_space=pltpu.SMEM),
            pl.BlockSpec(top.shape, lambda c, t: (0, 0)),
            pl.BlockSpec(low.shape, lambda c, t: (0, 0)),
            pl.BlockSpec((1, slab * planes, lanes), lambda c, t: (c, 0, t)),
            rim,
            rim,
        ],
        out_specs=(spec,) * 5,
        scratch_shapes=[
            pltpu.VMEM((slab + 2 * reach, width), jnp.bfloat16),
            pltpu.VMEM((slab + 2 * reach, width), jnp.bfloat16),
            pltpu.VMEM((slab, width), jnp.float32),
        ],
        cost_estimate=pl.CostEstimate(
            flops=0, bytes_accessed=9 * 4 * comps * slab * planes * width // 4, transcendentals=0
        ),
    )(viscosity, jnp.asarray(top), jnp.asarray(low), flat, before, after)


def final_kernel(
    core, m_both, held0, other0, held1, other1, before, after,
    inner, depth, along, across, sums, out, base_s, ghost_s, slope_s,
):
    step = pl.program_id(0)
    rows = inner.shape[2]
    quarter = held0.shape[3]
    slab = 4 * quarter
    inverse = 1.0 / code_scale

    def decoded(values):
        return values.astype(jnp.int32).astype(jnp.float32) * inverse

    def load(flow, ghost):
        for u in range(2):
            for k in range(2):
                first = streams[u][k] * quarter
                for c in range(3):
                    for p in range(2):

                        def fill(i, carry):
                            start = pl.multiple_of(i * 16, 16)
                            here = pl.ds(start, 16)
                            to = pl.ds(pl.multiple_of(start + first + reach, 16), 16)
                            values = decoded(flow[u][p, k, c, here, :])
                            base_s[c, p, to, :] = values.astype(jnp.bfloat16)
                            to = pl.ds(pl.multiple_of(start + first, 16), 16)
                            ghost_s[c, p, to, :] = ghost[u][p, k, c, here, :]
                            return carry

                        lax.fori_loop(0, quarter // 16, fill, 0)

    @pl.when(step == 0)
    def _():
        for c in range(3):
            for p in range(2):
                base_s[c, p, 0:reach] = decoded(before[p, c]).astype(jnp.bfloat16)
                base_s[c, p, reach + slab :] = decoded(after[p, c]).astype(jnp.bfloat16)

        @pl.when(core[0] == 0)
        def _():
            load((held0, held1), (other0, other1))

        @pl.when(core[0] != 0)
        def _():
            load((other0, other1), (held0, held1))

    origin = pl.multiple_of(step * rows, 32)
    for c in range(3):
        for p in range(2):
            both = product(m_both[...], base_s[c, p, pl.ds(origin, rows + 2 * reach), :])
            slope_s[c, p] = both[:rows] + both[rows:]

    def body(i, carry):
        start = pl.multiple_of(i * 16, 16)
        at = pl.ds(start, 16)
        there = pl.ds(pl.multiple_of(origin + start, 16), 16)
        inside = pl.ds(pl.multiple_of(origin + reach + start, 16), 16)
        flow = [
            [base_s[c, p, inside, :].astype(jnp.float32) for p in range(2)] for c in range(3)
        ]
        for p in range(2):
            move = [inner[c, p, at, :] for c in range(3)]
            for c in range(3):
                dz = decoded(ghost_s[c, p, there, :])
                if p == 0:
                    dz = dz + 0.75 * flow[c][1]
                else:
                    dz = dz - 0.75 * flow[c][0]
                dy = first_across(shifted_pairs(flow[c][p]))
                total = flow[0][p] * along[c, p, at, :] + flow[1][p] * across[c, p, at, :]
                total = total + flow[2][p] * depth[c, p, at, :]
                total = total + move[0] * slope_s[c, p, at, :] + move[1] * dy + move[2] * dz
                out[0, c, at, p, :] = sums[c, p, at, :] - section_step * total
        return carry

    lax.fori_loop(0, rows // 16, body, 0)


def final(core, pieces, before, after, terms, length):
    inner = terms[0]
    comps, pair, slab, width = inner.shape
    rows = 32
    high, low, _ = along_matrices(rows, length)
    both = np.concatenate([high, low], 0)
    whole = pl.BlockSpec(pieces[0].shape, lambda i: (0, 0, 0, 0, 0))
    rim = pl.BlockSpec(before.shape, lambda i: (0, 0, 0, 0))
    spec = pl.BlockSpec((comps, pair, rows, width), lambda i: (0, 0, i, 0))
    return pl.pallas_call(
        final_kernel,
        out_shape=jax.ShapeDtypeStruct((1, comps, slab, pair, width), jnp.float32),
        grid=(slab // rows,),
        in_specs=[
            pl.BlockSpec(memory_space=pltpu.SMEM),
            pl.BlockSpec(both.shape, lambda i: (0, 0)),
        ]
        + [whole] * 4
        + [rim] * 2
        + [spec] * 5,
        out_specs=pl.BlockSpec((1, comps, rows, pair, width), lambda i: (0, 0, i, 0, 0)),
        scratch_shapes=[
            pltpu.VMEM((comps, pair, slab + 2 * reach, width), jnp.bfloat16),
            pltpu.VMEM((comps, pair, slab, width), jnp.int16),
            pltpu.VMEM((comps, pair, rows, width), jnp.float32),
        ],
        cost_estimate=pl.CostEstimate(
            flops=0, bytes_accessed=7 * 4 * inner.size, transcendentals=0
        ),
    )(core, jnp.asarray(both), *pieces, before, after, *terms)


def ring(last, first):
    size = lax.axis_size("gx")
    up = [(i, (i + 1) % size) for i in range(size)]
    down = [(j, i) for i, j in up]
    return lax.ppermute(last, "gx", up), lax.ppermute(first, "gx", down)


def swap(array, bit):
    return lax.ppermute(array, "pert", [(i, i ^ bit) for i in range(lax.axis_size("pert"))])


def exchange(mine, theirs, root, fill_first, fill_second):
    me = lax.axis_index("pert")
    is_root = me == root
    place = (me // 2) ^ (root // 2)
    at_a, at_b, at_c = place == 0, place == 1, place == 2
    source = []
    for u in range(2):
        source.append(jnp.where(is_root, mine[u], swap(theirs[u], 1)))
    source = list(fill_first(*source))
    X = [[], []]
    Y = [[], []]
    terms = None
    for s in range(phases + 1):
        for u in range(2):
            k = min(s, phases - 1)
            one, two = source[u][0, k], source[u][1, k]
            if s == phases:
                one, two = two, one
            if s > 0:
                one = jnp.where(at_a, one, Y[u][s - 1])
                two = jnp.where(at_a, two, X[u][s - 1])
            X[u].append(swap(one, 2))
            Y[u].append(swap(two, 4))
        if s == 0:
            X[0][0], Y[0][0], terms = fill_second(X[0][0], Y[0][0])
    held = []
    for u in range(2):
        parts = []
        for h in range(2):
            P1, P2 = (X[u], Y[u]) if h == 0 else (Y[u], X[u])
            near, far = (at_b, at_c) if h == 0 else (at_c, at_b)
            row = []
            for k in range(phases):
                late = P1[k + 2] if k + 2 <= phases else P2[phases]
                value = jnp.where(near, P1[k], jnp.where(far, late, P2[k + 1]))
                row.append(jnp.where(at_a, source[u][h, k], value))
            parts.append(jnp.stack(row, 0))
        held.append(jnp.stack(parts, 0))
    other = [swap(h, 1) for h in held]
    return held[0], other[0], held[1], other[1], terms


def per_device(pert_field, base_store, section_owner, pert_ids, member_visc):
    _, comps, slab, planes, width = pert_field.shape
    length = slab * lax.axis_size("gx")
    member_pick = pert_ids[0] == jnp.arange(member_visc.shape[0], dtype=jnp.int32)
    viscosity = jnp.sum(jnp.where(member_pick, member_visc, 0.0))[None]
    levels_here = base_store.shape[0]
    owner_slot = section_owner[0] % levels_here
    owner_root = section_owner[0] // levels_here
    tiles = base_store.reshape(levels_here, comps, slab * planes, width)
    tile = tiles[0] if levels_here == 1 else lax.dynamic_index_in_dim(tiles, owner_slot, 0, False)
    field = pert_field[0]
    me = lax.axis_index("pert")
    in_pairs = lax.axis_size("pert") == 8
    core = (me % 2 if in_pairs else jnp.zeros_like(me)).astype(jnp.int32)[None]
    halves = [pack(tile, planes, core, u) for u in range(2)]
    before, after = ring(
        field[:, slab - reach :, 3:5],
        field[:, :reach, 3:5],
    )
    if in_pairs:
        held_field = []

        def fill_first(*source):
            kept = lax.optimization_barrier((field,) + source)
            held_field.append(kept[0])
            return kept[1:]

        def fill_second(x, y):
            terms = field_terms(held_field[0], before, after, viscosity, length)
            x, y, *terms = lax.optimization_barrier((x, y) + tuple(terms))
            return x, y, terms

        *pieces, terms = exchange(
            [h[0] for h in halves], [h[1] for h in halves], owner_root, fill_first, fill_second
        )
    else:
        terms = field_terms(field, before, after, viscosity, length)
        pieces = [
            lax.psum(jnp.where(me == owner_root, a, 0).astype(jnp.float32), "pert").astype(a.dtype)
            for h in halves
            for a in h
        ]
    rim = jnp.where(core[0] == 0, pieces[0], pieces[1])
    quarter = slab // 4
    base_before, base_after = ring(rim[:, 1, :, quarter - reach :], rim[:, 0, :, :reach])
    return final(core, pieces, base_before, base_after, terms, length)


def solution(mesh):
    placed = (
        P("pert", None, "gx", None, None),
        P("pert", None, "gx", None, None),
        P(),
        P("pert"),
        P(),
    )
    return jax.shard_map(
        per_device,
        mesh=mesh,
        in_specs=placed,
        out_specs=P("pert", None, "gx", None, None),
        check_vma=False,
    )
```

```python
import functools

import jax
import jax.numpy as jnp
import numpy as np
from jax import lax
from jax.experimental import pallas as pl
from jax.experimental.pallas import tpu as pltpu
from jax.sharding import PartitionSpec as P

section_step = 0.25
reach = 16
code_scale = 4096.0
phases = 2
streams = ((0, 3), (1, 2))


def grant(mib):
    return pltpu.CompilerParams(vmem_limit_bytes=mib << 20)


def compact_kernel(length):
    wave = 2.0 * np.pi * np.arange(length) / length
    symbol = 14.0 / 9.0 * np.sin(wave) + 1.0 / 18.0 * np.sin(2.0 * wave)
    symbol = 1j * symbol / (1.0 + 2.0 / 3.0 * np.cos(wave))
    return np.real(np.fft.ifft(symbol))


def along_matrices(rows, length):
    kernel = compact_kernel(length)
    first = np.zeros((rows, rows + 2 * reach))
    second = np.zeros((rows, rows + 2 * reach))
    for i in range(rows):
        for k in range(-reach, reach + 1):
            first[i, i + reach + k] = kernel[-k % length]
        for k, weight in ((0, -980.0), (1, 270.0), (2, -27.0), (3, 2.0)):
            second[i, i + reach + k] = weight
            second[i, i + reach - k] = weight
    high = first.astype(jnp.bfloat16)
    low = (first - high.astype(np.float64)).astype(jnp.bfloat16)
    return high, low, second.astype(jnp.bfloat16)


first_taps = ((1, 45.0), (2, -9.0), (3, 1.0))
second_taps = ((0, -490.0), (1, 270.0), (2, -27.0), (3, 2.0))


def depth_matrix(rows, planes, fields):
    matrix = np.zeros((len(fields) * rows, rows * planes))
    for f, taps in enumerate(fields):
        for i in range(rows):
            for z, weight in taps:
                matrix[f * rows + i, i * planes + z] += weight
    return matrix.astype(jnp.bfloat16)


def first_at(z):
    return [(z + k, w) for k, w in first_taps] + [(z - k, -w) for k, w in first_taps]


def second_at(z):
    taps = [(z + k, w) for k, w in second_taps]
    return taps + [(z - k, w) for k, w in second_taps if k > 0]


def product(a, b):
    return jnp.dot(a, b, preferred_element_type=jnp.float32)


def split(values):
    high = values.astype(jnp.bfloat16)
    return high, (values - high.astype(jnp.float32)).astype(jnp.bfloat16)


def shifted_pairs(values):
    width = values.shape[-1]
    return [
        (pltpu.roll(values, width - k, 1), pltpu.roll(values, k, 1)) for k in (1, 2, 3)
    ]


def first_across(pairs):
    (u1, d1), (u2, d2), (u3, d3) = pairs
    return 0.75 * (u1 - d1) - 0.15 * (u2 - d2) + (1.0 / 60.0) * (u3 - d3)


def pack_kernel(core, weights, tile, mine, theirs):
    rows = weights.shape[0] // 4
    blocks = mine.shape[3] // rows

    def store(kept, sent):
        for b in range(blocks):
            depth = weights.shape[1]
            mixed = product(weights[...], tile[0, b * depth : (b + 1) * depth])
            for f in range(4):
                scale = code_scale if f < 2 else code_scale / 60.0
                part = jnp.round(mixed[f * rows : (f + 1) * rows] * scale)
                target = kept if f < 2 else sent
                code = part.astype(jnp.int32).astype(jnp.int16)
                target[f % 2, 0, 0, b * rows : (b + 1) * rows] = code

    @pl.when(core[0] == 0)
    def _():
        store(mine, theirs)

    @pl.when(core[0] != 0)
    def _():
        store(theirs, mine)


def pack(tile, planes, core, which):
    comps, deep, width = tile.shape
    quarter = deep // planes // 4
    x_rows = min(quarter, 32)
    ghost = [[t for t in first_at(z) if t[0] not in (3, 4)] for z in (3, 4)]
    weights = depth_matrix(x_rows, planes, [[(3, 1.0)], [(4, 1.0)]] + ghost)
    first, second = streams[which]
    shape = jax.ShapeDtypeStruct((2, 2, comps, quarter, width), jnp.int16)
    spec = pl.BlockSpec((2, 1, 1, quarter, width), lambda k, c: (0, k, c, 0, 0))
    return pl.pallas_call(
        pack_kernel,
        out_shape=(shape,) * 2,
        grid=(2, comps),
        in_specs=[
            pl.BlockSpec(memory_space=pltpu.SMEM),
            pl.BlockSpec(weights.shape, lambda k, c: (0, 0)),
            pl.BlockSpec(
                (1, quarter * planes, width), lambda k, c: (c, first + k * (second - first), 0)
            ),
        ],
        out_specs=(spec,) * 2,
        compiler_params=grant(16),
        cost_estimate=pl.CostEstimate(
            flops=0, bytes_accessed=2 * comps * deep * width, transcendentals=0
        ),
    )(core, jnp.asarray(weights), tile)


def field_kernel(
    viscosity, m_top, m_low, field, before, after, inner, depth, along, across, sums, high_s, low_s, curve_s
):
    slab, width = inner.shape[2:]
    rows = m_low.shape[0]
    planes = field.shape[1] // slab
    lanes = field.shape[2]
    column = pl.program_id(1)
    comp = pl.program_id(0)
    gain = viscosity[0] * section_step
    side = pl.ds(pl.multiple_of(column * lanes, lanes), lanes)

    def unpack(i, carry):
        start = pl.multiple_of(i * 8, 8)
        plane = [field[0, pl.ds(start * planes + z, 8, planes), :] for z in range(planes)]
        at = (pl.ds(start, 8), side)
        for p in range(2):
            z = 3 + p
            centre = plane[z]
            u1, u2, u3 = plane[z + 1], plane[z + 2], plane[z + 3]
            d1, d2, d3 = plane[z - 1], plane[z - 2], plane[z - 3]
            slope = 0.75 * (u1 - d1) - 0.15 * (u2 - d2) + (1.0 / 60.0) * (u3 - d3)
            curve = 1.5 * (u1 + d1) - 0.15 * (u2 + d2) + (1.0 / 90.0) * (u3 + d3)
            inner[(comp, p) + at] = centre
            depth[(comp, p) + at] = slope
            sums[(comp, p) + at] = centre + gain * (curve - (49.0 / 18.0) * centre)
        return carry

    lax.fori_loop(0, slab // 8, unpack, 0, unroll=4)

    @pl.when(column == pl.num_programs(1) - 1)
    def _():
        field_rest(
            gain, m_top, m_low, before, after, inner.at[comp], along.at[comp], across.at[comp],
            sums.at[comp], high_s, low_s, curve_s,
        )


def field_rest(
    gain, m_top, m_low, before, after, inner, along, across, sums, high_s, low_s, curve_s
):
    slab = inner.shape[1]
    rows = m_low.shape[0]
    for p in range(2):
        for start, rim in ((0, before), (reach + slab, after)):
            high, low = split(rim[0, :, p])
            high_s[start : start + reach, :] = high
            low_s[start : start + reach, :] = low

        def fill(i, carry):
            start = pl.multiple_of(i * 16, 16)
            high, low = split(inner[p, pl.ds(start, 16), :])
            at = pl.ds(pl.multiple_of(start + reach, 16), 16)
            high_s[at, :] = high
            low_s[at, :] = low
            return carry

        lax.fori_loop(0, slab // 16, fill, 0, unroll=2)
        for b in range(slab // rows):
            window = pl.ds(b * rows, rows + 2 * reach)
            high, low = high_s[window, :], low_s[window, :]
            both = product(m_top[...], high) + product(m_top[...], low)
            along[p, b * rows : (b + 1) * rows] = both[:rows] + product(m_low[...], high)
            curve_s[b * rows : (b + 1) * rows] = both[rows:]

        def body(i, carry):
            at = pl.ds(pl.multiple_of(i * 8, 8), 8)
            pairs = shifted_pairs(inner[p, at, :])
            across[p, at, :] = first_across(pairs)
            (u1, d1), (u2, d2), (u3, d3) = pairs
            curve = 1.5 * (u1 + d1) - 0.15 * (u2 + d2) + (1.0 / 90.0) * (u3 + d3)
            curve = curve + (1.0 / 180.0) * curve_s[at, :]
            sums[p, at, :] = sums[p, at, :] + gain * curve
            return carry

        lax.fori_loop(0, slab // 8, body, 0, unroll=4)


def field_terms(field, viscosity, length):
    comps, slab, planes, width = field.shape
    before, after = ring(field[:, slab - reach :, 3:5], field[:, :reach, 3:5])
    lanes = 128
    flat = field.reshape(comps, slab * planes, width)
    rows = min(slab, 128)
    high, low, second = along_matrices(rows, length)
    top = np.concatenate([high, second], 0)
    shape = pltpu.VMEM((comps, 2, slab, width), jnp.float32)
    spec = pl.BlockSpec(memory_space=pltpu.VMEM)
    rim = pl.BlockSpec((1, reach, 2, width), lambda c, t: (c, 0, 0, 0))
    return pl.pallas_call(
        field_kernel,
        out_shape=(shape,) * 5,
        grid=(comps, width // lanes),
        in_specs=[
            pl.BlockSpec(memory_space=pltpu.SMEM),
            pl.BlockSpec(top.shape, lambda c, t: (0, 0)),
            pl.BlockSpec(low.shape, lambda c, t: (0, 0)),
            pl.BlockSpec((1, slab * planes, lanes), lambda c, t: (c, 0, t)),
            rim,
            rim,
        ],
        out_specs=(spec,) * 5,
        compiler_params=grant(14),
        scratch_shapes=[
            pltpu.VMEM((slab + 2 * reach, width), jnp.bfloat16),
            pltpu.VMEM((slab + 2 * reach, width), jnp.bfloat16),
            pltpu.VMEM((slab, width), jnp.float32),
        ],
        cost_estimate=pl.CostEstimate(
            flops=0, bytes_accessed=9 * 4 * comps * slab * planes * width // 4, transcendentals=0
        ),
    )(viscosity, jnp.asarray(top), jnp.asarray(low), flat, before, after)


def final_kernel(
    core, m_both, held0, other0, held1, other1, before, after,
    inner, depth, along, across, sums, out, base_s, ghost_s, slope_s,
):
    step = pl.program_id(0)
    rows = slope_s.shape[2]
    quarter = held0.shape[3]
    slab = 4 * quarter
    inverse = 1.0 / code_scale

    def decoded(values):
        return values.astype(jnp.int32).astype(jnp.float32) * inverse

    def load(flow, ghost):
        for u in range(2):
            for k in range(2):
                first = streams[u][k] * quarter
                for c in range(3):
                    for p in range(2):

                        def fill(i, carry):
                            start = pl.multiple_of(i * 16, 16)
                            here = pl.ds(start, 16)
                            to = pl.ds(pl.multiple_of(start + first + reach, 16), 16)
                            values = decoded(flow[u][p, k, c, here, :])
                            base_s[c, p, to, :] = values.astype(jnp.bfloat16)
                            to = pl.ds(pl.multiple_of(start + first, 16), 16)
                            ghost_s[c, p, to, :] = ghost[u][p, k, c, here, :]
                            return carry

                        lax.fori_loop(0, quarter // 16, fill, 0)

    @pl.when(step == 0)
    def _():
        for c in range(3):
            for p in range(2):
                base_s[c, p, 0:reach] = decoded(before[p, c]).astype(jnp.bfloat16)
                base_s[c, p, reach + slab :] = decoded(after[p, c]).astype(jnp.bfloat16)

        @pl.when(core[0] == 0)
        def _():
            load((held0, held1), (other0, other1))

        @pl.when(core[0] != 0)
        def _():
            load((other0, other1), (held0, held1))

    origin = pl.multiple_of(step * rows, 32)
    for c in range(3):
        for p in range(2):
            both = product(m_both[...], base_s[c, p, pl.ds(origin, rows + 2 * reach), :])
            slope_s[c, p] = both[:rows] + both[rows:]

    def body(i, carry):
        start = pl.multiple_of(i * 16, 16)
        at = pl.ds(start, 16)
        there = pl.ds(pl.multiple_of(origin + start, 16), 16)
        inside = pl.ds(pl.multiple_of(origin + reach + start, 16), 16)
        flow = [
            [base_s[c, p, inside, :].astype(jnp.float32) for p in range(2)] for c in range(3)
        ]
        for p in range(2):
            move = [inner[c, p, there, :] for c in range(3)]
            for c in range(3):
                dz = decoded(ghost_s[c, p, there, :])
                if p == 0:
                    dz = dz + 0.75 * flow[c][1]
                else:
                    dz = dz - 0.75 * flow[c][0]
                dy = first_across(shifted_pairs(flow[c][p]))
                total = flow[0][p] * along[c, p, there, :] + flow[1][p] * across[c, p, there, :]
                total = total + flow[2][p] * depth[c, p, there, :]
                total = total + move[0] * slope_s[c, p, at, :] + move[1] * dy + move[2] * dz
                out[0, c, at, p, :] = sums[c, p, there, :] - section_step * total
        return carry

    lax.fori_loop(0, rows // 16, body, 0)


def final(core, pieces, before, after, terms, length):
    comps, pair, slab, width = terms[0].shape
    rows = 32
    high, low, _ = along_matrices(rows, length)
    both = np.concatenate([high, low], 0)
    whole = pl.BlockSpec(
        pieces[0].shape, lambda i: (0, 0, 0, 0, 0), pipeline_mode=pl.Buffered(1)
    )
    rim = pl.BlockSpec(before.shape, lambda i: (0, 0, 0, 0))
    spec = pl.BlockSpec(memory_space=pltpu.VMEM)
    return pl.pallas_call(
        final_kernel,
        out_shape=jax.ShapeDtypeStruct((1, comps, slab, pair, width), jnp.float32),
        grid=(slab // rows,),
        in_specs=[
            pl.BlockSpec(memory_space=pltpu.SMEM),
            pl.BlockSpec(both.shape, lambda i: (0, 0)),
        ]
        + [whole] * 4
        + [rim] * 2
        + [spec] * 5,
        out_specs=pl.BlockSpec((1, comps, rows, pair, width), lambda i: (0, 0, i, 0, 0)),
        compiler_params=grant(24),
        scratch_shapes=[
            pltpu.VMEM((comps, pair, slab + 2 * reach, width), jnp.bfloat16),
            pltpu.VMEM((comps, pair, slab, width), jnp.int16),
            pltpu.VMEM((comps, pair, rows, width), jnp.float32),
        ],
        cost_estimate=pl.CostEstimate(
            flops=0, bytes_accessed=8 * comps * pair * slab * width, transcendentals=0
        ),
    )(core, jnp.asarray(both), *pieces, before, after, *terms)


def ring(last, first):
    size = lax.axis_size("gx")
    up = [(i, (i + 1) % size) for i in range(size)]
    down = [(j, i) for i, j in up]
    return lax.ppermute(last, "gx", up), lax.ppermute(first, "gx", down)


def swap(array, bit):
    return lax.ppermute(array, "pert", [(i, i ^ bit) for i in range(lax.axis_size("pert"))])


def exchange(mine, theirs, root, fill_first, fill_second):
    me = lax.axis_index("pert")
    is_root = me == root
    place = (me // 2) ^ (root // 2)
    at_a, at_b, at_c = place == 0, place == 1, place == 2
    source = []
    for u in range(2):
        source.append(jnp.where(is_root, mine[u], swap(theirs[u], 1)))
    source = list(fill_first(*source))
    X = [[], []]
    Y = [[], []]
    terms = None
    for s in range(phases + 1):
        for u in range(2):
            k = min(s, phases - 1)
            one, two = source[u][0, k], source[u][1, k]
            if s == phases:
                one, two = two, one
            if s > 0:
                one = jnp.where(at_a, one, Y[u][s - 1])
                two = jnp.where(at_a, two, X[u][s - 1])
                one, two = lax.optimization_barrier((one, two))
            X[u].append(swap(one, 2))
            Y[u].append(swap(two, 4))
        if s == 0:
            X[0][0], Y[0][0], terms = fill_second(X[0][0], Y[0][0])
    held = []
    for u in range(2):
        parts = []
        for h in range(2):
            P1, P2 = (X[u], Y[u]) if h == 0 else (Y[u], X[u])
            near, far = (at_b, at_c) if h == 0 else (at_c, at_b)
            row = []
            for k in range(phases):
                late = P1[k + 2] if k + 2 <= phases else P2[phases]
                value = jnp.where(near, P1[k], jnp.where(far, late, P2[k + 1]))
                row.append(jnp.where(at_a, source[u][h, k], value))
            parts.append(jnp.stack(row, 0))
        held.append(jnp.stack(parts, 0))
    other = [swap(h, 1) for h in held]
    return held[0], other[0], held[1], other[1], terms


def per_device(pert_field, base_store, section_owner, pert_ids, member_visc):
    _, comps, slab, planes, width = pert_field.shape
    length = slab * lax.axis_size("gx")
    member_pick = pert_ids[0] == jnp.arange(member_visc.shape[0], dtype=jnp.int32)
    viscosity = jnp.sum(jnp.where(member_pick, member_visc, 0.0))[None]
    levels_here = base_store.shape[0]
    owner_slot = section_owner[0] % levels_here
    owner_root = section_owner[0] // levels_here
    tiles = base_store.reshape(levels_here, comps, slab * planes, width)
    tile = tiles[0] if levels_here == 1 else lax.dynamic_index_in_dim(tiles, owner_slot, 0, False)
    field = pert_field[0]
    me = lax.axis_index("pert")
    in_pairs = lax.axis_size("pert") == 8
    core = (me % 2 if in_pairs else jnp.zeros_like(me)).astype(jnp.int32)[None]
    halves = [pack(tile, planes, core, u) for u in range(2)]
    if in_pairs:
        held_field = []

        def fill_first(*source):
            kept = lax.optimization_barrier((field,) + source)
            held_field.append(kept[0])
            return kept[1:]

        def fill_second(x, y):
            terms = field_terms(held_field[0], viscosity, length)
            x, y, *terms = lax.optimization_barrier((x, y) + tuple(terms))
            return x, y, terms

        *pieces, terms = exchange(
            [h[0] for h in halves], [h[1] for h in halves], owner_root, fill_first, fill_second
        )
    else:
        terms = field_terms(field, viscosity, length)
        pieces = [
            lax.psum(jnp.where(me == owner_root, a, 0).astype(jnp.float32), "pert").astype(a.dtype)
            for h in halves
            for a in h
        ]
    rim = jnp.where(core[0] == 0, pieces[0], pieces[1])
    quarter = slab // 4
    base_before, base_after = ring(rim[:, 1, :, quarter - reach :], rim[:, 0, :, :reach])
    return final(core, pieces, base_before, base_after, terms, length)


def solution(mesh):
    placed = (
        P("pert", None, "gx", None, None),
        P("pert", None, "gx", None, None),
        P(),
        P("pert"),
        P(),
    )
    return jax.shard_map(
        per_device,
        mesh=mesh,
        in_specs=placed,
        out_specs=P("pert", None, "gx", None, None),
        check_vma=False,
    )
```

```python
import functools

import jax
import jax.numpy as jnp
import numpy as np
from jax import lax
from jax.experimental import pallas as pl
from jax.experimental.pallas import tpu as pltpu
from jax.sharding import PartitionSpec as P

section_step = 0.25
reach = 16
lanes = 128
code_scale = 4096.0
phases = 2
streams = ((0, 3), (1, 2))


def grant(mib):
    return pltpu.CompilerParams(vmem_limit_bytes=mib << 20)


def compact_kernel(length):
    wave = 2.0 * np.pi * np.arange(length) / length
    symbol = 14.0 / 9.0 * np.sin(wave) + 1.0 / 18.0 * np.sin(2.0 * wave)
    symbol = 1j * symbol / (1.0 + 2.0 / 3.0 * np.cos(wave))
    return np.real(np.fft.ifft(symbol))


def along_matrices(rows, length):
    kernel = compact_kernel(length)
    first = np.zeros((rows, rows + 2 * reach))
    second = np.zeros((rows, rows + 2 * reach))
    for i in range(rows):
        for k in range(-reach, reach + 1):
            first[i, i + reach + k] = kernel[-k % length]
        for k, weight in ((0, -980.0), (1, 270.0), (2, -27.0), (3, 2.0)):
            second[i, i + reach + k] = weight
            second[i, i + reach - k] = weight
    high = first.astype(jnp.bfloat16)
    low = (first - high.astype(np.float64)).astype(jnp.bfloat16)
    return high, low, second.astype(jnp.bfloat16)


first_taps = ((1, 45.0), (2, -9.0), (3, 1.0))
second_taps = ((0, -490.0), (1, 270.0), (2, -27.0), (3, 2.0))


def depth_matrix(rows, planes, fields):
    matrix = np.zeros((len(fields) * rows, rows * planes))
    for f, taps in enumerate(fields):
        for i in range(rows):
            for z, weight in taps:
                matrix[f * rows + i, i * planes + z] += weight
    return matrix.astype(jnp.bfloat16)


def first_at(z):
    return [(z + k, w) for k, w in first_taps] + [(z - k, -w) for k, w in first_taps]


def second_at(z):
    taps = [(z + k, w) for k, w in second_taps]
    return taps + [(z - k, w) for k, w in second_taps if k > 0]


def across_matrix(orders):
    matrix = np.zeros((2 * lanes, lanes * len(orders)))
    for o, taps in enumerate(orders):
        for i in range(lanes):
            for k, weight in taps:
                matrix[lanes // 2 + i + k, o * lanes + i] += weight
    return matrix.astype(jnp.bfloat16)


def half_turned(values):
    half = lanes // 2
    return jnp.concatenate([values[:, -half:], values, values[:, :half]], 1)


def product(a, b):
    return jnp.dot(a, b, preferred_element_type=jnp.float32)


def split(values):
    high = values.astype(jnp.bfloat16)
    return high, (values - high.astype(jnp.float32)).astype(jnp.bfloat16)


def pack_kernel(core, weights, tile, mine, theirs):
    rows = weights.shape[0] // 4
    blocks = mine.shape[3] // rows

    def store(kept, sent):
        for b in range(blocks):
            depth = weights.shape[1]
            mixed = product(weights[...], tile[0, b * depth : (b + 1) * depth])
            for f in range(4):
                scale = code_scale if f < 2 else code_scale / 60.0
                part = jnp.round(mixed[f * rows : (f + 1) * rows] * scale)
                target = kept if f < 2 else sent
                code = part.astype(jnp.int32).astype(jnp.int16)
                target[f % 2, 0, 0, b * rows : (b + 1) * rows] = code

    @pl.when(core[0] == 0)
    def _():
        store(mine, theirs)

    @pl.when(core[0] != 0)
    def _():
        store(theirs, mine)


def pack(tile, planes, core, which):
    comps, deep, width = tile.shape
    quarter = deep // planes // 4
    x_rows = min(quarter, 32)
    ghost = [[t for t in first_at(z) if t[0] not in (3, 4)] for z in (3, 4)]
    weights = depth_matrix(x_rows, planes, [[(3, 1.0)], [(4, 1.0)]] + ghost)
    first, second = streams[which]
    shape = jax.ShapeDtypeStruct((2, 2, comps, quarter, width), jnp.int16)
    spec = pl.BlockSpec((2, 1, 1, quarter, width), lambda k, c: (0, k, c, 0, 0))
    return pl.pallas_call(
        pack_kernel,
        out_shape=(shape,) * 2,
        grid=(2, comps),
        in_specs=[
            pl.BlockSpec(memory_space=pltpu.SMEM),
            pl.BlockSpec(weights.shape, lambda k, c: (0, 0)),
            pl.BlockSpec(
                (1, quarter * planes, width), lambda k, c: (c, first + k * (second - first), 0)
            ),
        ],
        out_specs=(spec,) * 2,
        compiler_params=grant(16),
        cost_estimate=pl.CostEstimate(
            flops=0, bytes_accessed=2 * comps * deep * width, transcendentals=0
        ),
    )(core, jnp.asarray(weights), tile)


def depth_across_kernel(
    viscosity, turn, field, inner, depth, across, sums, token, columns, high_s, low_s, arrived
):
    slab, width = inner.shape[2:]
    planes = field.shape[1] // slab
    tiles = width // lanes
    gain = viscosity[0] * section_step

    def fetch(c, t):
        source = field.at[c, :, pl.ds(t * lanes, lanes)]
        return pltpu.make_async_copy(source, columns.at[t], arrived.at[t])

    c = pl.program_id(0)

    @pl.when(c == 0)
    def _():
        for t in range(tiles):
            fetch(0, t).start()

    for t in range(tiles):
        fetch(c, t).wait()

        def unpack(i, carry):
            start = pl.multiple_of(i * 8, 8)
            plane = [columns[t, pl.ds(start * planes + z, 8, planes), :] for z in range(planes)]
            at = (pl.ds(start, 8), pl.ds(t * lanes, lanes))
            for p in range(2):
                z = 3 + p
                centre = plane[z]
                u1, u2, u3 = plane[z + 1], plane[z + 2], plane[z + 3]
                d1, d2, d3 = plane[z - 1], plane[z - 2], plane[z - 3]
                slope = 0.75 * (u1 - d1) - 0.15 * (u2 - d2) + (1.0 / 60.0) * (u3 - d3)
                curve = 1.5 * (u1 + d1) - 0.15 * (u2 + d2) + (1.0 / 90.0) * (u3 + d3)
                inner[(0, p) + at] = centre
                depth[(0, p) + at] = slope
                sums[(0, p) + at] = centre + gain * (curve - (49.0 / 18.0) * centre)
            return carry

        lax.fori_loop(0, slab // 8, unpack, 0, unroll=4)

        @pl.when(c < pl.num_programs(0) - 1)
        def _():
            fetch(c + 1, t).start()

    for p in range(2):

        def fill(i, carry):
            at = pl.ds(pl.multiple_of(i * 16, 16), 16)
            high, low = split(inner[0, p, at, :])
            high_s[at, :] = half_turned(high)
            low_s[at, :] = half_turned(low)
            return carry

        lax.fori_loop(0, slab // 16, fill, 0, unroll=2)
        for t in range(tiles):
            side = pl.ds(t * lanes, lanes)
            window = pl.ds(t * lanes, 2 * lanes)
            both = product(high_s[:, window], turn[...]) + product(low_s[:, window], turn[...])
            across[0, p, :, side] = both[:, :lanes] * (1.0 / 60.0)
            curve = both[:, lanes:] * (gain / 180.0)
            sums[0, p, :, side] = sums[0, p, :, side] + curve
    token[...] = jnp.zeros_like(token)


def depth_across(field, viscosity):
    comps, slab, planes, width = field.shape
    flat = field.reshape(comps, slab * planes, width)
    turn = across_matrix([first_at(0), [t for t in second_at(0) if t[0] != 0]])
    shape = jax.ShapeDtypeStruct((comps, 2, slab, width), jnp.float32)
    spec = pl.BlockSpec((1, 2, slab, width), lambda c: (c, 0, 0, 0))
    mark = pl.BlockSpec((8, lanes), lambda c: (0, 0))
    return pl.pallas_call(
        depth_across_kernel,
        out_shape=(shape,) * 4 + (jax.ShapeDtypeStruct((8, lanes), jnp.int32),),
        grid=(comps,),
        in_specs=[
            pl.BlockSpec(memory_space=pltpu.SMEM),
            pl.BlockSpec(turn.shape, lambda c: (0, 0)),
            pl.BlockSpec(memory_space=pl.ANY),
        ],
        out_specs=(spec,) * 4 + (mark,),
        compiler_params=grant(56),
        scratch_shapes=[
            pltpu.VMEM((width // lanes, slab * planes, lanes), jnp.float32),
            pltpu.VMEM((slab, width + lanes), jnp.bfloat16),
            pltpu.VMEM((slab, width + lanes), jnp.bfloat16),
            pltpu.SemaphoreType.DMA((width // lanes,)),
        ],
        cost_estimate=pl.CostEstimate(
            flops=0, bytes_accessed=4 * comps * slab * planes * width * 2, transcendentals=0
        ),
    )(viscosity, jnp.asarray(turn), flat)


def along_kernel(
    viscosity, m_all, m_top, before, after, inner, partial, along, sums, token, high_s, low_s
):
    slab = inner.shape[2]
    rows = m_top.shape[0] // 2
    gain = viscosity[0] * (section_step / 180.0)

    for start, rim in ((0, before), (reach + slab, after)):
        high, low = split(rim[0, 0])
        high_s[start : start + reach, :] = high
        low_s[start : start + reach, :] = low

    def fill(i, carry):
        start = pl.multiple_of(i * 16, 16)
        high, low = split(inner[0, 0, pl.ds(start, 16), :])
        at = pl.ds(pl.multiple_of(start + reach, 16), 16)
        high_s[at, :] = high
        low_s[at, :] = low
        return carry

    lax.fori_loop(0, slab // 16, fill, 0, unroll=2)
    for b in range(slab // rows):
        window = pl.ds(b * rows, rows + 2 * reach)
        at = pl.ds(b * rows, rows)
        one = product(m_all[...], high_s[window, :])
        two = product(m_top[...], low_s[window, :])
        along[0, 0, at, :] = one[:rows] + one[2 * rows :] + two[:rows]
        curve = one[rows : 2 * rows] + two[rows:]
        sums[0, 0, at, :] = partial[0, 0, at, :] + gain * curve
    token[...] = jnp.zeros_like(token)


def along_terms(inner, partial, before, after, viscosity, length):
    comps, pair, slab, width = inner.shape
    rows = min(slab, 128)
    high, low, second = along_matrices(rows, length)
    top = np.concatenate([high, second], 0)
    everything = np.concatenate([high, second, low], 0)
    shape = jax.ShapeDtypeStruct(inner.shape, jnp.float32)
    spec = pl.BlockSpec((1, 1, slab, width), lambda c, p: (c, p, 0, 0))
    rim = pl.BlockSpec((1, 1, reach, width), lambda c, p: (c, p, 0, 0))
    mark = pl.BlockSpec((8, lanes), lambda c, p: (0, 0))
    return pl.pallas_call(
        along_kernel,
        out_shape=(shape, shape, jax.ShapeDtypeStruct((8, lanes), jnp.int32)),
        grid=(comps, pair),
        in_specs=[
            pl.BlockSpec(memory_space=pltpu.SMEM),
            pl.BlockSpec(everything.shape, lambda c, p: (0, 0)),
            pl.BlockSpec(top.shape, lambda c, p: (0, 0)),
            rim,
            rim,
            spec,
            spec,
        ],
        out_specs=(spec, spec, mark),
        compiler_params=grant(50),
        scratch_shapes=[
            pltpu.VMEM((slab + 2 * reach, width), jnp.bfloat16),
            pltpu.VMEM((slab + 2 * reach, width), jnp.bfloat16),
        ],
        cost_estimate=pl.CostEstimate(
            flops=0, bytes_accessed=4 * inner.size * 5, transcendentals=0
        ),
    )(viscosity, jnp.asarray(everything), jnp.asarray(top), before, after, inner, partial)


def final_kernel(
    core, m_both, turn, held0, other0, held1, other1, before, after,
    inner, depth, along, across, sums, out, base_s, turned_s, flow_s, ghost_s, slope_s, side_s, arrived,
):
    step = pl.program_id(0)
    rows = slope_s.shape[2]
    quarter = held0.shape[3]
    slab = 4 * quarter
    inverse = 1.0 / code_scale

    def decoded(values):
        return values.astype(jnp.int32).astype(jnp.float32) * inverse

    def load(flow, ghost):
        copies = []
        for u in range(2):
            for k in range(2):
                at = pl.ds(streams[u][k] * quarter, quarter)
                for n, (source, target) in enumerate(((flow, flow_s), (ghost, ghost_s))):
                    copies.append(
                        pltpu.make_async_copy(
                            source[u].at[k], target.at[:, :, at], arrived.at[4 * n + 2 * u + k]
                        )
                    )
        for copy in copies:
            copy.start()
        for copy in copies:
            copy.wait()

    @pl.when(step == 0)
    def _():
        for c in range(3):
            for p in range(2):
                base_s[c, p, 0:reach] = decoded(before[p, c]).astype(jnp.bfloat16)
                base_s[c, p, reach + slab :] = decoded(after[p, c]).astype(jnp.bfloat16)

        @pl.when(core[0] == 0)
        def _():
            load((held0, held1), (other0, other1))

        @pl.when(core[0] != 0)
        def _():
            load((other0, other1), (held0, held1))

        def fill(i, carry):
            start = pl.multiple_of(i * 16, 16)
            to = pl.ds(pl.multiple_of(start + reach, 16), 16)
            for c in range(3):
                for p in range(2):
                    values = decoded(flow_s[p, c, pl.ds(start, 16), :])
                    base_s[c, p, to, :] = values.astype(jnp.bfloat16)
            return carry

        lax.fori_loop(0, slab // 16, fill, 0)

    origin = pl.multiple_of(step * rows, 32)
    def derive(c, carry):
        for p in range(2):
            both = product(m_both[...], base_s[c, p, pl.ds(origin, rows + 2 * reach), :])
            slope_s[c, p] = both[:rows] + both[rows:]
            for r in range(0, rows, 16):
                here = pl.ds(pl.multiple_of(origin + reach + r, 16), 16)
                turned_s[r : r + 16, :] = half_turned(base_s[c, p, here, :])
            for t in range(side_s.shape[3] // lanes):
                window = turned_s[:, pl.ds(t * lanes, 2 * lanes)]
                side_s[c, p, :, pl.ds(t * lanes, lanes)] = product(window, turn[...])
        return carry

    lax.fori_loop(0, 3, derive, 0)

    def body(i, carry):
        start = pl.multiple_of(i * 16, 16)
        at = pl.ds(start, 16)
        there = pl.ds(pl.multiple_of(origin + start, 16), 16)
        inside = pl.ds(pl.multiple_of(origin + reach + start, 16), 16)
        flow = [
            [base_s[c, p, inside, :].astype(jnp.float32) for p in range(2)] for c in range(3)
        ]
        for p in range(2):
            move = [inner[c, p, at, :] for c in range(3)]
            for c in range(3):
                dz = decoded(ghost_s[p, c, there, :])
                if p == 0:
                    dz = dz + 0.75 * flow[c][1]
                else:
                    dz = dz - 0.75 * flow[c][0]
                dy = side_s[c, p, at, :] * (1.0 / 60.0)
                total = flow[0][p] * along[c, p, at, :] + flow[1][p] * across[c, p, at, :]
                total = total + flow[2][p] * depth[c, p, at, :]
                total = total + move[0] * slope_s[c, p, at, :] + move[1] * dy + move[2] * dz
                out[0, c, at, p, :] = sums[c, p, at, :] - section_step * total
        return carry

    lax.fori_loop(0, rows // 16, body, 0)


def final(core, pieces, before, after, terms, length):
    comps, pair, slab, width = terms[0].shape
    rows = min(slab, 32)
    turn = across_matrix([first_at(0)])
    high, low, _ = along_matrices(rows, length)
    both = np.concatenate([high, low], 0)
    whole = pl.BlockSpec(memory_space=pl.ANY)
    rim = pl.BlockSpec(before.shape, lambda i: (0, 0, 0, 0))
    spec = pl.BlockSpec((comps, pair, rows, width), lambda i: (0, 0, i, 0))
    return pl.pallas_call(
        final_kernel,
        out_shape=jax.ShapeDtypeStruct((1, comps, slab, pair, width), jnp.float32),
        grid=(slab // rows,),
        in_specs=[
            pl.BlockSpec(memory_space=pltpu.SMEM),
            pl.BlockSpec(both.shape, lambda i: (0, 0)),
            pl.BlockSpec(turn.shape, lambda i: (0, 0)),
        ]
        + [whole] * 4
        + [rim] * 2
        + [spec] * 5,
        out_specs=pl.BlockSpec((1, comps, rows, pair, width), lambda i: (0, 0, i, 0, 0)),
        compiler_params=grant(58),
        scratch_shapes=[
            pltpu.VMEM((comps, pair, slab + 2 * reach, width), jnp.bfloat16),
            pltpu.VMEM((rows, width + lanes), jnp.bfloat16),
            pltpu.VMEM((pair, comps, slab, width), jnp.int16),
            pltpu.VMEM((pair, comps, slab, width), jnp.int16),
            pltpu.VMEM((comps, pair, rows, width), jnp.float32),
            pltpu.VMEM((comps, pair, rows, width), jnp.float32),
            pltpu.SemaphoreType.DMA((8,)),
        ],
        cost_estimate=pl.CostEstimate(
            flops=0, bytes_accessed=8 * comps * pair * slab * width, transcendentals=0
        ),
    )(core, jnp.asarray(both), jnp.asarray(turn), *pieces, before, after, *terms)


def ring(last, first):
    size = lax.axis_size("gx")
    up = [(i, (i + 1) % size) for i in range(size)]
    down = [(j, i) for i, j in up]
    return lax.ppermute(last, "gx", up), lax.ppermute(first, "gx", down)


def swap(array, bit):
    return lax.ppermute(array, "pert", [(i, i ^ bit) for i in range(lax.axis_size("pert"))])


def exchange(mine, theirs, root, gate, work):
    me = lax.axis_index("pert")
    is_root = me == root
    place = (me // 2) ^ (root // 2)
    at_a, at_b, at_c = place == 0, place == 1, place == 2
    handed = [swap(t, 1) for t in theirs]

    def owned(u, h, k):
        return jnp.where(is_root, mine[u][h, k], handed[u][h, k])

    opening = [owned(u, h, 0) for u in range(2) for h in range(2)]
    opening = gate(opening)
    source = [
        [[opening[2 * u + h]] + [owned(u, h, k) for k in range(1, phases)] for h in range(2)]
        for u in range(2)
    ]
    X = [[], []]
    Y = [[], []]
    for s in range(phases + 1):
        for u in range(2):
            k = min(s, phases - 1)
            one, two = source[u][0][k], source[u][1][k]
            if s == phases:
                one, two = two, one
            if s > 0:
                one = jnp.where(at_a, one, Y[u][s - 1])
                two = jnp.where(at_a, two, X[u][s - 1])
                one, two = lax.optimization_barrier((one, two))
            X[u].append(swap(one, 2))
            Y[u].append(swap(two, 4))
        if s < phases:
            place = place + work[s]()
            at_a, at_b, at_c = place == 0, place == 1, place == 2
    held = []
    for u in range(2):
        parts = []
        for k in range(phases):
            row = []
            for h in range(2):
                P1, P2 = (X[u], Y[u]) if h == 0 else (Y[u], X[u])
                near, far = (at_b, at_c) if h == 0 else (at_c, at_b)
                late = P1[k + 2] if k + 2 <= phases else P2[phases]
                value = jnp.where(near, P1[k], jnp.where(far, late, P2[k + 1]))
                row.append(jnp.where(at_a, source[u][h][k], value))
            parts.append(jnp.stack(row, 0))
        held.append(jnp.stack(parts, 0))
    other = [swap(h, 1) for h in held]
    return held[0], other[0], held[1], other[1]


def per_device(pert_field, base_store, section_owner, pert_ids, member_visc):
    _, comps, slab, planes, width = pert_field.shape
    length = slab * lax.axis_size("gx")
    member_pick = pert_ids[0] == jnp.arange(member_visc.shape[0], dtype=jnp.int32)
    viscosity = jnp.sum(jnp.where(member_pick, member_visc, 0.0))[None]
    levels_here = base_store.shape[0]
    owner_slot = section_owner[0] % levels_here
    owner_root = section_owner[0] // levels_here
    tiles = base_store.reshape(levels_here, comps, slab * planes, width)
    tile = tiles[0] if levels_here == 1 else lax.dynamic_index_in_dim(tiles, owner_slot, 0, False)
    me = lax.axis_index("pert")
    in_pairs = lax.axis_size("pert") == 8
    core = (me % 2 if in_pairs else jnp.zeros_like(me)).astype(jnp.int32)[None]
    halves = [pack(tile, planes, core, u) for u in range(2)]
    done = {"field": pert_field[0], "viscosity": viscosity}

    def gate(opening):
        field, *opening = lax.optimization_barrier((done["field"], *opening))
        done["field"] = field
        return opening

    def early():
        *done["early"], token = depth_across(done["field"], viscosity)
        inner = done["early"][0]
        done["rims"] = ring(inner[:, :, slab - reach :], inner[:, :, :reach])
        return token[0, 0]

    def late():
        inner, depth, across, partial = done["early"]
        along, sums, token = along_terms(inner, partial, *done["rims"], viscosity, length)
        done["terms"] = (inner, depth, along, across, sums)
        return token[0, 0]

    if in_pairs:
        pieces = exchange(
            [h[0] for h in halves], [h[1] for h in halves], owner_root, gate, (early, late)
        )
    else:
        early()
        late()
        pieces = [
            lax.psum(jnp.where(me == owner_root, a, 0).astype(jnp.float32), "pert").astype(a.dtype)
            for h in halves
            for a in h
        ]
        pieces = [a.transpose(1, 0, 2, 3, 4) for a in pieces]
    quarter = slab // 4
    edges = [(1, slice(quarter - reach, quarter)), (0, slice(0, reach))]
    edges = [
        jnp.where(core[0] == 0, pieces[0][k][:, :, at], pieces[1][k][:, :, at]) for k, at in edges
    ]
    base_before, base_after = ring(*edges)
    return final(core, pieces, base_before, base_after, done["terms"], length)


def solution(mesh):
    placed = (
        P("pert", None, "gx", None, None),
        P("pert", None, "gx", None, None),
        P(),
        P("pert"),
        P(),
    )
    return jax.shard_map(
        per_device,
        mesh=mesh,
        in_specs=placed,
        out_specs=P("pert", None, "gx", None, None),
        check_vma=False,
    )
```

```python
import functools

import jax
import jax.numpy as jnp
import numpy as np
from jax import lax
from jax.experimental import pallas as pl
from jax.experimental.pallas import tpu as pltpu
from jax.sharding import PartitionSpec as P

section_step = 0.25
reach = 16
lanes = 128
code_scale = 4096.0
phases = 2
streams = ((0, 3), (1, 2))


def grant(mib):
    return pltpu.CompilerParams(vmem_limit_bytes=mib << 20)


def compact_kernel(length):
    wave = 2.0 * np.pi * np.arange(length) / length
    symbol = 14.0 / 9.0 * np.sin(wave) + 1.0 / 18.0 * np.sin(2.0 * wave)
    symbol = 1j * symbol / (1.0 + 2.0 / 3.0 * np.cos(wave))
    return np.real(np.fft.ifft(symbol))


def along_matrices(rows, length):
    kernel = compact_kernel(length)
    first = np.zeros((rows, rows + 2 * reach))
    second = np.zeros((rows, rows + 2 * reach))
    for i in range(rows):
        for k in range(-reach, reach + 1):
            first[i, i + reach + k] = kernel[-k % length]
        for k, weight in ((0, -980.0), (1, 270.0), (2, -27.0), (3, 2.0)):
            second[i, i + reach + k] = weight
            second[i, i + reach - k] = weight
    high = first.astype(jnp.bfloat16)
    low = (first - high.astype(np.float64)).astype(jnp.bfloat16)
    return high, low, second.astype(jnp.bfloat16)


first_taps = ((1, 45.0), (2, -9.0), (3, 1.0))
second_taps = ((0, -490.0), (1, 270.0), (2, -27.0), (3, 2.0))


def depth_matrix(rows, planes, fields):
    matrix = np.zeros((len(fields) * rows, rows * planes))
    for f, taps in enumerate(fields):
        for i in range(rows):
            for z, weight in taps:
                matrix[f * rows + i, i * planes + z] += weight
    return matrix.astype(jnp.bfloat16)


def first_at(z):
    return [(z + k, w) for k, w in first_taps] + [(z - k, -w) for k, w in first_taps]


def second_at(z):
    taps = [(z + k, w) for k, w in second_taps]
    return taps + [(z - k, w) for k, w in second_taps if k > 0]


def across_matrix(orders):
    matrix = np.zeros((2 * lanes, lanes * len(orders)))
    for o, taps in enumerate(orders):
        for i in range(lanes):
            for k, weight in taps:
                matrix[lanes // 2 + i + k, o * lanes + i] += weight
    return matrix.astype(jnp.bfloat16)


def half_turned(values):
    half = lanes // 2
    return jnp.concatenate([values[:, -half:], values, values[:, :half]], 1)


def product(a, b):
    return jnp.dot(a, b, preferred_element_type=jnp.float32)


def split(values):
    high = values.astype(jnp.bfloat16)
    return high, (values - high.astype(jnp.float32)).astype(jnp.bfloat16)


def pack_kernel(core, weights, tile, mine, theirs):
    rows = weights.shape[0] // 4
    blocks = mine.shape[3] // rows

    def store(kept, sent):
        for b in range(blocks):
            depth = weights.shape[1]
            mixed = product(weights[...], tile[0, b * depth : (b + 1) * depth])
            for f in range(4):
                scale = code_scale if f < 2 else code_scale / 60.0
                part = jnp.round(mixed[f * rows : (f + 1) * rows] * scale)
                target = kept if f < 2 else sent
                code = part.astype(jnp.int32).astype(jnp.int16)
                target[f % 2, 0, 0, b * rows : (b + 1) * rows] = code

    @pl.when(core[0] == 0)
    def _():
        store(mine, theirs)

    @pl.when(core[0] != 0)
    def _():
        store(theirs, mine)


def pack(tile, planes, core, which):
    comps, deep, width = tile.shape
    quarter = deep // planes // 4
    x_rows = min(quarter, 32)
    ghost = [[t for t in first_at(z) if t[0] not in (3, 4)] for z in (3, 4)]
    weights = depth_matrix(x_rows, planes, [[(3, 1.0)], [(4, 1.0)]] + ghost)
    first, second = streams[which]
    shape = jax.ShapeDtypeStruct((2, 2, comps, quarter, width), jnp.int16)
    spec = pl.BlockSpec((2, 1, 1, quarter, width), lambda k, c: (0, k, c, 0, 0))
    return pl.pallas_call(
        pack_kernel,
        out_shape=(shape,) * 2,
        grid=(2, comps),
        in_specs=[
            pl.BlockSpec(memory_space=pltpu.SMEM),
            pl.BlockSpec(weights.shape, lambda k, c: (0, 0)),
            pl.BlockSpec(
                (1, quarter * planes, width), lambda k, c: (c, first + k * (second - first), 0)
            ),
        ],
        out_specs=(spec,) * 2,
        compiler_params=grant(16),
        cost_estimate=pl.CostEstimate(
            flops=0, bytes_accessed=2 * comps * deep * width, transcendentals=0
        ),
    )(core, jnp.asarray(weights), tile)


def field_kernel(
    viscosity, turn, m_all, m_top, before, after, field, inner, depth, along, across, sums, token,
    columns, high_s, low_s, high_x, low_x, arrived,
):
    slab, width = inner.shape[2:]
    planes = field.shape[1] // slab
    tiles = width // lanes
    gain = viscosity[0] * section_step

    def fetch(c, t):
        source = field.at[c, :, pl.ds(t * lanes, lanes)]
        return pltpu.make_async_copy(source, columns.at[t], arrived.at[t])

    c = pl.program_id(0)

    @pl.when(c == 0)
    def _():
        for t in range(tiles):
            fetch(0, t).start()

    for t in range(tiles):
        fetch(c, t).wait()

        def unpack(i, carry):
            start = pl.multiple_of(i * 8, 8)
            plane = [columns[t, pl.ds(start * planes + z, 8, planes), :] for z in range(planes)]
            at = (pl.ds(start, 8), pl.ds(t * lanes, lanes))
            for p in range(2):
                z = 3 + p
                centre = plane[z]
                u1, u2, u3 = plane[z + 1], plane[z + 2], plane[z + 3]
                d1, d2, d3 = plane[z - 1], plane[z - 2], plane[z - 3]
                slope = 0.75 * (u1 - d1) - 0.15 * (u2 - d2) + (1.0 / 60.0) * (u3 - d3)
                curve = 1.5 * (u1 + d1) - 0.15 * (u2 + d2) + (1.0 / 90.0) * (u3 + d3)
                inner[(0, p) + at] = centre
                depth[(0, p) + at] = slope
                sums[(0, p) + at] = centre + gain * (curve - (49.0 / 18.0) * centre)
            return carry

        lax.fori_loop(0, slab // 8, unpack, 0, unroll=4)

        @pl.when(c < pl.num_programs(0) - 1)
        def _():
            fetch(c + 1, t).start()

    rows = m_top.shape[0] // 2
    for p in range(2):
        for start, rim in ((0, before), (reach + slab, after)):
            high, low = split(rim[0, :, p])
            high_x[start : start + reach, :] = high
            low_x[start : start + reach, :] = low

        def fill(i, carry):
            start = pl.multiple_of(i * 16, 16)
            at = pl.ds(start, 16)
            to = pl.ds(pl.multiple_of(start + reach, 16), 16)
            high, low = split(inner[0, p, at, :])
            high_x[to, :] = high
            low_x[to, :] = low
            high_s[at, :] = half_turned(high)
            low_s[at, :] = half_turned(low)
            return carry

        lax.fori_loop(0, slab // 16, fill, 0, unroll=2)
        for b in range(slab // rows):
            window = pl.ds(b * rows, rows + 2 * reach)
            at = pl.ds(b * rows, rows)
            one = product(m_all[...], high_x[window, :])
            two = product(m_top[...], low_x[window, :])
            along[0, p, at, :] = one[:rows] + one[2 * rows :] + two[:rows]
            curve = (gain / 180.0) * (one[rows : 2 * rows] + two[rows:])
            sums[0, p, at, :] = sums[0, p, at, :] + curve
        for t in range(tiles):
            side = pl.ds(t * lanes, lanes)
            window = pl.ds(t * lanes, 2 * lanes)
            both = product(high_s[:, window], turn[...]) + product(low_s[:, window], turn[...])
            across[0, p, :, side] = both[:, :lanes] * (1.0 / 60.0)
            curve = both[:, lanes:] * (gain / 180.0)
            sums[0, p, :, side] = sums[0, p, :, side] + curve
    token[...] = jnp.zeros_like(token)


def field_terms(field, before, after, viscosity, length):
    comps, slab, planes, width = field.shape
    flat = field.reshape(comps, slab * planes, width)
    rows = min(slab, 128)
    high, low, second = along_matrices(rows, length)
    top = np.concatenate([high, second], 0)
    everything = np.concatenate([high, second, low], 0)
    rim = pl.BlockSpec((1, reach, 2, width), lambda c: (c, 0, 0, 0))
    turn = across_matrix([first_at(0), [t for t in second_at(0) if t[0] != 0]])
    shape = jax.ShapeDtypeStruct((comps, 2, slab, width), jnp.float32)
    spec = pl.BlockSpec((1, 2, slab, width), lambda c: (c, 0, 0, 0))
    mark = pl.BlockSpec((8, lanes), lambda c: (0, 0))
    return pl.pallas_call(
        field_kernel,
        out_shape=(shape,) * 5 + (jax.ShapeDtypeStruct((8, lanes), jnp.int32),),
        grid=(comps,),
        in_specs=[
            pl.BlockSpec(memory_space=pltpu.SMEM),
            pl.BlockSpec(turn.shape, lambda c: (0, 0)),
            pl.BlockSpec(everything.shape, lambda c: (0, 0)),
            pl.BlockSpec(top.shape, lambda c: (0, 0)),
            rim,
            rim,
            pl.BlockSpec(memory_space=pl.ANY),
        ],
        out_specs=(spec,) * 5 + (mark,),
        compiler_params=grant(42),
        scratch_shapes=[
            pltpu.VMEM((width // lanes, slab * planes, lanes), jnp.float32),
            pltpu.VMEM((slab, width + lanes), jnp.bfloat16),
            pltpu.VMEM((slab, width + lanes), jnp.bfloat16),
            pltpu.VMEM((slab + 2 * reach, width), jnp.bfloat16),
            pltpu.VMEM((slab + 2 * reach, width), jnp.bfloat16),
            pltpu.SemaphoreType.DMA((width // lanes,)),
        ],
        cost_estimate=pl.CostEstimate(
            flops=0, bytes_accessed=4 * comps * slab * planes * width * 2, transcendentals=0
        ),
    )(
        viscosity, jnp.asarray(turn), jnp.asarray(everything), jnp.asarray(top), before, after, flat
    )


def final_kernel(
    core, m_both, turn, held0, other0, held1, other1, before, after,
    inner, depth, along, across, sums, out, base_s, turned_s, flow_s, ghost_s, slope_s, side_s, arrived,
):
    step = pl.program_id(0)
    rows = slope_s.shape[2]
    quarter = held0.shape[3]
    slab = 4 * quarter
    inverse = 1.0 / code_scale

    def decoded(values):
        return values.astype(jnp.int32).astype(jnp.float32) * inverse

    def load(flow, ghost):
        copies = []
        for u in range(2):
            for k in range(2):
                at = pl.ds(streams[u][k] * quarter, quarter)
                for n, (source, target) in enumerate(((flow, flow_s), (ghost, ghost_s))):
                    copies.append(
                        pltpu.make_async_copy(
                            source[u].at[k], target.at[:, :, at], arrived.at[4 * n + 2 * u + k]
                        )
                    )
        for copy in copies:
            copy.start()
        for copy in copies:
            copy.wait()

    @pl.when(step == 0)
    def _():
        for c in range(3):
            for p in range(2):
                base_s[c, p, 0:reach] = decoded(before[p, c]).astype(jnp.bfloat16)
                base_s[c, p, reach + slab :] = decoded(after[p, c]).astype(jnp.bfloat16)

        @pl.when(core[0] == 0)
        def _():
            load((held0, held1), (other0, other1))

        @pl.when(core[0] != 0)
        def _():
            load((other0, other1), (held0, held1))

        def fill(i, carry):
            start = pl.multiple_of(i * 16, 16)
            to = pl.ds(pl.multiple_of(start + reach, 16), 16)
            for c in range(3):
                for p in range(2):
                    values = decoded(flow_s[p, c, pl.ds(start, 16), :])
                    base_s[c, p, to, :] = values.astype(jnp.bfloat16)
            return carry

        lax.fori_loop(0, slab // 16, fill, 0)

    origin = pl.multiple_of(step * rows, 32)
    def derive(c, carry):
        for p in range(2):
            both = product(m_both[...], base_s[c, p, pl.ds(origin, rows + 2 * reach), :])
            slope_s[c, p] = both[:rows] + both[rows:]
            for r in range(0, rows, 16):
                here = pl.ds(pl.multiple_of(origin + reach + r, 16), 16)
                turned_s[r : r + 16, :] = half_turned(base_s[c, p, here, :])
            for t in range(side_s.shape[3] // lanes):
                window = turned_s[:, pl.ds(t * lanes, 2 * lanes)]
                side_s[c, p, :, pl.ds(t * lanes, lanes)] = product(window, turn[...])
        return carry

    lax.fori_loop(0, 3, derive, 0)

    def body(i, carry):
        start = pl.multiple_of(i * 16, 16)
        at = pl.ds(start, 16)
        there = pl.ds(pl.multiple_of(origin + start, 16), 16)
        inside = pl.ds(pl.multiple_of(origin + reach + start, 16), 16)
        flow = [
            [base_s[c, p, inside, :].astype(jnp.float32) for p in range(2)] for c in range(3)
        ]
        for p in range(2):
            move = [inner[c, p, at, :] for c in range(3)]
            for c in range(3):
                dz = decoded(ghost_s[p, c, there, :])
                if p == 0:
                    dz = dz + 0.75 * flow[c][1]
                else:
                    dz = dz - 0.75 * flow[c][0]
                dy = side_s[c, p, at, :] * (1.0 / 60.0)
                total = flow[0][p] * along[c, p, at, :] + flow[1][p] * across[c, p, at, :]
                total = total + flow[2][p] * depth[c, p, at, :]
                total = total + move[0] * slope_s[c, p, at, :] + move[1] * dy + move[2] * dz
                out[0, c, at, p, :] = sums[c, p, at, :] - section_step * total
        return carry

    lax.fori_loop(0, rows // 16, body, 0)


def final(core, pieces, before, after, terms, length):
    comps, pair, slab, width = terms[0].shape
    rows = min(slab, 32)
    turn = across_matrix([first_at(0)])
    high, low, _ = along_matrices(rows, length)
    both = np.concatenate([high, low], 0)
    whole = pl.BlockSpec(memory_space=pl.ANY)
    rim = pl.BlockSpec(before.shape, lambda i: (0, 0, 0, 0))
    spec = pl.BlockSpec((comps, pair, rows, width), lambda i: (0, 0, i, 0))
    return pl.pallas_call(
        final_kernel,
        out_shape=jax.ShapeDtypeStruct((1, comps, slab, pair, width), jnp.float32),
        grid=(slab // rows,),
        in_specs=[
            pl.BlockSpec(memory_space=pltpu.SMEM),
            pl.BlockSpec(both.shape, lambda i: (0, 0)),
            pl.BlockSpec(turn.shape, lambda i: (0, 0)),
        ]
        + [whole] * 4
        + [rim] * 2
        + [spec] * 5,
        out_specs=pl.BlockSpec((1, comps, rows, pair, width), lambda i: (0, 0, i, 0, 0)),
        compiler_params=grant(58),
        scratch_shapes=[
            pltpu.VMEM((comps, pair, slab + 2 * reach, width), jnp.bfloat16),
            pltpu.VMEM((rows, width + lanes), jnp.bfloat16),
            pltpu.VMEM((pair, comps, slab, width), jnp.int16),
            pltpu.VMEM((pair, comps, slab, width), jnp.int16),
            pltpu.VMEM((comps, pair, rows, width), jnp.float32),
            pltpu.VMEM((comps, pair, rows, width), jnp.float32),
            pltpu.SemaphoreType.DMA((8,)),
        ],
        cost_estimate=pl.CostEstimate(
            flops=0, bytes_accessed=8 * comps * pair * slab * width, transcendentals=0
        ),
    )(core, jnp.asarray(both), jnp.asarray(turn), *pieces, before, after, *terms)


def ring(last, first):
    size = lax.axis_size("gx")
    up = [(i, (i + 1) % size) for i in range(size)]
    down = [(j, i) for i, j in up]
    return lax.ppermute(last, "gx", up), lax.ppermute(first, "gx", down)


def swap(array, bit):
    return lax.ppermute(array, "pert", [(i, i ^ bit) for i in range(lax.axis_size("pert"))])


def exchange(mine, theirs, root, core, gate, work):
    me = lax.axis_index("pert")
    is_root = me == root
    place = (me // 2) ^ (root // 2)
    at_a, at_b, at_c = place == 0, place == 1, place == 2
    handed = [swap(t, 1) for t in theirs]

    def owned(u, h, k):
        return jnp.where(is_root, mine[u][h, k], handed[u][h, k])

    opening = [owned(u, h, 0) for u in range(2) for h in range(2)]
    opening = gate(opening)
    source = [
        [[opening[2 * u + h]] + [owned(u, h, k) for k in range(1, phases)] for h in range(2)]
        for u in range(2)
    ]
    X = [[], []]
    Y = [[], []]
    for s in range(phases + 1):
        for u in range(2):
            k = min(s, phases - 1)
            one, two = source[u][0][k], source[u][1][k]
            if s == phases:
                one, two = two, one
            if s > 0:
                one = jnp.where(at_a, one, Y[u][s - 1])
                two = jnp.where(at_a, two, X[u][s - 1])
                one, two, place = lax.optimization_barrier((one, two, place))
                at_a, at_b, at_c = place == 0, place == 1, place == 2
            X[u].append(swap(one, 2))
            Y[u].append(swap(two, 4))
        if s == 0:
            place = place + work()
            at_a, at_b, at_c = place == 0, place == 1, place == 2
    held = []
    for u in range(2):
        parts = []
        for k in range(phases):
            row = []
            for h in range(2):
                P1, P2 = (X[u], Y[u]) if h == 0 else (Y[u], X[u])
                near, far = (at_b, at_c) if h == 0 else (at_c, at_b)
                late = P1[k + 2] if k + 2 <= phases else P2[phases]
                value = jnp.where(near, P1[k], jnp.where(far, late, P2[k + 1]))
                row.append(jnp.where(at_a, source[u][h][k], value))
            parts.append(jnp.stack(row, 0))
        held.append(jnp.stack(parts, 0))
    quarter = held[0].shape[3]
    size = lax.axis_size("gx")
    pairs = [
        (c * size + i, c * size + (i + 1) % size)
        for c in range(0, lax.axis_size("pert"), 2)
        for i in range(size)
    ]
    both = ("pert", "gx")
    before = lax.ppermute(held[0][1][:, :, quarter - reach :], both, pairs)
    after = lax.ppermute(held[0][0][:, :, :reach], both, [(j, i) for i, j in pairs])
    rims = jnp.stack([before, after], 0)
    other = [swap(h, 1) for h in held]
    rims = jnp.where(core == 0, rims, swap(rims, 1))
    return (held[0], other[0], held[1], other[1]), rims[0], rims[1]


def per_device(pert_field, base_store, section_owner, pert_ids, member_visc):
    _, comps, slab, planes, width = pert_field.shape
    length = slab * lax.axis_size("gx")
    member_pick = pert_ids[0] == jnp.arange(member_visc.shape[0], dtype=jnp.int32)
    viscosity = jnp.sum(jnp.where(member_pick, member_visc, 0.0))[None]
    levels_here = base_store.shape[0]
    owner_slot = section_owner[0] % levels_here
    owner_root = section_owner[0] // levels_here
    tiles = base_store.reshape(levels_here, comps, slab * planes, width)
    tile = tiles[0] if levels_here == 1 else lax.dynamic_index_in_dim(tiles, owner_slot, 0, False)
    me = lax.axis_index("pert")
    in_pairs = lax.axis_size("pert") == 8
    core = (me % 2 if in_pairs else jnp.zeros_like(me)).astype(jnp.int32)[None]
    field = pert_field[0]
    last, first, tile = lax.optimization_barrier(
        (field[:, slab - reach :, 3:5], field[:, :reach, 3:5], tile)
    )
    before, after = ring(last, first)
    halves = [pack(tile, planes, core, u) for u in range(2)]
    done = {"field": field}

    def gate(opening):
        done["field"], *opening = lax.optimization_barrier((done["field"], *opening))
        return opening

    def work():
        *done["terms"], token = field_terms(done["field"], before, after, viscosity, length)
        return token[0, 0]

    if in_pairs:
        mine, theirs = [h[0] for h in halves], [h[1] for h in halves]
        pieces, base_before, base_after = exchange(mine, theirs, owner_root, core[0], gate, work)
    else:
        work()
        pieces = [
            lax.psum(jnp.where(me == owner_root, a, 0).astype(jnp.float32), "pert").astype(a.dtype)
            for h in halves
            for a in h
        ]
        pieces = [a.transpose(1, 0, 2, 3, 4) for a in pieces]
        quarter = slab // 4
        base_before, base_after = ring(
            pieces[0][1][:, :, quarter - reach :], pieces[0][0][:, :, :reach]
        )
    return final(core, pieces, base_before, base_after, done["terms"], length)


def solution(mesh):
    placed = (
        P("pert", None, "gx", None, None),
        P("pert", None, "gx", None, None),
        P(),
        P("pert"),
        P(),
    )
    return jax.shard_map(
        per_device,
        mesh=mesh,
        in_specs=placed,
        out_specs=P("pert", None, "gx", None, None),
        check_vma=False,
    )
```

```python
import functools

import jax
import jax.numpy as jnp
import numpy as np
from jax import lax
from jax.experimental import pallas as pl
from jax.experimental.pallas import tpu as pltpu
from jax.sharding import PartitionSpec as P

section_step = 0.25
reach = 16
lanes = 128
code_scale = 4096.0
phases = 2
streams = ((0, 3), (1, 2))
shares = {(0, 1): 0, (1, 1): 1, (2, 0): 2}


def grant(mib):
    return pltpu.CompilerParams(vmem_limit_bytes=mib << 20)


def compact_kernel(length):
    wave = 2.0 * np.pi * np.arange(length) / length
    symbol = 14.0 / 9.0 * np.sin(wave) + 1.0 / 18.0 * np.sin(2.0 * wave)
    symbol = 1j * symbol / (1.0 + 2.0 / 3.0 * np.cos(wave))
    return np.real(np.fft.ifft(symbol))


def along_matrices(rows, length):
    kernel = compact_kernel(length)
    first = np.zeros((rows, rows + 2 * reach))
    second = np.zeros((rows, rows + 2 * reach))
    for i in range(rows):
        for k in range(-reach, reach + 1):
            first[i, i + reach + k] = kernel[-k % length]
        for k, weight in ((0, -980.0), (1, 270.0), (2, -27.0), (3, 2.0)):
            second[i, i + reach + k] = weight
            second[i, i + reach - k] = weight
    high = first.astype(jnp.bfloat16)
    low = (first - high.astype(np.float64)).astype(jnp.bfloat16)
    return high, low, second.astype(jnp.bfloat16)


first_taps = ((1, 45.0), (2, -9.0), (3, 1.0))
second_taps = ((0, -490.0), (1, 270.0), (2, -27.0), (3, 2.0))


def depth_matrix(rows, planes, fields):
    matrix = np.zeros((len(fields) * rows, rows * planes))
    for f, taps in enumerate(fields):
        for i in range(rows):
            for z, weight in taps:
                matrix[f * rows + i, i * planes + z] += weight
    return matrix.astype(jnp.bfloat16)


def first_at(z):
    return [(z + k, w) for k, w in first_taps] + [(z - k, -w) for k, w in first_taps]


def second_at(z):
    taps = [(z + k, w) for k, w in second_taps]
    return taps + [(z - k, w) for k, w in second_taps if k > 0]


def across_matrix(orders):
    matrix = np.zeros((2 * lanes, lanes * len(orders)))
    for o, taps in enumerate(orders):
        for i in range(lanes):
            for k, weight in taps:
                matrix[lanes // 2 + i + k, o * lanes + i] += weight
    return matrix.astype(jnp.bfloat16)


def half_turned(values):
    half = lanes // 2
    return jnp.concatenate([values[:, -half:], values, values[:, :half]], 1)


def product(a, b):
    return jnp.dot(a, b, preferred_element_type=jnp.float32)


def split(values):
    high = values.astype(jnp.bfloat16)
    return high, (values - high.astype(jnp.float32)).astype(jnp.bfloat16)


def pack_kernel(core, weights, tile, mine, theirs):
    rows = weights.shape[0] // 4
    blocks = mine.shape[3] // rows

    def store(kept, sent):
        for b in range(blocks):
            depth = weights.shape[1]
            mixed = product(weights[...], tile[0, b * depth : (b + 1) * depth])
            for f in range(4):
                scale = code_scale if f < 2 else code_scale / 60.0
                part = jnp.round(mixed[f * rows : (f + 1) * rows] * scale)
                target = kept if f < 2 else sent
                code = part.astype(jnp.int32).astype(jnp.int16)
                target[f % 2, 0, 0, b * rows : (b + 1) * rows] = code

    @pl.when(core[0] == 0)
    def _():
        store(mine, theirs)

    @pl.when(core[0] != 0)
    def _():
        store(theirs, mine)


def pack(tile, planes, core, which):
    comps, deep, width = tile.shape
    quarter = deep // planes // 4
    x_rows = min(quarter, 32)
    ghost = [[t for t in first_at(z) if t[0] not in (3, 4)] for z in (3, 4)]
    weights = depth_matrix(x_rows, planes, [[(3, 1.0)], [(4, 1.0)]] + ghost)
    first, second = streams[which]
    shape = jax.ShapeDtypeStruct((2, 2, comps, quarter, width), jnp.int16)
    spec = pl.BlockSpec((2, 1, 1, quarter, width), lambda k, c: (0, k, c, 0, 0))
    return pl.pallas_call(
        pack_kernel,
        out_shape=(shape,) * 2,
        grid=(2, comps),
        in_specs=[
            pl.BlockSpec(memory_space=pltpu.SMEM),
            pl.BlockSpec(weights.shape, lambda k, c: (0, 0)),
            pl.BlockSpec(
                (1, quarter * planes, width), lambda k, c: (c, first + k * (second - first), 0)
            ),
        ],
        out_specs=(spec,) * 2,
        compiler_params=grant(16),
        cost_estimate=pl.CostEstimate(
            flops=0, bytes_accessed=2 * comps * deep * width, transcendentals=0
        ),
    )(core, jnp.asarray(weights), tile)


def field_kernel(
    c, viscosity, turn, m_all, m_top, before, after, field, inner, depth, along, across, sums, token,
    columns, high_s, low_s, high_x, low_x, arrived,
):
    slab, width = inner.shape[2:]
    planes = field.shape[1] // slab
    tiles = width // lanes
    gain = viscosity[0] * section_step

    def fetch(t):
        source = field.at[c, :, pl.ds(t * lanes, lanes)]
        return pltpu.make_async_copy(source, columns.at[t], arrived.at[t])

    for t in range(tiles):
        fetch(t).start()
    for t in range(tiles):
        fetch(t).wait()

        def unpack(i, carry):
            start = pl.multiple_of(i * 8, 8)
            plane = [columns[t, pl.ds(start * planes + z, 8, planes), :] for z in range(planes)]
            at = (pl.ds(start, 8), pl.ds(t * lanes, lanes))
            for p in range(2):
                z = 3 + p
                centre = plane[z]
                u1, u2, u3 = plane[z + 1], plane[z + 2], plane[z + 3]
                d1, d2, d3 = plane[z - 1], plane[z - 2], plane[z - 3]
                slope = 0.75 * (u1 - d1) - 0.15 * (u2 - d2) + (1.0 / 60.0) * (u3 - d3)
                curve = 1.5 * (u1 + d1) - 0.15 * (u2 + d2) + (1.0 / 90.0) * (u3 + d3)
                inner[(0, p) + at] = centre
                depth[(0, p) + at] = slope
                sums[(0, p) + at] = centre + gain * (curve - (49.0 / 18.0) * centre)
            return carry

        lax.fori_loop(0, slab // 8, unpack, 0, unroll=4)

    rows = m_top.shape[0] // 2
    for p in range(2):
        for start, rim in ((0, before), (reach + slab, after)):
            high, low = split(rim[0, :, p])
            high_x[start : start + reach, :] = high
            low_x[start : start + reach, :] = low

        def fill(i, carry):
            start = pl.multiple_of(i * 16, 16)
            at = pl.ds(start, 16)
            to = pl.ds(pl.multiple_of(start + reach, 16), 16)
            high, low = split(inner[0, p, at, :])
            high_x[to, :] = high
            low_x[to, :] = low
            high_s[at, :] = half_turned(high)
            low_s[at, :] = half_turned(low)
            return carry

        lax.fori_loop(0, slab // 16, fill, 0, unroll=2)
        for b in range(slab // rows):
            window = pl.ds(b * rows, rows + 2 * reach)
            at = pl.ds(b * rows, rows)
            one = product(m_all[...], high_x[window, :])
            two = product(m_top[...], low_x[window, :])
            along[0, p, at, :] = one[:rows] + one[2 * rows :] + two[:rows]
            curve = (gain / 180.0) * (one[rows : 2 * rows] + two[rows:])
            sums[0, p, at, :] = sums[0, p, at, :] + curve
        for t in range(tiles):
            side = pl.ds(t * lanes, lanes)
            window = pl.ds(t * lanes, 2 * lanes)
            both = product(high_s[:, window], turn[...]) + product(low_s[:, window], turn[...])
            across[0, p, :, side] = both[:, :lanes] * (1.0 / 60.0)
            curve = both[:, lanes:] * (gain / 180.0)
            sums[0, p, :, side] = sums[0, p, :, side] + curve
    token[...] = jnp.zeros_like(token)


def field_terms(c, field, before, after, viscosity, length):
    comps, slab, planes, width = field.shape
    flat = field.reshape(comps, slab * planes, width)
    rows = min(slab, 128)
    high, low, second = along_matrices(rows, length)
    top = np.concatenate([high, second], 0)
    everything = np.concatenate([high, second, low], 0)
    rim = pl.BlockSpec((1, reach, 2, width), lambda i: (c, 0, 0, 0))
    turn = across_matrix([first_at(0), [t for t in second_at(0) if t[0] != 0]])
    shape = jax.ShapeDtypeStruct((1, 2, slab, width), jnp.float32)
    spec = pl.BlockSpec((1, 2, slab, width), lambda i: (0, 0, 0, 0))
    mark = pl.BlockSpec((8, lanes), lambda i: (0, 0))
    return pl.pallas_call(
        functools.partial(field_kernel, c),
        out_shape=(shape,) * 5 + (jax.ShapeDtypeStruct((8, lanes), jnp.int32),),
        grid=(1,),
        in_specs=[
            pl.BlockSpec(memory_space=pltpu.SMEM),
            pl.BlockSpec(turn.shape, lambda i: (0, 0)),
            pl.BlockSpec(everything.shape, lambda i: (0, 0)),
            pl.BlockSpec(top.shape, lambda i: (0, 0)),
            rim,
            rim,
            pl.BlockSpec(memory_space=pl.ANY),
        ],
        out_specs=(spec,) * 5 + (mark,),
        compiler_params=grant(57),
        scratch_shapes=[
            pltpu.VMEM((width // lanes, slab * planes, lanes), jnp.float32),
            pltpu.VMEM((slab, width + lanes), jnp.bfloat16),
            pltpu.VMEM((slab, width + lanes), jnp.bfloat16),
            pltpu.VMEM((slab + 2 * reach, width), jnp.bfloat16),
            pltpu.VMEM((slab + 2 * reach, width), jnp.bfloat16),
            pltpu.SemaphoreType.DMA((width // lanes,)),
        ],
        cost_estimate=pl.CostEstimate(
            flops=0, bytes_accessed=4 * slab * planes * width * 2, transcendentals=0
        ),
    )(
        viscosity, jnp.asarray(turn), jnp.asarray(everything), jnp.asarray(top), before, after, flat
    )


def final_kernel(core, m_both, turn, held0, other0, held1, other1, before, after, *refs):
    terms, scratch = refs[:15], refs[15:]
    inner, depth, along, across, sums = [terms[n::5] for n in range(5)]
    out, base_s, turned_s, flow_s, ghost_s, slope_s, side_s, arrived = scratch
    step = pl.program_id(0)
    rows = slope_s.shape[2]
    quarter = held0.shape[3]
    slab = 4 * quarter
    inverse = 1.0 / code_scale

    def decoded(values):
        return values.astype(jnp.int32).astype(jnp.float32) * inverse

    def load(flow, ghost):
        copies = []
        for u in range(2):
            for k in range(2):
                at = pl.ds(streams[u][k] * quarter, quarter)
                for n, (source, target) in enumerate(((flow, flow_s), (ghost, ghost_s))):
                    copies.append(
                        pltpu.make_async_copy(
                            source[u].at[k], target.at[:, :, at], arrived.at[4 * n + 2 * u + k]
                        )
                    )
        for copy in copies:
            copy.start()
        for copy in copies:
            copy.wait()

    @pl.when(step == 0)
    def _():
        for c in range(3):
            for p in range(2):
                base_s[c, p, 0:reach] = decoded(before[p, c]).astype(jnp.bfloat16)
                base_s[c, p, reach + slab :] = decoded(after[p, c]).astype(jnp.bfloat16)

        @pl.when(core[0] == 0)
        def _():
            load((held0, held1), (other0, other1))

        @pl.when(core[0] != 0)
        def _():
            load((other0, other1), (held0, held1))

        def fill(i, carry):
            start = pl.multiple_of(i * 16, 16)
            to = pl.ds(pl.multiple_of(start + reach, 16), 16)
            for c in range(3):
                for p in range(2):
                    values = decoded(flow_s[p, c, pl.ds(start, 16), :])
                    base_s[c, p, to, :] = values.astype(jnp.bfloat16)
            return carry

        lax.fori_loop(0, slab // 16, fill, 0)

    origin = pl.multiple_of(step * rows, 32)
    def derive(c, carry):
        for p in range(2):
            both = product(m_both[...], base_s[c, p, pl.ds(origin, rows + 2 * reach), :])
            slope_s[c, p] = both[:rows] + both[rows:]
            for r in range(0, rows, 16):
                here = pl.ds(pl.multiple_of(origin + reach + r, 16), 16)
                turned_s[r : r + 16, :] = half_turned(base_s[c, p, here, :])
            for t in range(side_s.shape[3] // lanes):
                window = turned_s[:, pl.ds(t * lanes, 2 * lanes)]
                side_s[c, p, :, pl.ds(t * lanes, lanes)] = product(window, turn[...])
        return carry

    lax.fori_loop(0, 3, derive, 0)

    def body(i, carry):
        start = pl.multiple_of(i * 16, 16)
        at = pl.ds(start, 16)
        there = pl.ds(pl.multiple_of(origin + start, 16), 16)
        inside = pl.ds(pl.multiple_of(origin + reach + start, 16), 16)
        flow = [
            [base_s[c, p, inside, :].astype(jnp.float32) for p in range(2)] for c in range(3)
        ]
        for p in range(2):
            move = [inner[c][0, p, at, :] for c in range(3)]
            for c in range(3):
                dz = decoded(ghost_s[p, c, there, :])
                if p == 0:
                    dz = dz + 0.75 * flow[c][1]
                else:
                    dz = dz - 0.75 * flow[c][0]
                dy = side_s[c, p, at, :] * (1.0 / 60.0)
                total = flow[0][p] * along[c][0, p, at, :] + flow[1][p] * across[c][0, p, at, :]
                total = total + flow[2][p] * depth[c][0, p, at, :]
                total = total + move[0] * slope_s[c, p, at, :] + move[1] * dy + move[2] * dz
                out[0, c, at, p, :] = sums[c][0, p, at, :] - section_step * total
        return carry

    lax.fori_loop(0, rows // 16, body, 0)


def final(core, pieces, before, after, terms, length):
    _, pair, slab, width = terms[0].shape
    comps = len(terms) // 5
    rows = min(slab, 32)
    turn = across_matrix([first_at(0)])
    high, low, _ = along_matrices(rows, length)
    both = np.concatenate([high, low], 0)
    whole = pl.BlockSpec(memory_space=pl.ANY)
    rim = pl.BlockSpec(before.shape, lambda i: (0, 0, 0, 0))
    spec = pl.BlockSpec((1, pair, rows, width), lambda i: (0, 0, i, 0))
    return pl.pallas_call(
        final_kernel,
        out_shape=jax.ShapeDtypeStruct((1, comps, slab, pair, width), jnp.float32),
        grid=(slab // rows,),
        in_specs=[
            pl.BlockSpec(memory_space=pltpu.SMEM),
            pl.BlockSpec(both.shape, lambda i: (0, 0)),
            pl.BlockSpec(turn.shape, lambda i: (0, 0)),
        ]
        + [whole] * 4
        + [rim] * 2
        + [spec] * 15,
        out_specs=pl.BlockSpec((1, comps, rows, pair, width), lambda i: (0, 0, i, 0, 0)),
        compiler_params=grant(58),
        scratch_shapes=[
            pltpu.VMEM((comps, pair, slab + 2 * reach, width), jnp.bfloat16),
            pltpu.VMEM((rows, width + lanes), jnp.bfloat16),
            pltpu.VMEM((pair, comps, slab, width), jnp.int16),
            pltpu.VMEM((pair, comps, slab, width), jnp.int16),
            pltpu.VMEM((comps, pair, rows, width), jnp.float32),
            pltpu.VMEM((comps, pair, rows, width), jnp.float32),
            pltpu.SemaphoreType.DMA((8,)),
        ],
        cost_estimate=pl.CostEstimate(
            flops=0, bytes_accessed=8 * comps * pair * slab * width, transcendentals=0
        ),
    )(core, jnp.asarray(both), jnp.asarray(turn), *pieces, before, after, *terms)


def ring(last, first):
    size = lax.axis_size("gx")
    up = [(i, (i + 1) % size) for i in range(size)]
    down = [(j, i) for i, j in up]
    return lax.ppermute(last, "gx", up), lax.ppermute(first, "gx", down)


def swap(array, bit):
    return lax.ppermute(array, "pert", [(i, i ^ bit) for i in range(lax.axis_size("pert"))])


def exchange(mine, theirs, root, core, gate, work):
    me = lax.axis_index("pert")
    is_root = me == root
    place = (me // 2) ^ (root // 2)
    at_a, at_b, at_c = place == 0, place == 1, place == 2
    handed = [swap(t, 1) for t in theirs]

    def owned(u, h, k):
        return jnp.where(is_root, mine[u][h, k], handed[u][h, k])

    opening = [owned(u, h, 0) for u in range(2) for h in range(2)]
    opening = gate(*opening)
    source = [
        [[opening[2 * u + h]] + [owned(u, h, k) for k in range(1, phases)] for h in range(2)]
        for u in range(2)
    ]
    X = [[], []]
    Y = [[], []]
    for s in range(phases + 1):
        for u in range(2):
            k = min(s, phases - 1)
            one, two = source[u][0][k], source[u][1][k]
            if s == phases:
                one, two = two, one
            if s > 0:
                one = jnp.where(at_a, one, Y[u][s - 1])
                two = jnp.where(at_a, two, X[u][s - 1])
                one, two, place = gate(one, two, place)
                at_a, at_b, at_c = place == 0, place == 1, place == 2
            X[u].append(swap(one, 2))
            Y[u].append(swap(two, 4))
            if (s, u) in shares:
                place = place + work(shares[s, u])
                at_a, at_b, at_c = place == 0, place == 1, place == 2
    held = []
    for u in range(2):
        parts = []
        for k in range(phases):
            row = []
            for h in range(2):
                P1, P2 = (X[u], Y[u]) if h == 0 else (Y[u], X[u])
                near, far = (at_b, at_c) if h == 0 else (at_c, at_b)
                late = P1[k + 2] if k + 2 <= phases else P2[phases]
                value = jnp.where(near, P1[k], jnp.where(far, late, P2[k + 1]))
                row.append(jnp.where(at_a, source[u][h][k], value))
            parts.append(jnp.stack(row, 0))
        held.append(jnp.stack(parts, 0))
        if u == 0:
            quarter = held[0].shape[3]
            size = lax.axis_size("gx")
            pairs = [
                (c * size + i, c * size + (i + 1) % size)
                for c in range(0, lax.axis_size("pert"), 2)
                for i in range(size)
            ]
            both = ("pert", "gx")
            before = lax.ppermute(held[0][1][:, :, quarter - reach :], both, pairs)
            after = lax.ppermute(held[0][0][:, :, :reach], both, [(j, i) for i, j in pairs])
            rims = jnp.stack([before, after], 0)
            before, after, place = lax.optimization_barrier((before, after, place))
            at_a, at_b, at_c = place == 0, place == 1, place == 2
    other = [swap(h, 1) for h in held]
    rims = jnp.where(core == 0, rims, swap(rims, 1))
    return (held[0], other[0], held[1], other[1]), rims[0], rims[1]


def per_device(pert_field, base_store, section_owner, pert_ids, member_visc):
    _, comps, slab, planes, width = pert_field.shape
    length = slab * lax.axis_size("gx")
    member_pick = pert_ids[0] == jnp.arange(member_visc.shape[0], dtype=jnp.int32)
    viscosity = jnp.sum(jnp.where(member_pick, member_visc, 0.0))[None]
    levels_here = base_store.shape[0]
    owner_slot = section_owner[0] % levels_here
    owner_root = section_owner[0] // levels_here
    tiles = base_store.reshape(levels_here, comps, slab * planes, width)
    tile = tiles[0] if levels_here == 1 else lax.dynamic_index_in_dim(tiles, owner_slot, 0, False)
    me = lax.axis_index("pert")
    in_pairs = lax.axis_size("pert") == 8
    core = (me % 2 if in_pairs else jnp.zeros_like(me)).astype(jnp.int32)[None]
    field = pert_field[0]
    last, first, tile = lax.optimization_barrier(
        (field[:, slab - reach :, 3:5], field[:, :reach, 3:5], tile)
    )
    before, after = ring(last, first)
    halves = [pack(tile, planes, core, u) for u in range(2)]
    done = {"field": field, "terms": []}

    def gate(*values):
        done["field"], *values = lax.optimization_barrier((done["field"], *values))
        return values

    def work(c):
        *terms, token = field_terms(c, done["field"], before, after, viscosity, length)
        done["terms"] += terms
        return token[0, 0]

    if in_pairs:
        mine, theirs = [h[0] for h in halves], [h[1] for h in halves]
        pieces, base_before, base_after = exchange(mine, theirs, owner_root, core[0], gate, work)
    else:
        for c in range(comps):
            work(c)
        pieces = [
            lax.psum(jnp.where(me == owner_root, a, 0).astype(jnp.float32), "pert").astype(a.dtype)
            for h in halves
            for a in h
        ]
        pieces = [a.transpose(1, 0, 2, 3, 4) for a in pieces]
        quarter = slab // 4
        base_before, base_after = ring(
            pieces[0][1][:, :, quarter - reach :], pieces[0][0][:, :, :reach]
        )
    return final(core, pieces, base_before, base_after, done["terms"], length)


def solution(mesh):
    placed = (
        P("pert", None, "gx", None, None),
        P("pert", None, "gx", None, None),
        P(),
        P("pert"),
        P(),
    )
    return jax.shard_map(
        per_device,
        mesh=mesh,
        in_specs=placed,
        out_specs=P("pert", None, "gx", None, None),
        check_vma=False,
    )
```

```python
import functools

import jax
import jax.numpy as jnp
import numpy as np
from jax import lax
from jax.experimental import pallas as pl
from jax.experimental.pallas import tpu as pltpu
from jax.sharding import PartitionSpec as P

section_step = 0.25
reach = 16
lanes = 128
code_scale = 4096.0
phases = 2
streams = ((0, 3), (1, 2))
shares = {(0, 1): 0, (1, 1): 1, (2, 0): 2}


def grant(mib):
    return pltpu.CompilerParams(vmem_limit_bytes=mib << 20)


def compact_kernel(length):
    wave = 2.0 * np.pi * np.arange(length) / length
    symbol = 14.0 / 9.0 * np.sin(wave) + 1.0 / 18.0 * np.sin(2.0 * wave)
    symbol = 1j * symbol / (1.0 + 2.0 / 3.0 * np.cos(wave))
    return np.real(np.fft.ifft(symbol))


def along_matrices(rows, length):
    kernel = compact_kernel(length)
    first = np.zeros((rows, rows + 2 * reach))
    second = np.zeros((rows, rows + 2 * reach))
    for i in range(rows):
        for k in range(-reach, reach + 1):
            first[i, i + reach + k] = kernel[-k % length]
        for k, weight in ((0, -980.0), (1, 270.0), (2, -27.0), (3, 2.0)):
            second[i, i + reach + k] = weight
            second[i, i + reach - k] = weight
    high = first.astype(jnp.bfloat16)
    low = (first - high.astype(np.float64)).astype(jnp.bfloat16)
    return high, low, second.astype(jnp.bfloat16)


first_taps = ((1, 45.0), (2, -9.0), (3, 1.0))
second_taps = ((0, -490.0), (1, 270.0), (2, -27.0), (3, 2.0))


def depth_matrix(rows, planes, fields):
    matrix = np.zeros((len(fields) * rows, rows * planes))
    for f, taps in enumerate(fields):
        for i in range(rows):
            for z, weight in taps:
                matrix[f * rows + i, i * planes + z] += weight
    return matrix.astype(jnp.bfloat16)


def first_at(z):
    return [(z + k, w) for k, w in first_taps] + [(z - k, -w) for k, w in first_taps]


def second_at(z):
    taps = [(z + k, w) for k, w in second_taps]
    return taps + [(z - k, w) for k, w in second_taps if k > 0]


def across_matrix(orders):
    matrix = np.zeros((2 * lanes, lanes * len(orders)))
    for o, taps in enumerate(orders):
        for i in range(lanes):
            for k, weight in taps:
                matrix[lanes // 2 + i + k, o * lanes + i] += weight
    return matrix.astype(jnp.bfloat16)


def half_turned(values):
    half = lanes // 2
    return jnp.concatenate([values[:, -half:], values, values[:, :half]], 1)


def product(a, b):
    return jnp.dot(a, b, preferred_element_type=jnp.float32)


def split(values):
    high = values.astype(jnp.bfloat16)
    return high, (values - high.astype(jnp.float32)).astype(jnp.bfloat16)


def pack_kernel(core, weights, tile, mine, theirs):
    rows = weights.shape[0] // 4
    blocks = mine.shape[3] // rows

    def store(kept, sent):
        for b in range(blocks):
            depth = weights.shape[1]
            mixed = product(weights[...], tile[0, b * depth : (b + 1) * depth])
            for f in range(4):
                scale = code_scale if f < 2 else code_scale / 60.0
                part = jnp.round(mixed[f * rows : (f + 1) * rows] * scale)
                target = kept if f < 2 else sent
                code = part.astype(jnp.int32).astype(jnp.int16)
                target[f % 2, 0, 0, b * rows : (b + 1) * rows] = code

    @pl.when(core[0] == 0)
    def _():
        store(mine, theirs)

    @pl.when(core[0] != 0)
    def _():
        store(theirs, mine)


def pack(tile, planes, core, which):
    comps, deep, width = tile.shape
    quarter = deep // planes // 4
    x_rows = min(quarter, 32)
    ghost = [[t for t in first_at(z) if t[0] not in (3, 4)] for z in (3, 4)]
    weights = depth_matrix(x_rows, planes, [[(3, 1.0)], [(4, 1.0)]] + ghost)
    first, second = streams[which]
    shape = jax.ShapeDtypeStruct((2, 2, comps, quarter, width), jnp.int16)
    spec = pl.BlockSpec((2, 1, 1, quarter, width), lambda k, c: (0, k, c, 0, 0))
    return pl.pallas_call(
        pack_kernel,
        out_shape=(shape,) * 2,
        grid=(2, comps),
        in_specs=[
            pl.BlockSpec(memory_space=pltpu.SMEM),
            pl.BlockSpec(weights.shape, lambda k, c: (0, 0)),
            pl.BlockSpec(
                (1, quarter * planes, width), lambda k, c: (c, first + k * (second - first), 0)
            ),
        ],
        out_specs=(spec,) * 2,
        compiler_params=grant(16),
        cost_estimate=pl.CostEstimate(
            flops=0, bytes_accessed=2 * comps * deep * width, transcendentals=0
        ),
    )(core, jnp.asarray(weights), tile)


def field_kernel(
    c, viscosity, turn, m_all, m_top, before, after, field, *refs
):
    outs, token, terms = refs[:5], refs[5], refs[6:11]
    columns, high_s, low_s, high_x, low_x, arrived, left = refs[11:]
    inner, depth, along, across, sums = terms

    def send(n, p):
        return pltpu.make_async_copy(terms[n].at[0, p], outs[n].at[0, p], left.at[n, p])

    slab, width = inner.shape[2:]
    planes = field.shape[1] // slab
    tiles = width // lanes
    gain = viscosity[0] * section_step

    def fetch(t):
        source = field.at[c, :, pl.ds(t * lanes, lanes)]
        return pltpu.make_async_copy(source, columns.at[t], arrived.at[t])

    for t in range(tiles):
        fetch(t).start()
    for t in range(tiles):
        fetch(t).wait()

        def unpack(i, carry):
            start = pl.multiple_of(i * 8, 8)
            plane = [columns[t, pl.ds(start * planes + z, 8, planes), :] for z in range(planes)]
            at = (pl.ds(start, 8), pl.ds(t * lanes, lanes))
            for p in range(2):
                z = 3 + p
                centre = plane[z]
                u1, u2, u3 = plane[z + 1], plane[z + 2], plane[z + 3]
                d1, d2, d3 = plane[z - 1], plane[z - 2], plane[z - 3]
                slope = 0.75 * (u1 - d1) - 0.15 * (u2 - d2) + (1.0 / 60.0) * (u3 - d3)
                curve = 1.5 * (u1 + d1) - 0.15 * (u2 + d2) + (1.0 / 90.0) * (u3 + d3)
                inner[(0, p) + at] = centre
                depth[(0, p) + at] = slope
                sums[(0, p) + at] = centre + gain * (curve - (49.0 / 18.0) * centre)
            return carry

        lax.fori_loop(0, slab // 8, unpack, 0, unroll=4)

    for p in range(2):
        send(0, p).start()
        send(1, p).start()
    rows = m_top.shape[0] // 2
    for p in range(2):
        for start, rim in ((0, before), (reach + slab, after)):
            high, low = split(rim[c, :, p])
            high_x[start : start + reach, :] = high
            low_x[start : start + reach, :] = low

        def fill(i, carry):
            start = pl.multiple_of(i * 16, 16)
            at = pl.ds(start, 16)
            to = pl.ds(pl.multiple_of(start + reach, 16), 16)
            high, low = split(inner[0, p, at, :])
            high_x[to, :] = high
            low_x[to, :] = low
            high_s[at, :] = half_turned(high)
            low_s[at, :] = half_turned(low)
            return carry

        lax.fori_loop(0, slab // 16, fill, 0, unroll=2)
        for b in range(slab // rows):
            window = pl.ds(b * rows, rows + 2 * reach)
            at = pl.ds(b * rows, rows)
            one = product(m_all[...], high_x[window, :])
            two = product(m_top[...], low_x[window, :])
            along[0, p, at, :] = one[:rows] + one[2 * rows :] + two[:rows]
            curve = (gain / 180.0) * (one[rows : 2 * rows] + two[rows:])
            sums[0, p, at, :] = sums[0, p, at, :] + curve
        send(2, p).start()
        for t in range(tiles):
            side = pl.ds(t * lanes, lanes)
            window = pl.ds(t * lanes, 2 * lanes)
            both = product(high_s[:, window], turn[...]) + product(low_s[:, window], turn[...])
            across[0, p, :, side] = both[:, :lanes] * (1.0 / 60.0)
            curve = both[:, lanes:] * (gain / 180.0)
            sums[0, p, :, side] = sums[0, p, :, side] + curve
        send(3, p).start()
        send(4, p).start()
    token[...] = jnp.zeros_like(token)
    for n in range(5):
        for p in range(2):
            send(n, p).wait()


def field_terms(c, field, before, after, viscosity, length):
    comps, slab, planes, width = field.shape
    flat = field.reshape(comps, slab * planes, width)
    rows = min(slab, 128)
    high, low, second = along_matrices(rows, length)
    top = np.concatenate([high, second], 0)
    everything = np.concatenate([high, second, low], 0)
    turn = across_matrix([first_at(0), [t for t in second_at(0) if t[0] != 0]])
    shape = jax.ShapeDtypeStruct((1, 2, slab, width), jnp.float32)
    spec = pl.BlockSpec(memory_space=pltpu.HBM)
    near = pl.BlockSpec(memory_space=pltpu.VMEM)
    return pl.pallas_call(
        functools.partial(field_kernel, c),
        out_shape=(shape,) * 5 + (jax.ShapeDtypeStruct((8, lanes), jnp.int32),),
        in_specs=[pl.BlockSpec(memory_space=pltpu.SMEM)]
        + [near] * 5
        + [pl.BlockSpec(memory_space=pl.ANY)],
        out_specs=(spec,) * 5 + (near,),
        compiler_params=grant(57),
        scratch_shapes=[pltpu.VMEM((1, 2, slab, width), jnp.float32)] * 5
        + [
            pltpu.VMEM((width // lanes, slab * planes, lanes), jnp.float32),
            pltpu.VMEM((slab, width + lanes), jnp.bfloat16),
            pltpu.VMEM((slab, width + lanes), jnp.bfloat16),
            pltpu.VMEM((slab + 2 * reach, width), jnp.bfloat16),
            pltpu.VMEM((slab + 2 * reach, width), jnp.bfloat16),
            pltpu.SemaphoreType.DMA((width // lanes,)),
            pltpu.SemaphoreType.DMA((5, 2)),
        ],
        cost_estimate=pl.CostEstimate(
            flops=0, bytes_accessed=4 * slab * planes * width * 2, transcendentals=0
        ),
    )(
        viscosity, jnp.asarray(turn), jnp.asarray(everything), jnp.asarray(top), before, after, flat
    )


def final_kernel(core, m_both, turn, held0, other0, held1, other1, before, after, *refs):
    terms, scratch = refs[:15], refs[15:]
    inner, depth, along, across, sums = [terms[n::5] for n in range(5)]
    out, base_s, turned_s, flow_s, ghost_s, slope_s, side_s, arrived = scratch
    step = pl.program_id(0)
    rows = slope_s.shape[2]
    quarter = held0.shape[3]
    slab = 4 * quarter
    inverse = 1.0 / code_scale

    def decoded(values):
        return values.astype(jnp.int32).astype(jnp.float32) * inverse

    def load(flow, ghost):
        copies = []
        for u in range(2):
            for k in range(2):
                at = pl.ds(streams[u][k] * quarter, quarter)
                for n, (source, target) in enumerate(((flow, flow_s), (ghost, ghost_s))):
                    copies.append(
                        pltpu.make_async_copy(
                            source[u].at[k], target.at[:, :, at], arrived.at[4 * n + 2 * u + k]
                        )
                    )
        for copy in copies:
            copy.start()
        for copy in copies:
            copy.wait()

    @pl.when(step == 0)
    def _():
        for c in range(3):
            for p in range(2):
                base_s[c, p, 0:reach] = decoded(before[p, c]).astype(jnp.bfloat16)
                base_s[c, p, reach + slab :] = decoded(after[p, c]).astype(jnp.bfloat16)

        @pl.when(core[0] == 0)
        def _():
            load((held0, held1), (other0, other1))

        @pl.when(core[0] != 0)
        def _():
            load((other0, other1), (held0, held1))

        def fill(i, carry):
            start = pl.multiple_of(i * 16, 16)
            to = pl.ds(pl.multiple_of(start + reach, 16), 16)
            for c in range(3):
                for p in range(2):
                    values = decoded(flow_s[p, c, pl.ds(start, 16), :])
                    base_s[c, p, to, :] = values.astype(jnp.bfloat16)
            return carry

        lax.fori_loop(0, slab // 16, fill, 0)

    origin = pl.multiple_of(step * rows, 32)
    def derive(c, carry):
        for p in range(2):
            both = product(m_both[...], base_s[c, p, pl.ds(origin, rows + 2 * reach), :])
            slope_s[c, p] = both[:rows] + both[rows:]
            for r in range(0, rows, 16):
                here = pl.ds(pl.multiple_of(origin + reach + r, 16), 16)
                turned_s[r : r + 16, :] = half_turned(base_s[c, p, here, :])
            for t in range(side_s.shape[3] // lanes):
                window = turned_s[:, pl.ds(t * lanes, 2 * lanes)]
                side_s[c, p, :, pl.ds(t * lanes, lanes)] = product(window, turn[...])
        return carry

    lax.fori_loop(0, 3, derive, 0)

    def body(i, carry):
        start = pl.multiple_of(i * 16, 16)
        at = pl.ds(start, 16)
        there = pl.ds(pl.multiple_of(origin + start, 16), 16)
        inside = pl.ds(pl.multiple_of(origin + reach + start, 16), 16)
        flow = [
            [base_s[c, p, inside, :].astype(jnp.float32) for p in range(2)] for c in range(3)
        ]
        for p in range(2):
            move = [inner[c][0, p, at, :] for c in range(3)]
            for c in range(3):
                dz = decoded(ghost_s[p, c, there, :])
                if p == 0:
                    dz = dz + 0.75 * flow[c][1]
                else:
                    dz = dz - 0.75 * flow[c][0]
                dy = side_s[c, p, at, :] * (1.0 / 60.0)
                total = flow[0][p] * along[c][0, p, at, :] + flow[1][p] * across[c][0, p, at, :]
                total = total + flow[2][p] * depth[c][0, p, at, :]
                total = total + move[0] * slope_s[c, p, at, :] + move[1] * dy + move[2] * dz
                out[0, c, at, p, :] = sums[c][0, p, at, :] - section_step * total
        return carry

    lax.fori_loop(0, rows // 16, body, 0)


def final(core, pieces, before, after, terms, length):
    _, pair, slab, width = terms[0].shape
    comps = len(terms) // 5
    rows = min(slab, 32)
    turn = across_matrix([first_at(0)])
    high, low, _ = along_matrices(rows, length)
    both = np.concatenate([high, low], 0)
    whole = pl.BlockSpec(memory_space=pl.ANY)
    rim = pl.BlockSpec(before.shape, lambda i: (0, 0, 0, 0))
    spec = pl.BlockSpec((1, pair, rows, width), lambda i: (0, 0, i, 0))
    return pl.pallas_call(
        final_kernel,
        out_shape=jax.ShapeDtypeStruct((1, comps, slab, pair, width), jnp.float32),
        grid=(slab // rows,),
        in_specs=[
            pl.BlockSpec(memory_space=pltpu.SMEM),
            pl.BlockSpec(both.shape, lambda i: (0, 0)),
            pl.BlockSpec(turn.shape, lambda i: (0, 0)),
        ]
        + [whole] * 4
        + [rim] * 2
        + [spec] * 15,
        out_specs=pl.BlockSpec((1, comps, rows, pair, width), lambda i: (0, 0, i, 0, 0)),
        compiler_params=grant(58),
        scratch_shapes=[
            pltpu.VMEM((comps, pair, slab + 2 * reach, width), jnp.bfloat16),
            pltpu.VMEM((rows, width + lanes), jnp.bfloat16),
            pltpu.VMEM((pair, comps, slab, width), jnp.int16),
            pltpu.VMEM((pair, comps, slab, width), jnp.int16),
            pltpu.VMEM((comps, pair, rows, width), jnp.float32),
            pltpu.VMEM((comps, pair, rows, width), jnp.float32),
            pltpu.SemaphoreType.DMA((8,)),
        ],
        cost_estimate=pl.CostEstimate(
            flops=0, bytes_accessed=8 * comps * pair * slab * width, transcendentals=0
        ),
    )(core, jnp.asarray(both), jnp.asarray(turn), *pieces, before, after, *terms)


def ring(last, first):
    size = lax.axis_size("gx")
    up = [(i, (i + 1) % size) for i in range(size)]
    down = [(j, i) for i, j in up]
    return lax.ppermute(last, "gx", up), lax.ppermute(first, "gx", down)


def swap(array, bit):
    return lax.ppermute(array, "pert", [(i, i ^ bit) for i in range(lax.axis_size("pert"))])


def exchange(mine, theirs, root, core, gate, work):
    me = lax.axis_index("pert")
    is_root = me == root
    place = (me // 2) ^ (root // 2)
    at_a, at_b, at_c = place == 0, place == 1, place == 2
    handed = [swap(t, 1) for t in theirs]

    def owned(u, h, k):
        return jnp.where(is_root, mine[u][h, k], handed[u][h, k])

    opening = [owned(u, h, 0) for u in range(2) for h in range(2)]
    opening = gate(*opening)
    source = [
        [[opening[2 * u + h]] + [owned(u, h, k) for k in range(1, phases)] for h in range(2)]
        for u in range(2)
    ]
    X = [[], []]
    Y = [[], []]
    for s in range(phases + 1):
        for u in range(2):
            k = min(s, phases - 1)
            one, two = source[u][0][k], source[u][1][k]
            if s == phases:
                one, two = two, one
            if s > 0:
                one = jnp.where(at_a, one, Y[u][s - 1])
                two = jnp.where(at_a, two, X[u][s - 1])
                one, two, place = gate(one, two, place)
                at_a, at_b, at_c = place == 0, place == 1, place == 2
            X[u].append(swap(one, 2))
            Y[u].append(swap(two, 4))
            if (s, u) in shares:
                place = place + work(shares[s, u])
                at_a, at_b, at_c = place == 0, place == 1, place == 2
    held = []
    for u in range(2):
        parts = []
        for k in range(phases):
            row = []
            for h in range(2):
                P1, P2 = (X[u], Y[u]) if h == 0 else (Y[u], X[u])
                near, far = (at_b, at_c) if h == 0 else (at_c, at_b)
                late = P1[k + 2] if k + 2 <= phases else P2[phases]
                value = jnp.where(near, P1[k], jnp.where(far, late, P2[k + 1]))
                row.append(jnp.where(at_a, source[u][h][k], value))
            parts.append(jnp.stack(row, 0))
        held.append(jnp.stack(parts, 0))
        if u == 0:
            quarter = held[0].shape[3]
            size = lax.axis_size("gx")
            pairs = [
                (c * size + i, c * size + (i + 1) % size)
                for c in range(0, lax.axis_size("pert"), 2)
                for i in range(size)
            ]
            both = ("pert", "gx")
            before = lax.ppermute(held[0][1][:, :, quarter - reach :], both, pairs)
            after = lax.ppermute(held[0][0][:, :, :reach], both, [(j, i) for i, j in pairs])
            rims = jnp.stack([before, after], 0)
            before, after, place = lax.optimization_barrier((before, after, place))
            at_a, at_b, at_c = place == 0, place == 1, place == 2
    other = [swap(h, 1) for h in held]
    rims = jnp.where(core == 0, rims, swap(rims, 1))
    return (held[0], other[0], held[1], other[1]), rims[0], rims[1]


def per_device(pert_field, base_store, section_owner, pert_ids, member_visc):
    _, comps, slab, planes, width = pert_field.shape
    length = slab * lax.axis_size("gx")
    member_pick = pert_ids[0] == jnp.arange(member_visc.shape[0], dtype=jnp.int32)
    viscosity = jnp.sum(jnp.where(member_pick, member_visc, 0.0))[None]
    levels_here = base_store.shape[0]
    owner_slot = section_owner[0] % levels_here
    owner_root = section_owner[0] // levels_here
    tiles = base_store.reshape(levels_here, comps, slab * planes, width)
    tile = tiles[0] if levels_here == 1 else lax.dynamic_index_in_dim(tiles, owner_slot, 0, False)
    me = lax.axis_index("pert")
    in_pairs = lax.axis_size("pert") == 8
    core = (me % 2 if in_pairs else jnp.zeros_like(me)).astype(jnp.int32)[None]
    field = pert_field[0]
    last, first, tile = lax.optimization_barrier(
        (field[:, slab - reach :, 3:5], field[:, :reach, 3:5], tile)
    )
    before, after = ring(last, first)
    halves = [pack(tile, planes, core, u) for u in range(2)]
    done = {"field": field, "terms": []}

    def gate(*values):
        done["field"], *values = lax.optimization_barrier((done["field"], *values))
        return values

    def work(c):
        *terms, token = field_terms(c, done["field"], before, after, viscosity, length)
        done["terms"] += terms
        return token[0, 0]

    if in_pairs:
        mine, theirs = [h[0] for h in halves], [h[1] for h in halves]
        pieces, base_before, base_after = exchange(mine, theirs, owner_root, core[0], gate, work)
    else:
        for c in range(comps):
            work(c)
        pieces = [
            lax.psum(jnp.where(me == owner_root, a, 0).astype(jnp.float32), "pert").astype(a.dtype)
            for h in halves
            for a in h
        ]
        pieces = [a.transpose(1, 0, 2, 3, 4) for a in pieces]
        quarter = slab // 4
        base_before, base_after = ring(
            pieces[0][1][:, :, quarter - reach :], pieces[0][0][:, :, :reach]
        )
    return final(core, pieces, base_before, base_after, done["terms"], length)


def solution(mesh):
    placed = (
        P("pert", None, "gx", None, None),
        P("pert", None, "gx", None, None),
        P(),
        P("pert"),
        P(),
    )
    return jax.shard_map(
        per_device,
        mesh=mesh,
        in_specs=placed,
        out_specs=P("pert", None, "gx", None, None),
        check_vma=False,
    )
```

```python
import functools

import jax
import jax.numpy as jnp
import numpy as np
from jax import lax
from jax.experimental import pallas as pl
from jax.experimental.pallas import tpu as pltpu
from jax.sharding import PartitionSpec as P

section_step = 0.25
reach = 16
lanes = 128
code_scale = 4096.0
phases = 2
streams = ((0, 3), (1, 2))
shares = {(0, 1): ((0, 1), 44), (1, 1): ((2,), 52)}


def grant(mib):
    return pltpu.CompilerParams(vmem_limit_bytes=mib << 20)


def compact_kernel(length):
    wave = 2.0 * np.pi * np.arange(length) / length
    symbol = 14.0 / 9.0 * np.sin(wave) + 1.0 / 18.0 * np.sin(2.0 * wave)
    symbol = 1j * symbol / (1.0 + 2.0 / 3.0 * np.cos(wave))
    return np.real(np.fft.ifft(symbol))


def along_matrices(rows, length):
    kernel = compact_kernel(length)
    first = np.zeros((rows, rows + 2 * reach))
    second = np.zeros((rows, rows + 2 * reach))
    for i in range(rows):
        for k in range(-reach, reach + 1):
            first[i, i + reach + k] = kernel[-k % length]
        for k, weight in ((0, -980.0), (1, 270.0), (2, -27.0), (3, 2.0)):
            second[i, i + reach + k] = weight
            second[i, i + reach - k] = weight
    high = first.astype(jnp.bfloat16)
    low = (first - high.astype(np.float64)).astype(jnp.bfloat16)
    return high, low, second.astype(jnp.bfloat16)


first_taps = ((1, 45.0), (2, -9.0), (3, 1.0))
second_taps = ((0, -490.0), (1, 270.0), (2, -27.0), (3, 2.0))


def depth_matrix(rows, planes, fields):
    matrix = np.zeros((len(fields) * rows, rows * planes))
    for f, taps in enumerate(fields):
        for i in range(rows):
            for z, weight in taps:
                matrix[f * rows + i, i * planes + z] += weight
    return matrix.astype(jnp.bfloat16)


def first_at(z):
    return [(z + k, w) for k, w in first_taps] + [(z - k, -w) for k, w in first_taps]


def second_at(z):
    taps = [(z + k, w) for k, w in second_taps]
    return taps + [(z - k, w) for k, w in second_taps if k > 0]


def across_matrix(orders):
    matrix = np.zeros((2 * lanes, lanes * len(orders)))
    for o, taps in enumerate(orders):
        for i in range(lanes):
            for k, weight in taps:
                matrix[lanes // 2 + i + k, o * lanes + i] += weight
    return matrix.astype(jnp.bfloat16)


def half_turned(values):
    half = lanes // 2
    return jnp.concatenate([values[:, -half:], values, values[:, :half]], 1)


def product(a, b):
    return jnp.dot(a, b, preferred_element_type=jnp.float32)


def split(values):
    high = values.astype(jnp.bfloat16)
    return high, (values - high.astype(jnp.float32)).astype(jnp.bfloat16)


def pack_kernel(core, weights, tile, mine, theirs):
    rows = weights.shape[0] // 4
    blocks = mine.shape[3] // rows

    def store(kept, sent):
        for b in range(blocks):
            depth = weights.shape[1]
            mixed = product(weights[...], tile[0, b * depth : (b + 1) * depth])
            for f in range(4):
                scale = code_scale if f < 2 else code_scale / 60.0
                part = jnp.round(mixed[f * rows : (f + 1) * rows] * scale)
                target = kept if f < 2 else sent
                code = part.astype(jnp.int32).astype(jnp.int16)
                target[f % 2, 0, 0, b * rows : (b + 1) * rows] = code

    @pl.when(core[0] == 0)
    def _():
        store(mine, theirs)

    @pl.when(core[0] != 0)
    def _():
        store(theirs, mine)


def pack(tile, planes, core, which):
    comps, deep, width = tile.shape
    quarter = deep // planes // 4
    x_rows = min(quarter, 32)
    ghost = [[t for t in first_at(z) if t[0] not in (3, 4)] for z in (3, 4)]
    weights = depth_matrix(x_rows, planes, [[(3, 1.0)], [(4, 1.0)]] + ghost)
    first, second = streams[which]
    shape = jax.ShapeDtypeStruct((2, 2, comps, quarter, width), jnp.int16)
    spec = pl.BlockSpec((2, 1, 1, quarter, width), lambda k, c: (0, k, c, 0, 0))
    return pl.pallas_call(
        pack_kernel,
        out_shape=(shape,) * 2,
        grid=(2, comps),
        in_specs=[
            pl.BlockSpec(memory_space=pltpu.SMEM),
            pl.BlockSpec(weights.shape, lambda k, c: (0, 0)),
            pl.BlockSpec(
                (1, quarter * planes, width), lambda k, c: (c, first + k * (second - first), 0)
            ),
        ],
        out_specs=(spec,) * 2,
        compiler_params=grant(16),
        cost_estimate=pl.CostEstimate(
            flops=0, bytes_accessed=2 * comps * deep * width, transcendentals=0
        ),
    )(core, jnp.asarray(weights), tile)


def field_kernel(comps, viscosity, turn, m_all, m_top, before, after, field, out, token, *scratch):
    terms = scratch[:5]
    columns, high_s, low_s, high_x, low_x, arrived, left = scratch[5:]
    inner, depth, along, across, sums = terms

    def send(i, n, p):
        return pltpu.make_async_copy(terms[n].at[0, p], out.at[i, n, p], left.at[n, p])

    slab, width = inner.shape[2:]
    planes = field.shape[1] // slab
    tiles = width // lanes
    gain = viscosity[0] * section_step

    def fetch(c, t):
        source = field.at[c, :, pl.ds(t * lanes, lanes)]
        return pltpu.make_async_copy(source, columns.at[t], arrived.at[t])

    for t in range(tiles):
        fetch(comps[0], t).start()
    for i, c in enumerate(comps):
        for t in range(tiles):
            fetch(c, t).wait()

            def unpack(r, carry):
                start = pl.multiple_of(r * 8, 8)
                plane = [columns[t, pl.ds(start * planes + z, 8, planes), :] for z in range(planes)]
                at = (pl.ds(start, 8), pl.ds(t * lanes, lanes))
                for p in range(2):
                    z = 3 + p
                    centre = plane[z]
                    u1, u2, u3 = plane[z + 1], plane[z + 2], plane[z + 3]
                    d1, d2, d3 = plane[z - 1], plane[z - 2], plane[z - 3]
                    slope = 0.75 * (u1 - d1) - 0.15 * (u2 - d2) + (1.0 / 60.0) * (u3 - d3)
                    curve = 1.5 * (u1 + d1) - 0.15 * (u2 + d2) + (1.0 / 90.0) * (u3 + d3)
                    inner[(0, p) + at] = centre
                    depth[(0, p) + at] = slope
                    sums[(0, p) + at] = centre + gain * (curve - (49.0 / 18.0) * centre)
                return carry

            lax.fori_loop(0, slab // 8, unpack, 0, unroll=4)
            if i + 1 < len(comps):
                fetch(comps[i + 1], t).start()

        for p in range(2):
            send(i, 0, p).start()
            send(i, 1, p).start()
        rows = m_top.shape[0] // 2
        for p in range(2):
            for start, rim in ((0, before), (reach + slab, after)):
                high, low = split(rim[c, :, p])
                high_x[start : start + reach, :] = high
                low_x[start : start + reach, :] = low

            def fill(r, carry):
                start = pl.multiple_of(r * 16, 16)
                at = pl.ds(start, 16)
                to = pl.ds(pl.multiple_of(start + reach, 16), 16)
                high, low = split(inner[0, p, at, :])
                high_x[to, :] = high
                low_x[to, :] = low
                high_s[at, :] = half_turned(high)
                low_s[at, :] = half_turned(low)
                return carry

            lax.fori_loop(0, slab // 16, fill, 0, unroll=8)
            for b in range(slab // rows):
                window = pl.ds(b * rows, rows + 2 * reach)
                at = pl.ds(b * rows, rows)
                one = product(m_all[...], high_x[window, :])
                two = product(m_top[...], low_x[window, :])
                along[0, p, at, :] = one[:rows] + one[2 * rows :] + two[:rows]
                curve = (gain / 180.0) * (one[rows : 2 * rows] + two[rows:])
                sums[0, p, at, :] = sums[0, p, at, :] + curve
            send(i, 2, p).start()
            for t in range(tiles):
                side = pl.ds(t * lanes, lanes)
                window = pl.ds(t * lanes, 2 * lanes)
                both = product(high_s[:, window], turn[...]) + product(low_s[:, window], turn[...])
                across[0, p, :, side] = both[:, :lanes] * (1.0 / 60.0)
                curve = both[:, lanes:] * (gain / 180.0)
                sums[0, p, :, side] = sums[0, p, :, side] + curve
            send(i, 3, p).start()
            send(i, 4, p).start()
        for n in range(5):
            for p in range(2):
                send(i, n, p).wait()
    token[0] = 0


def field_terms(comps, room, field, before, after, viscosity, length):
    _, slab, planes, width = field.shape
    flat = field.reshape(-1, slab * planes, width)
    rows = min(slab, 128)
    high, low, second = along_matrices(rows, length)
    top = np.concatenate([high, second], 0)
    everything = np.concatenate([high, second, low], 0)
    turn = across_matrix([first_at(0), [t for t in second_at(0) if t[0] != 0]])
    shape = jax.ShapeDtypeStruct((len(comps), 5, 2, slab, width), jnp.float32)
    spec = pl.BlockSpec(memory_space=pltpu.HBM)
    near = pl.BlockSpec(memory_space=pltpu.VMEM)
    return pl.pallas_call(
        functools.partial(field_kernel, comps),
        out_shape=(shape, jax.ShapeDtypeStruct((1,), jnp.int32)),
        in_specs=[pl.BlockSpec(memory_space=pltpu.SMEM)]
        + [near] * 5
        + [pl.BlockSpec(memory_space=pl.ANY)],
        out_specs=(spec, pl.BlockSpec(memory_space=pltpu.SMEM)),
        compiler_params=grant(room),
        scratch_shapes=[pltpu.VMEM((1, 2, slab, width), jnp.float32)] * 5
        + [
            pltpu.VMEM((width // lanes, slab * planes, lanes), jnp.float32),
            pltpu.VMEM((slab, width + lanes), jnp.bfloat16),
            pltpu.VMEM((slab, width + lanes), jnp.bfloat16),
            pltpu.VMEM((slab + 2 * reach, width), jnp.bfloat16),
            pltpu.VMEM((slab + 2 * reach, width), jnp.bfloat16),
            pltpu.SemaphoreType.DMA((width // lanes,)),
            pltpu.SemaphoreType.DMA((5, 2)),
        ],
        cost_estimate=pl.CostEstimate(
            flops=0, bytes_accessed=4 * len(comps) * slab * planes * width * 2, transcendentals=0
        ),
    )(
        viscosity, jnp.asarray(turn), jnp.asarray(everything), jnp.asarray(top), before, after, flat
    )


def final_kernel(
    groups, core, m_both, turn, held0, other0, held1, other1, before, after, before2, after2, *refs
):
    terms, scratch = refs[: len(groups)], refs[len(groups) :]
    kept = {c: (g, i) for g, comps in enumerate(groups) for i, c in enumerate(comps)}
    inner, depth, along, across, sums = [
        [terms[kept[c][0]].at[kept[c][1], n] for c in range(3)] for n in range(5)
    ]
    out, base_s, turned_s, flow_s, ghost_s, slope_s, side_s, arrived = scratch
    step = pl.program_id(0)
    rows = slope_s.shape[2]
    quarter = held0.shape[3]
    slab = 4 * quarter
    inverse = 1.0 / code_scale

    def decoded(values):
        return values.astype(jnp.int32).astype(jnp.float32) * inverse

    def load(flow, ghost, before, after):
        for c in range(3):
            for p in range(2):
                base_s[c, p, 0:reach] = decoded(before[p, c]).astype(jnp.bfloat16)
                base_s[c, p, reach + slab :] = decoded(after[p, c]).astype(jnp.bfloat16)
        copies = []
        for u in range(2):
            for k in range(2):
                at = pl.ds(streams[u][k] * quarter, quarter)
                for n, (source, target) in enumerate(((flow, flow_s), (ghost, ghost_s))):
                    copies.append(
                        pltpu.make_async_copy(
                            source[u].at[k], target.at[:, :, at], arrived.at[4 * n + 2 * u + k]
                        )
                    )
        for copy in copies:
            copy.start()
        for copy in copies:
            copy.wait()

    @pl.when(step == 0)
    def _():
        @pl.when(core[0] == 0)
        def _():
            load((held0, held1), (other0, other1), before, after)

        @pl.when(core[0] != 0)
        def _():
            load((other0, other1), (held0, held1), before2, after2)

        def fill(i, carry):
            start = pl.multiple_of(i * 16, 16)
            to = pl.ds(pl.multiple_of(start + reach, 16), 16)
            for c in range(3):
                for p in range(2):
                    values = decoded(flow_s[p, c, pl.ds(start, 16), :])
                    base_s[c, p, to, :] = values.astype(jnp.bfloat16)
            return carry

        lax.fori_loop(0, slab // 16, fill, 0)

    origin = pl.multiple_of(step * rows, 32)
    def derive(c, carry):
        for p in range(2):
            both = product(m_both[...], base_s[c, p, pl.ds(origin, rows + 2 * reach), :])
            slope_s[c, p] = both[:rows] + both[rows:]
            for r in range(0, rows, 16):
                here = pl.ds(pl.multiple_of(origin + reach + r, 16), 16)
                turned_s[r : r + 16, :] = half_turned(base_s[c, p, here, :])
            for t in range(side_s.shape[3] // lanes):
                window = turned_s[:, pl.ds(t * lanes, 2 * lanes)]
                side_s[c, p, :, pl.ds(t * lanes, lanes)] = product(window, turn[...])
        return carry

    lax.fori_loop(0, 3, derive, 0)

    def body(i, carry):
        start = pl.multiple_of(i * 16, 16)
        at = pl.ds(start, 16)
        there = pl.ds(pl.multiple_of(origin + start, 16), 16)
        inside = pl.ds(pl.multiple_of(origin + reach + start, 16), 16)
        flow = [
            [base_s[c, p, inside, :].astype(jnp.float32) for p in range(2)] for c in range(3)
        ]
        for p in range(2):
            move = [inner[c][p, at, :] for c in range(3)]
            for c in range(3):
                dz = decoded(ghost_s[p, c, there, :])
                if p == 0:
                    dz = dz + 0.75 * flow[c][1]
                else:
                    dz = dz - 0.75 * flow[c][0]
                dy = side_s[c, p, at, :] * (1.0 / 60.0)
                total = flow[0][p] * along[c][p, at, :] + flow[1][p] * across[c][p, at, :]
                total = total + flow[2][p] * depth[c][p, at, :]
                total = total + move[0] * slope_s[c, p, at, :] + move[1] * dy + move[2] * dz
                out[0, c, at, p, :] = sums[c][p, at, :] - section_step * total
        return carry

    lax.fori_loop(0, rows // 16, body, 0)


def final(core, pieces, rims, terms, length):
    _, _, pair, slab, width = terms[0].shape
    comps = sum(t.shape[0] for t in terms)
    groups = tuple(comps_of for comps_of, _ in shares.values())
    rows = min(slab, 32)
    turn = across_matrix([first_at(0)])
    high, low, _ = along_matrices(rows, length)
    both = np.concatenate([high, low], 0)
    whole = pl.BlockSpec(memory_space=pl.ANY)
    rim = pl.BlockSpec(rims[0].shape, lambda i: (0, 0, 0, 0))
    specs = [
        pl.BlockSpec((t.shape[0], 5, pair, rows, width), lambda i: (0, 0, 0, i, 0)) for t in terms
    ]
    return pl.pallas_call(
        functools.partial(final_kernel, groups),
        out_shape=jax.ShapeDtypeStruct((1, comps, slab, pair, width), jnp.float32),
        grid=(slab // rows,),
        in_specs=[
            pl.BlockSpec(memory_space=pltpu.SMEM),
            pl.BlockSpec(both.shape, lambda i: (0, 0)),
            pl.BlockSpec(turn.shape, lambda i: (0, 0)),
        ]
        + [whole] * 4
        + [rim] * 4
        + specs,
        out_specs=pl.BlockSpec((1, comps, rows, pair, width), lambda i: (0, 0, i, 0, 0)),
        compiler_params=grant(58),
        scratch_shapes=[
            pltpu.VMEM((comps, pair, slab + 2 * reach, width), jnp.bfloat16),
            pltpu.VMEM((rows, width + lanes), jnp.bfloat16),
            pltpu.VMEM((pair, comps, slab, width), jnp.int16),
            pltpu.VMEM((pair, comps, slab, width), jnp.int16),
            pltpu.VMEM((comps, pair, rows, width), jnp.float32),
            pltpu.VMEM((comps, pair, rows, width), jnp.float32),
            pltpu.SemaphoreType.DMA((8,)),
        ],
        cost_estimate=pl.CostEstimate(
            flops=0, bytes_accessed=8 * comps * pair * slab * width, transcendentals=0
        ),
    )(core, jnp.asarray(both), jnp.asarray(turn), *pieces, *rims, *terms)


def ring(last, first):
    size = lax.axis_size("gx")
    up = [(i, (i + 1) % size) for i in range(size)]
    down = [(j, i) for i, j in up]
    return lax.ppermute(last, "gx", up), lax.ppermute(first, "gx", down)


def swap(array, bit):
    return lax.ppermute(array, "pert", [(i, i ^ bit) for i in range(lax.axis_size("pert"))])


def exchange(mine, theirs, root, gate, work):
    me = lax.axis_index("pert")
    is_root = me == root
    place = (me // 2) ^ (root // 2)
    at_a, at_b, at_c = place == 0, place == 1, place == 2
    handed = [swap(t, 1) for t in theirs]

    def owned(u, h, k):
        return jnp.where(is_root, mine[u][h, k], handed[u][h, k])

    opening = [owned(u, h, 0) for u in range(2) for h in range(2)]
    opening = gate(*opening)
    source = [
        [[opening[2 * u + h]] + [owned(u, h, k) for k in range(1, phases)] for h in range(2)]
        for u in range(2)
    ]
    X = [[], []]
    Y = [[], []]
    for s in range(phases + 1):
        for u in range(2):
            k = min(s, phases - 1)
            one, two = source[u][0][k], source[u][1][k]
            if s == phases:
                one, two = two, one
            if s > 0:
                one = jnp.where(at_a, one, Y[u][s - 1])
                two = jnp.where(at_a, two, X[u][s - 1])
                one, two, place = gate(one, two, place)
                at_a, at_b, at_c = place == 0, place == 1, place == 2
            X[u].append(swap(one, 2))
            Y[u].append(swap(two, 4))
            if (s, u) in shares:
                place = place + work(shares[s, u])
                at_a, at_b, at_c = place == 0, place == 1, place == 2
    held = []
    for u in range(2):
        parts = []
        for k in range(phases):
            row = []
            for h in range(2):
                P1, P2 = (X[u], Y[u]) if h == 0 else (Y[u], X[u])
                near, far = (at_b, at_c) if h == 0 else (at_c, at_b)
                late = P1[k + 2] if k + 2 <= phases else P2[phases]
                value = jnp.where(near, P1[k], jnp.where(far, late, P2[k + 1]))
                row.append(jnp.where(at_a, source[u][h][k], value))
            parts.append(jnp.stack(row, 0))
        held.append(jnp.stack(parts, 0))
        if u == 0:
            quarter = held[0].shape[3]
            size = lax.axis_size("gx")
            pairs = [
                (c * size + i, c * size + (i + 1) % size)
                for c in range(0, lax.axis_size("pert"), 2)
                for i in range(size)
            ]
            both = ("pert", "gx")
            before = lax.ppermute(held[0][1][:, :, quarter - reach :], both, pairs)
            after = lax.ppermute(held[0][0][:, :, :reach], both, [(j, i) for i, j in pairs])
            before, after, place = lax.optimization_barrier((before, after, place))
            second = [swap(before, 1), swap(after, 1)]
            at_a, at_b, at_c = place == 0, place == 1, place == 2
    other = [swap(h, 1) for h in held]
    return (held[0], other[0], held[1], other[1]), (before, after, *second)


def per_device(pert_field, base_store, section_owner, pert_ids, member_visc):
    _, comps, slab, planes, width = pert_field.shape
    length = slab * lax.axis_size("gx")
    member_pick = pert_ids[0] == jnp.arange(member_visc.shape[0], dtype=jnp.int32)
    viscosity = jnp.sum(jnp.where(member_pick, member_visc, 0.0))[None]
    levels_here = base_store.shape[0]
    owner_slot = section_owner[0] % levels_here
    owner_root = section_owner[0] // levels_here
    tiles = base_store.reshape(levels_here, comps, slab * planes, width)
    tile = tiles[0] if levels_here == 1 else lax.dynamic_index_in_dim(tiles, owner_slot, 0, False)
    me = lax.axis_index("pert")
    in_pairs = lax.axis_size("pert") == 8
    core = (me % 2 if in_pairs else jnp.zeros_like(me)).astype(jnp.int32)[None]
    field = pert_field[0]
    last, first, tile = lax.optimization_barrier(
        (field[:, slab - reach :, 3:5], field[:, :reach, 3:5], tile)
    )
    before, after = ring(last, first)
    halves = [pack(tile, planes, core, u) for u in range(2)]
    done = {"field": field, "terms": []}

    def gate(*values):
        done["field"], *values = lax.optimization_barrier((done["field"], *values))
        return values

    def work(share):
        terms, token = field_terms(*share, done["field"], before, after, viscosity, length)
        done["terms"].append(terms)
        return token[0]

    if in_pairs:
        mine, theirs = [h[0] for h in halves], [h[1] for h in halves]
        pieces, rims = exchange(mine, theirs, owner_root, gate, work)
    else:
        for share in shares.values():
            work(share)
        pieces = [
            lax.psum(jnp.where(me == owner_root, a, 0).astype(jnp.float32), "pert").astype(a.dtype)
            for h in halves
            for a in h
        ]
        pieces = [a.transpose(1, 0, 2, 3, 4) for a in pieces]
        quarter = slab // 4
        rims = ring(pieces[0][1][:, :, quarter - reach :], pieces[0][0][:, :, :reach]) * 2
    return final(core, pieces, rims, done["terms"], length)


def solution(mesh):
    placed = (
        P("pert", None, "gx", None, None),
        P("pert", None, "gx", None, None),
        P(),
        P("pert"),
        P(),
    )
    return jax.shard_map(
        per_device,
        mesh=mesh,
        in_specs=placed,
        out_specs=P("pert", None, "gx", None, None),
        check_vma=False,
    )
```

```python
import functools

import jax
import jax.numpy as jnp
import numpy as np
from jax import lax
from jax.experimental import pallas as pl
from jax.experimental.pallas import tpu as pltpu
from jax.sharding import PartitionSpec as P

section_step = 0.25
reach = 16
lanes = 128
code_scale = 4096.0
phases = 2
streams = ((0, 3), (1, 2))
shares = {(0, 1): ((0,), 57), (1, 1): ((1, 2), 57)}


def grant(mib):
    return pltpu.CompilerParams(vmem_limit_bytes=mib << 20)


def compact_kernel(length):
    wave = 2.0 * np.pi * np.arange(length) / length
    symbol = 14.0 / 9.0 * np.sin(wave) + 1.0 / 18.0 * np.sin(2.0 * wave)
    symbol = 1j * symbol / (1.0 + 2.0 / 3.0 * np.cos(wave))
    return np.real(np.fft.ifft(symbol))


def along_matrices(rows, length):
    kernel = compact_kernel(length)
    first = np.zeros((rows, rows + 2 * reach))
    second = np.zeros((rows, rows + 2 * reach))
    for i in range(rows):
        for k in range(-reach, reach + 1):
            first[i, i + reach + k] = kernel[-k % length]
        for k, weight in ((0, -980.0), (1, 270.0), (2, -27.0), (3, 2.0)):
            second[i, i + reach + k] = weight
            second[i, i + reach - k] = weight
    high = first.astype(jnp.bfloat16)
    low = (first - high.astype(np.float64)).astype(jnp.bfloat16)
    return high, low, second.astype(jnp.bfloat16)


first_taps = ((1, 45.0), (2, -9.0), (3, 1.0))
second_taps = ((0, -490.0), (1, 270.0), (2, -27.0), (3, 2.0))


def depth_matrix(rows, planes, fields):
    matrix = np.zeros((len(fields) * rows, rows * planes))
    for f, taps in enumerate(fields):
        for i in range(rows):
            for z, weight in taps:
                matrix[f * rows + i, i * planes + z] += weight
    return matrix.astype(jnp.bfloat16)


def first_at(z):
    return [(z + k, w) for k, w in first_taps] + [(z - k, -w) for k, w in first_taps]


def second_at(z):
    taps = [(z + k, w) for k, w in second_taps]
    return taps + [(z - k, w) for k, w in second_taps if k > 0]


def across_matrix(orders):
    matrix = np.zeros((2 * lanes, lanes * len(orders)))
    for o, taps in enumerate(orders):
        for i in range(lanes):
            for k, weight in taps:
                matrix[lanes // 2 + i + k, o * lanes + i] += weight
    return matrix.astype(jnp.bfloat16)


def half_turned(values):
    half = lanes // 2
    return jnp.concatenate([values[:, -half:], values, values[:, :half]], 1)


def product(a, b):
    return jnp.dot(a, b, preferred_element_type=jnp.float32)


def split(values):
    high = values.astype(jnp.bfloat16)
    return high, (values - high.astype(jnp.float32)).astype(jnp.bfloat16)


def pack_kernel(core, weights, tile, mine, theirs):
    rows = weights.shape[0] // 4
    blocks = mine.shape[3] // rows

    def store(kept, sent):
        for b in range(blocks):
            depth = weights.shape[1]
            mixed = product(weights[...], tile[0, b * depth : (b + 1) * depth])
            for f in range(4):
                scale = code_scale if f < 2 else code_scale / 60.0
                part = jnp.round(mixed[f * rows : (f + 1) * rows] * scale)
                target = kept if f < 2 else sent
                code = part.astype(jnp.int32).astype(jnp.int16)
                target[f % 2, 0, 0, b * rows : (b + 1) * rows] = code

    @pl.when(core[0] == 0)
    def _():
        store(mine, theirs)

    @pl.when(core[0] != 0)
    def _():
        store(theirs, mine)


def pack(tile, planes, core, which):
    comps, deep, width = tile.shape
    quarter = deep // planes // 4
    x_rows = min(quarter, 32)
    ghost = [[t for t in first_at(z) if t[0] not in (3, 4)] for z in (3, 4)]
    weights = depth_matrix(x_rows, planes, [[(3, 1.0)], [(4, 1.0)]] + ghost)
    first, second = streams[which]
    shape = jax.ShapeDtypeStruct((2, 2, comps, quarter, width), jnp.int16)
    spec = pl.BlockSpec((2, 1, 1, quarter, width), lambda k, c: (0, k, c, 0, 0))
    return pl.pallas_call(
        pack_kernel,
        out_shape=(shape,) * 2,
        grid=(2, comps),
        in_specs=[
            pl.BlockSpec(memory_space=pltpu.SMEM),
            pl.BlockSpec(weights.shape, lambda k, c: (0, 0)),
            pl.BlockSpec(
                (1, quarter * planes, width), lambda k, c: (c, first + k * (second - first), 0)
            ),
        ],
        out_specs=(spec,) * 2,
        compiler_params=grant(16),
        cost_estimate=pl.CostEstimate(
            flops=0, bytes_accessed=2 * comps * deep * width, transcendentals=0
        ),
    )(core, jnp.asarray(weights), tile)


def field_kernel(comps, viscosity, turn, m_all, m_top, before, after, field, out, token, *scratch):
    terms = scratch[:5]
    columns, high_s, low_s, high_x, low_x, arrived, left = scratch[5:]
    inner, depth, along, across, sums = terms

    def send(i, n, p):
        return pltpu.make_async_copy(terms[n].at[0, p], out.at[i, n, p], left.at[n, p])

    slab, width = inner.shape[2:]
    planes = field.shape[1] // slab
    tiles = width // lanes
    gain = viscosity[0] * section_step

    def fetch(c, t):
        source = field.at[c, :, pl.ds(t * lanes, lanes)]
        return pltpu.make_async_copy(source, columns.at[t], arrived.at[t])

    for t in range(tiles):
        fetch(comps[0], t).start()
    for i, c in enumerate(comps):
        for t in range(tiles):
            fetch(c, t).wait()

            def unpack(r, carry):
                start = pl.multiple_of(r * 8, 8)
                plane = [columns[t, pl.ds(start * planes + z, 8, planes), :] for z in range(planes)]
                at = (pl.ds(start, 8), pl.ds(t * lanes, lanes))
                for p in range(2):
                    z = 3 + p
                    centre = plane[z]
                    u1, u2, u3 = plane[z + 1], plane[z + 2], plane[z + 3]
                    d1, d2, d3 = plane[z - 1], plane[z - 2], plane[z - 3]
                    slope = 0.75 * (u1 - d1) - 0.15 * (u2 - d2) + (1.0 / 60.0) * (u3 - d3)
                    curve = 1.5 * (u1 + d1) - 0.15 * (u2 + d2) + (1.0 / 90.0) * (u3 + d3)
                    inner[(0, p) + at] = centre
                    depth[(0, p) + at] = slope
                    sums[(0, p) + at] = centre + gain * (curve - (49.0 / 18.0) * centre)
                return carry

            lax.fori_loop(0, slab // 8, unpack, 0, unroll=4)
            if i + 1 < len(comps):
                fetch(comps[i + 1], t).start()

        for p in range(2):
            send(i, 0, p).start()
            send(i, 1, p).start()
        rows = m_top.shape[0] // 2
        for p in range(2):
            for start, rim in ((0, before), (reach + slab, after)):
                high, low = split(rim[c, :, p])
                high_x[start : start + reach, :] = high
                low_x[start : start + reach, :] = low

            def fill(r, carry):
                start = pl.multiple_of(r * 16, 16)
                at = pl.ds(start, 16)
                to = pl.ds(pl.multiple_of(start + reach, 16), 16)
                high, low = split(inner[0, p, at, :])
                high_x[to, :] = high
                low_x[to, :] = low
                high_s[at, :] = half_turned(high)
                low_s[at, :] = half_turned(low)
                return carry

            lax.fori_loop(0, slab // 16, fill, 0, unroll=8)
            for b in range(slab // rows):
                window = pl.ds(b * rows, rows + 2 * reach)
                at = pl.ds(b * rows, rows)
                one = product(m_all[...], high_x[window, :])
                two = product(m_top[...], low_x[window, :])
                along[0, p, at, :] = one[:rows] + one[2 * rows :] + two[:rows]
                curve = (gain / 180.0) * (one[rows : 2 * rows] + two[rows:])
                sums[0, p, at, :] = sums[0, p, at, :] + curve
            send(i, 2, p).start()
            for t in range(tiles):
                side = pl.ds(t * lanes, lanes)
                window = pl.ds(t * lanes, 2 * lanes)
                both = product(high_s[:, window], turn[...]) + product(low_s[:, window], turn[...])
                across[0, p, :, side] = both[:, :lanes] * (1.0 / 60.0)
                curve = both[:, lanes:] * (gain / 180.0)
                sums[0, p, :, side] = sums[0, p, :, side] + curve
            send(i, 3, p).start()
            send(i, 4, p).start()
        for n in range(5):
            for p in range(2):
                send(i, n, p).wait()
    token[0] = 0


def field_terms(comps, room, field, before, after, viscosity, length):
    _, slab, planes, width = field.shape
    flat = field.reshape(-1, slab * planes, width)
    rows = min(slab, 128)
    high, low, second = along_matrices(rows, length)
    top = np.concatenate([high, second], 0)
    everything = np.concatenate([high, second, low], 0)
    turn = across_matrix([first_at(0), [t for t in second_at(0) if t[0] != 0]])
    shape = jax.ShapeDtypeStruct((len(comps), 5, 2, slab, width), jnp.float32)
    spec = pl.BlockSpec(memory_space=pltpu.HBM)
    near = pl.BlockSpec(memory_space=pltpu.VMEM)
    return pl.pallas_call(
        functools.partial(field_kernel, comps),
        out_shape=(shape, jax.ShapeDtypeStruct((1,), jnp.int32)),
        in_specs=[pl.BlockSpec(memory_space=pltpu.SMEM)]
        + [near] * 5
        + [pl.BlockSpec(memory_space=pl.ANY)],
        out_specs=(spec, pl.BlockSpec(memory_space=pltpu.SMEM)),
        compiler_params=grant(room),
        scratch_shapes=[pltpu.VMEM((1, 2, slab, width), jnp.float32)] * 5
        + [
            pltpu.VMEM((width // lanes, slab * planes, lanes), jnp.float32),
            pltpu.VMEM((slab, width + lanes), jnp.bfloat16),
            pltpu.VMEM((slab, width + lanes), jnp.bfloat16),
            pltpu.VMEM((slab + 2 * reach, width), jnp.bfloat16),
            pltpu.VMEM((slab + 2 * reach, width), jnp.bfloat16),
            pltpu.SemaphoreType.DMA((width // lanes,)),
            pltpu.SemaphoreType.DMA((5, 2)),
        ],
        cost_estimate=pl.CostEstimate(
            flops=0, bytes_accessed=4 * len(comps) * slab * planes * width * 2, transcendentals=0
        ),
    )(
        viscosity, jnp.asarray(turn), jnp.asarray(everything), jnp.asarray(top), before, after, flat
    )


def final_kernel(
    groups, core, m_both, turn, held0, other0, held1, other1, before, after, before2, after2, *refs
):
    terms, scratch = refs[: len(groups)], refs[len(groups) :]
    kept = {c: (g, i) for g, comps in enumerate(groups) for i, c in enumerate(comps)}
    inner, depth, along, across, sums = [
        [terms[kept[c][0]].at[kept[c][1], n] for c in range(3)] for n in range(5)
    ]
    out, base_s, turned_s, flow_s, ghost_s, slope_s, side_s, arrived = scratch
    step = pl.program_id(0)
    rows = slope_s.shape[2]
    quarter = held0.shape[3]
    slab = 4 * quarter
    inverse = 1.0 / code_scale

    def decoded(values):
        return values.astype(jnp.int32).astype(jnp.float32) * inverse

    def load(flow, ghost, before, after):
        for c in range(3):
            for p in range(2):
                base_s[c, p, 0:reach] = decoded(before[p, c]).astype(jnp.bfloat16)
                base_s[c, p, reach + slab :] = decoded(after[p, c]).astype(jnp.bfloat16)
        copies = []
        for u in range(2):
            for k in range(2):
                at = pl.ds(streams[u][k] * quarter, quarter)
                for n, (source, target) in enumerate(((flow, flow_s), (ghost, ghost_s))):
                    copies.append(
                        pltpu.make_async_copy(
                            source[u].at[k], target.at[:, :, at], arrived.at[4 * n + 2 * u + k]
                        )
                    )
        for copy in copies:
            copy.start()
        for copy in copies:
            copy.wait()

    @pl.when(step == 0)
    def _():
        @pl.when(core[0] == 0)
        def _():
            load((held0, held1), (other0, other1), before, after)

        @pl.when(core[0] != 0)
        def _():
            load((other0, other1), (held0, held1), before2, after2)

        def fill(i, carry):
            start = pl.multiple_of(i * 16, 16)
            to = pl.ds(pl.multiple_of(start + reach, 16), 16)
            for c in range(3):
                for p in range(2):
                    values = decoded(flow_s[p, c, pl.ds(start, 16), :])
                    base_s[c, p, to, :] = values.astype(jnp.bfloat16)
            return carry

        lax.fori_loop(0, slab // 16, fill, 0)

    origin = pl.multiple_of(step * rows, 32)
    def derive(c, carry):
        for p in range(2):
            both = product(m_both[...], base_s[c, p, pl.ds(origin, rows + 2 * reach), :])
            slope_s[c, p] = both[:rows] + both[rows:]
            for r in range(0, rows, 16):
                here = pl.ds(pl.multiple_of(origin + reach + r, 16), 16)
                turned_s[r : r + 16, :] = half_turned(base_s[c, p, here, :])
            for t in range(side_s.shape[3] // lanes):
                window = turned_s[:, pl.ds(t * lanes, 2 * lanes)]
                side_s[c, p, :, pl.ds(t * lanes, lanes)] = product(window, turn[...])
        return carry

    lax.fori_loop(0, 3, derive, 0)

    def body(i, carry):
        start = pl.multiple_of(i * 16, 16)
        at = pl.ds(start, 16)
        there = pl.ds(pl.multiple_of(origin + start, 16), 16)
        inside = pl.ds(pl.multiple_of(origin + reach + start, 16), 16)
        flow = [
            [base_s[c, p, inside, :].astype(jnp.float32) for p in range(2)] for c in range(3)
        ]
        for p in range(2):
            move = [inner[c][p, at, :] for c in range(3)]
            for c in range(3):
                dz = decoded(ghost_s[p, c, there, :])
                if p == 0:
                    dz = dz + 0.75 * flow[c][1]
                else:
                    dz = dz - 0.75 * flow[c][0]
                dy = side_s[c, p, at, :] * (1.0 / 60.0)
                total = flow[0][p] * along[c][p, at, :] + flow[1][p] * across[c][p, at, :]
                total = total + flow[2][p] * depth[c][p, at, :]
                total = total + move[0] * slope_s[c, p, at, :] + move[1] * dy + move[2] * dz
                out[0, c, at, p, :] = sums[c][p, at, :] - section_step * total
        return carry

    lax.fori_loop(0, rows // 16, body, 0)


def final(core, pieces, rims, terms, length):
    _, _, pair, slab, width = terms[0].shape
    comps = sum(t.shape[0] for t in terms)
    groups = tuple(comps_of for comps_of, _ in shares.values())
    rows = min(slab, 64)
    turn = across_matrix([first_at(0)])
    high, low, _ = along_matrices(rows, length)
    both = np.concatenate([high, low], 0)
    whole = pl.BlockSpec(memory_space=pl.ANY)
    rim = pl.BlockSpec(rims[0].shape, lambda i: (0, 0, 0, 0))
    specs = [
        pl.BlockSpec((t.shape[0], 5, pair, rows, width), lambda i: (0, 0, 0, i, 0)) for t in terms
    ]
    return pl.pallas_call(
        functools.partial(final_kernel, groups),
        out_shape=jax.ShapeDtypeStruct((1, comps, slab, pair, width), jnp.float32),
        grid=(slab // rows,),
        in_specs=[
            pl.BlockSpec(memory_space=pltpu.SMEM),
            pl.BlockSpec(both.shape, lambda i: (0, 0)),
            pl.BlockSpec(turn.shape, lambda i: (0, 0)),
        ]
        + [whole] * 4
        + [rim] * 4
        + specs,
        out_specs=pl.BlockSpec((1, comps, rows, pair, width), lambda i: (0, 0, i, 0, 0)),
        compiler_params=grant(58),
        scratch_shapes=[
            pltpu.VMEM((comps, pair, slab + 2 * reach, width), jnp.bfloat16),
            pltpu.VMEM((rows, width + lanes), jnp.bfloat16),
            pltpu.VMEM((pair, comps, slab, width), jnp.int16),
            pltpu.VMEM((pair, comps, slab, width), jnp.int16),
            pltpu.VMEM((comps, pair, rows, width), jnp.float32),
            pltpu.VMEM((comps, pair, rows, width), jnp.float32),
            pltpu.SemaphoreType.DMA((8,)),
        ],
        cost_estimate=pl.CostEstimate(
            flops=0, bytes_accessed=8 * comps * pair * slab * width, transcendentals=0
        ),
    )(core, jnp.asarray(both), jnp.asarray(turn), *pieces, *rims, *terms)


def ring(last, first):
    size = lax.axis_size("gx")
    up = [(i, (i + 1) % size) for i in range(size)]
    down = [(j, i) for i, j in up]
    return lax.ppermute(last, "gx", up), lax.ppermute(first, "gx", down)


def swap(array, bit):
    return lax.ppermute(array, "pert", [(i, i ^ bit) for i in range(lax.axis_size("pert"))])


def exchange(mine, theirs, root, gate, work):
    me = lax.axis_index("pert")
    is_root = me == root
    place = (me // 2) ^ (root // 2)
    at_a, at_b, at_c = place == 0, place == 1, place == 2
    handed = [swap(t, 1) for t in theirs]

    def owned(u, h, k):
        return jnp.where(is_root, mine[u][h, k], handed[u][h, k])

    opening = [owned(u, h, 0) for u in range(2) for h in range(2)]
    opening = gate(*opening)
    source = [
        [[opening[2 * u + h]] + [owned(u, h, k) for k in range(1, phases)] for h in range(2)]
        for u in range(2)
    ]
    X = [[], []]
    Y = [[], []]
    for s in range(phases + 1):
        for u in range(2):
            k = min(s, phases - 1)
            one, two = source[u][0][k], source[u][1][k]
            if s == phases:
                one, two = two, one
            if s > 0:
                one = jnp.where(at_a, one, Y[u][s - 1])
                two = jnp.where(at_a, two, X[u][s - 1])
                one, two, place = gate(one, two, place)
                at_a, at_b, at_c = place == 0, place == 1, place == 2
            X[u].append(swap(one, 2))
            Y[u].append(swap(two, 4))
            if (s, u) in shares:
                place = place + work(shares[s, u])
                at_a, at_b, at_c = place == 0, place == 1, place == 2
    held = []
    for u in range(2):
        parts = []
        for k in range(phases):
            row = []
            for h in range(2):
                P1, P2 = (X[u], Y[u]) if h == 0 else (Y[u], X[u])
                near, far = (at_b, at_c) if h == 0 else (at_c, at_b)
                late = P1[k + 2] if k + 2 <= phases else P2[phases]
                value = jnp.where(near, P1[k], jnp.where(far, late, P2[k + 1]))
                row.append(jnp.where(at_a, source[u][h][k], value))
            parts.append(jnp.stack(row, 0))
        held.append(jnp.stack(parts, 0))
        if u == 0:
            quarter = held[0].shape[3]
            size = lax.axis_size("gx")
            pairs = [
                (c * size + i, c * size + (i + 1) % size)
                for c in range(0, lax.axis_size("pert"), 2)
                for i in range(size)
            ]
            both = ("pert", "gx")
            before = lax.ppermute(held[0][1][:, :, quarter - reach :], both, pairs)
            after = lax.ppermute(held[0][0][:, :, :reach], both, [(j, i) for i, j in pairs])
            before, after, place = lax.optimization_barrier((before, after, place))
            second = [swap(before, 1), swap(after, 1)]
            at_a, at_b, at_c = place == 0, place == 1, place == 2
    other = [swap(h, 1) for h in held]
    return (held[0], other[0], held[1], other[1]), (before, after, *second)


def per_device(pert_field, base_store, section_owner, pert_ids, member_visc):
    _, comps, slab, planes, width = pert_field.shape
    length = slab * lax.axis_size("gx")
    member_pick = pert_ids[0] == jnp.arange(member_visc.shape[0], dtype=jnp.int32)
    viscosity = jnp.sum(jnp.where(member_pick, member_visc, 0.0))[None]
    levels_here = base_store.shape[0]
    owner_slot = section_owner[0] % levels_here
    owner_root = section_owner[0] // levels_here
    tiles = base_store.reshape(levels_here, comps, slab * planes, width)
    tile = tiles[0] if levels_here == 1 else lax.dynamic_index_in_dim(tiles, owner_slot, 0, False)
    me = lax.axis_index("pert")
    in_pairs = lax.axis_size("pert") == 8
    core = (me % 2 if in_pairs else jnp.zeros_like(me)).astype(jnp.int32)[None]
    field = pert_field[0]
    last, first, tile = lax.optimization_barrier(
        (field[:, slab - reach :, 3:5], field[:, :reach, 3:5], tile)
    )
    before, after = ring(last, first)
    halves = [pack(tile, planes, core, u) for u in range(2)]
    done = {"field": field, "terms": []}

    def gate(*values):
        done["field"], *values = lax.optimization_barrier((done["field"], *values))
        return values

    def work(share):
        terms, token = field_terms(*share, done["field"], before, after, viscosity, length)
        done["terms"].append(terms)
        return token[0]

    if in_pairs:
        mine, theirs = [h[0] for h in halves], [h[1] for h in halves]
        pieces, rims = exchange(mine, theirs, owner_root, gate, work)
    else:
        for share in shares.values():
            work(share)
        pieces = [
            lax.psum(jnp.where(me == owner_root, a, 0).astype(jnp.float32), "pert").astype(a.dtype)
            for h in halves
            for a in h
        ]
        pieces = [a.transpose(1, 0, 2, 3, 4) for a in pieces]
        quarter = slab // 4
        rims = ring(pieces[0][1][:, :, quarter - reach :], pieces[0][0][:, :, :reach]) * 2
    return final(core, pieces, rims, done["terms"], length)


def solution(mesh):
    placed = (
        P("pert", None, "gx", None, None),
        P("pert", None, "gx", None, None),
        P(),
        P("pert"),
        P(),
    )
    return jax.shard_map(
        per_device,
        mesh=mesh,
        in_specs=placed,
        out_specs=P("pert", None, "gx", None, None),
        check_vma=False,
    )
```

```python
import functools

import jax
import jax.numpy as jnp
import numpy as np
from jax import lax
from jax.experimental import pallas as pl
from jax.experimental.pallas import tpu as pltpu
from jax.sharding import PartitionSpec as P

section_step = 0.25
reach = 16
lanes = 128
code_scale = 4096.0
phases = 2
streams = ((0, 3), (1, 2))
shares = {(0, 1): ((0,), 57), (1, 1): ((1, 2), 57)}


def grant(mib):
    return pltpu.CompilerParams(vmem_limit_bytes=mib << 20)


def compact_kernel(length):
    wave = 2.0 * np.pi * np.arange(length) / length
    symbol = 14.0 / 9.0 * np.sin(wave) + 1.0 / 18.0 * np.sin(2.0 * wave)
    symbol = 1j * symbol / (1.0 + 2.0 / 3.0 * np.cos(wave))
    return np.real(np.fft.ifft(symbol))


def along_matrices(rows, length):
    kernel = compact_kernel(length)
    first = np.zeros((rows, rows + 2 * reach))
    second = np.zeros((rows, rows + 2 * reach))
    for i in range(rows):
        for k in range(-reach, reach + 1):
            first[i, i + reach + k] = kernel[-k % length]
        for k, weight in ((0, -980.0), (1, 270.0), (2, -27.0), (3, 2.0)):
            second[i, i + reach + k] = weight
            second[i, i + reach - k] = weight
    high = first.astype(jnp.bfloat16)
    low = (first - high.astype(np.float64)).astype(jnp.bfloat16)
    return high, low, second.astype(jnp.bfloat16)


first_taps = ((1, 45.0), (2, -9.0), (3, 1.0))
second_taps = ((0, -490.0), (1, 270.0), (2, -27.0), (3, 2.0))


def depth_matrix(rows, planes, fields):
    matrix = np.zeros((len(fields) * rows, rows * planes))
    for f, taps in enumerate(fields):
        for i in range(rows):
            for z, weight in taps:
                matrix[f * rows + i, i * planes + z] += weight
    return matrix.astype(jnp.bfloat16)


def first_at(z):
    return [(z + k, w) for k, w in first_taps] + [(z - k, -w) for k, w in first_taps]


def second_at(z):
    taps = [(z + k, w) for k, w in second_taps]
    return taps + [(z - k, w) for k, w in second_taps if k > 0]


def across_matrix(orders):
    matrix = np.zeros((2 * lanes, lanes * len(orders)))
    for o, taps in enumerate(orders):
        for i in range(lanes):
            for k, weight in taps:
                matrix[lanes // 2 + i + k, o * lanes + i] += weight
    return matrix.astype(jnp.bfloat16)


def half_turned(values):
    half = lanes // 2
    return jnp.concatenate([values[:, -half:], values, values[:, :half]], 1)


def product(a, b):
    return jnp.dot(a, b, preferred_element_type=jnp.float32)


def split(values):
    high = values.astype(jnp.bfloat16)
    return high, (values - high.astype(jnp.float32)).astype(jnp.bfloat16)


def pack_kernel(core, weights, tile, mine, theirs):
    rows = weights.shape[0] // 4
    blocks = mine.shape[3] // rows

    def store(kept, sent):
        for b in range(blocks):
            depth = weights.shape[1]
            mixed = product(weights[...], tile[0, b * depth : (b + 1) * depth])
            for f in range(4):
                scale = code_scale if f < 2 else code_scale / 60.0
                part = jnp.round(mixed[f * rows : (f + 1) * rows] * scale)
                target = kept if f < 2 else sent
                code = part.astype(jnp.int32).astype(jnp.int16)
                target[f % 2, 0, 0, b * rows : (b + 1) * rows] = code

    @pl.when(core[0] == 0)
    def _():
        store(mine, theirs)

    @pl.when(core[0] != 0)
    def _():
        store(theirs, mine)


def pack(tile, planes, core, which):
    comps, deep, width = tile.shape
    quarter = deep // planes // 4
    x_rows = min(quarter, 32)
    ghost = [[t for t in first_at(z) if t[0] not in (3, 4)] for z in (3, 4)]
    weights = depth_matrix(x_rows, planes, [[(3, 1.0)], [(4, 1.0)]] + ghost)
    first, second = streams[which]
    shape = jax.ShapeDtypeStruct((2, 2, comps, quarter, width), jnp.int16)
    spec = pl.BlockSpec((2, 1, 1, quarter, width), lambda k, c: (0, k, c, 0, 0))
    return pl.pallas_call(
        pack_kernel,
        out_shape=(shape,) * 2,
        grid=(2, comps),
        in_specs=[
            pl.BlockSpec(memory_space=pltpu.SMEM),
            pl.BlockSpec(weights.shape, lambda k, c: (0, 0)),
            pl.BlockSpec(
                (1, quarter * planes, width), lambda k, c: (c, first + k * (second - first), 0)
            ),
        ],
        out_specs=(spec,) * 2,
        compiler_params=grant(16),
        cost_estimate=pl.CostEstimate(
            flops=0, bytes_accessed=2 * comps * deep * width, transcendentals=0
        ),
    )(core, jnp.asarray(weights), tile)


def field_kernel(comps, viscosity, turn, m_all, m_top, before, after, field, out, token, *scratch):
    terms = scratch[:5]
    columns, high_s, low_s, high_x, low_x, arrived, left = scratch[5:]
    inner, depth, along, across, sums = terms

    def send(i, n, p):
        return pltpu.make_async_copy(terms[n].at[0, p], out.at[i, n, p], left.at[n, p])

    slab, width = inner.shape[2:]
    planes = field.shape[1] // slab
    tiles = width // lanes
    gain = viscosity[0] * section_step

    def fetch(c, t):
        source = field.at[c, :, pl.ds(t * lanes, lanes)]
        return pltpu.make_async_copy(source, columns.at[t], arrived.at[t])

    for t in range(tiles):
        fetch(comps[0], t).start()
    for i, c in enumerate(comps):
        for t in range(tiles):
            fetch(c, t).wait()

            def unpack(r, carry):
                start = pl.multiple_of(r * 8, 8)
                plane = [columns[t, pl.ds(start * planes + z, 8, planes), :] for z in range(planes)]
                at = (pl.ds(start, 8), pl.ds(t * lanes, lanes))
                for p in range(2):
                    z = 3 + p
                    centre = plane[z]
                    u1, u2, u3 = plane[z + 1], plane[z + 2], plane[z + 3]
                    d1, d2, d3 = plane[z - 1], plane[z - 2], plane[z - 3]
                    slope = 0.75 * (u1 - d1) - 0.15 * (u2 - d2) + (1.0 / 60.0) * (u3 - d3)
                    curve = 1.5 * (u1 + d1) - 0.15 * (u2 + d2) + (1.0 / 90.0) * (u3 + d3)
                    inner[(0, p) + at] = centre
                    depth[(0, p) + at] = slope
                    sums[(0, p) + at] = centre + gain * (curve - (49.0 / 18.0) * centre)
                return carry

            lax.fori_loop(0, slab // 8, unpack, 0, unroll=4)
            if i + 1 < len(comps):
                fetch(comps[i + 1], t).start()

        for p in range(2):
            send(i, 0, p).start()
            send(i, 1, p).start()
        rows = m_top.shape[0] // 2
        for p in range(2):
            for start, rim in ((0, before), (reach + slab, after)):
                high, low = split(rim[c, :, p])
                high_x[start : start + reach, :] = high
                low_x[start : start + reach, :] = low

            def fill(r, carry):
                start = pl.multiple_of(r * 16, 16)
                at = pl.ds(start, 16)
                to = pl.ds(pl.multiple_of(start + reach, 16), 16)
                high, low = split(inner[0, p, at, :])
                high_x[to, :] = high
                low_x[to, :] = low
                high_s[at, :] = half_turned(high)
                low_s[at, :] = half_turned(low)
                return carry

            lax.fori_loop(0, slab // 16, fill, 0, unroll=8)
            for b in range(slab // rows):
                window = pl.ds(b * rows, rows + 2 * reach)
                at = pl.ds(b * rows, rows)
                one = product(m_all[...], high_x[window, :])
                two = product(m_top[...], low_x[window, :])
                along[0, p, at, :] = one[:rows] + one[2 * rows :] + two[:rows]
                curve = (gain / 180.0) * (one[rows : 2 * rows] + two[rows:])
                sums[0, p, at, :] = sums[0, p, at, :] + curve
            send(i, 2, p).start()
            for t in range(tiles):
                side = pl.ds(t * lanes, lanes)
                window = pl.ds(t * lanes, 2 * lanes)
                both = product(high_s[:, window], turn[...]) + product(low_s[:, window], turn[...])
                across[0, p, :, side] = both[:, :lanes] * (1.0 / 60.0)
                curve = both[:, lanes:] * (gain / 180.0)
                sums[0, p, :, side] = sums[0, p, :, side] + curve
            send(i, 3, p).start()
            send(i, 4, p).start()
        for n in range(5):
            for p in range(2):
                send(i, n, p).wait()
    token[0] = 0


def field_terms(comps, room, field, before, after, viscosity, length):
    _, slab, planes, width = field.shape
    flat = field.reshape(-1, slab * planes, width)
    rows = min(slab, 128)
    high, low, second = along_matrices(rows, length)
    top = np.concatenate([high, second], 0)
    everything = np.concatenate([high, second, low], 0)
    turn = across_matrix([first_at(0), [t for t in second_at(0) if t[0] != 0]])
    shape = jax.ShapeDtypeStruct((len(comps), 5, 2, slab, width), jnp.float32)
    spec = pl.BlockSpec(memory_space=pltpu.HBM)
    near = pl.BlockSpec(memory_space=pltpu.VMEM)
    return pl.pallas_call(
        functools.partial(field_kernel, comps),
        out_shape=(shape, jax.ShapeDtypeStruct((1,), jnp.int32)),
        in_specs=[pl.BlockSpec(memory_space=pltpu.SMEM)]
        + [near] * 5
        + [pl.BlockSpec(memory_space=pl.ANY)],
        out_specs=(spec, pl.BlockSpec(memory_space=pltpu.SMEM)),
        compiler_params=grant(room),
        scratch_shapes=[pltpu.VMEM((1, 2, slab, width), jnp.float32)] * 5
        + [
            pltpu.VMEM((width // lanes, slab * planes, lanes), jnp.float32),
            pltpu.VMEM((slab, width + lanes), jnp.bfloat16),
            pltpu.VMEM((slab, width + lanes), jnp.bfloat16),
            pltpu.VMEM((slab + 2 * reach, width), jnp.bfloat16),
            pltpu.VMEM((slab + 2 * reach, width), jnp.bfloat16),
            pltpu.SemaphoreType.DMA((width // lanes,)),
            pltpu.SemaphoreType.DMA((5, 2)),
        ],
        cost_estimate=pl.CostEstimate(
            flops=0, bytes_accessed=4 * len(comps) * slab * planes * width * 2, transcendentals=0
        ),
    )(
        viscosity, jnp.asarray(turn), jnp.asarray(everything), jnp.asarray(top), before, after, flat
    )


def final_kernel(
    groups, core, m_both, turn, held0, other0, held1, other1, before, after, before2, after2, *refs
):
    terms, scratch = refs[: len(groups)], refs[len(groups) :]
    kept = {c: (g, i) for g, comps in enumerate(groups) for i, c in enumerate(comps)}
    inner, depth, along, across, sums = [
        [terms[kept[c][0]].at[kept[c][1], n] for c in range(3)] for n in range(5)
    ]
    out, base_s, turned_s, flow_s, ghost_s, slope_s, side_s, arrived = scratch
    step = pl.program_id(0)
    rows = slope_s.shape[2]
    quarter = held0.shape[3]
    slab = 4 * quarter
    inverse = 1.0 / code_scale

    def decoded(values):
        return values.astype(jnp.int32).astype(jnp.float32) * inverse

    def load(flow, ghost, before, after):
        for c in range(3):
            for p in range(2):
                base_s[c, p, 0:reach] = decoded(before[p, c]).astype(jnp.bfloat16)
                base_s[c, p, reach + slab :] = decoded(after[p, c]).astype(jnp.bfloat16)
        copies = []
        for u in range(2):
            for k in range(2):
                at = pl.ds(streams[u][k] * quarter, quarter)
                for n, (source, target) in enumerate(((flow, flow_s), (ghost, ghost_s))):
                    copies.append(
                        pltpu.make_async_copy(
                            source[u].at[k], target.at[:, :, at], arrived.at[4 * n + 2 * u + k]
                        )
                    )
        for copy in copies:
            copy.start()
        for copy in copies:
            copy.wait()

    @pl.when(step == 0)
    def _():
        @pl.when(core[0] == 0)
        def _():
            load((held0, held1), (other0, other1), before, after)

        @pl.when(core[0] != 0)
        def _():
            load((other0, other1), (held0, held1), before2, after2)

        def fill(i, carry):
            start = pl.multiple_of(i * 16, 16)
            to = pl.ds(pl.multiple_of(start + reach, 16), 16)
            for c in range(3):
                for p in range(2):
                    values = decoded(flow_s[p, c, pl.ds(start, 16), :])
                    base_s[c, p, to, :] = values.astype(jnp.bfloat16)
            return carry

        lax.fori_loop(0, slab // 16, fill, 0)

    origin = pl.multiple_of(step * rows, 32)
    def derive(c, carry):
        for p in range(2):
            both = product(m_both[...], base_s[c, p, pl.ds(origin, rows + 2 * reach), :])
            slope_s[c, p] = both[:rows] + both[rows:]
            for r in range(0, rows, 16):
                here = pl.ds(pl.multiple_of(origin + reach + r, 16), 16)
                turned_s[r : r + 16, :] = half_turned(base_s[c, p, here, :])
            for t in range(side_s.shape[3] // lanes):
                window = turned_s[:, pl.ds(t * lanes, 2 * lanes)]
                side_s[c, p, :, pl.ds(t * lanes, lanes)] = product(window, turn[...])
        return carry

    lax.fori_loop(0, 3, derive, 0)

    def body(i, carry):
        start = pl.multiple_of(i * 16, 16)
        at = pl.ds(start, 16)
        there = pl.ds(pl.multiple_of(origin + start, 16), 16)
        inside = pl.ds(pl.multiple_of(origin + reach + start, 16), 16)
        flow = [
            [base_s[c, p, inside, :].astype(jnp.float32) for p in range(2)] for c in range(3)
        ]
        for p in range(2):
            move = [inner[c][p, at, :] for c in range(3)]
            for c in range(3):
                dz = decoded(ghost_s[p, c, there, :])
                if p == 0:
                    dz = dz + 0.75 * flow[c][1]
                else:
                    dz = dz - 0.75 * flow[c][0]
                dy = side_s[c, p, at, :] * (1.0 / 60.0)
                total = flow[0][p] * along[c][p, at, :] + flow[1][p] * across[c][p, at, :]
                total = total + flow[2][p] * depth[c][p, at, :]
                total = total + move[0] * slope_s[c, p, at, :] + move[1] * dy + move[2] * dz
                out[0, c, at, p, :] = sums[c][p, at, :] - section_step * total
        return carry

    lax.fori_loop(0, rows // 16, body, 0)


def final(core, pieces, rims, terms, length):
    _, _, pair, slab, width = terms[0].shape
    comps = sum(t.shape[0] for t in terms)
    groups = tuple(comps_of for comps_of, _ in shares.values())
    rows = min(slab, 64)
    turn = across_matrix([first_at(0)])
    high, low, _ = along_matrices(rows, length)
    both = np.concatenate([high, low], 0)
    whole = pl.BlockSpec(memory_space=pl.ANY)
    rim = pl.BlockSpec(rims[0].shape, lambda i: (0, 0, 0, 0))
    specs = [
        pl.BlockSpec((t.shape[0], 5, pair, rows, width), lambda i: (0, 0, 0, i, 0)) for t in terms
    ]
    return pl.pallas_call(
        functools.partial(final_kernel, groups),
        out_shape=jax.ShapeDtypeStruct((1, comps, slab, pair, width), jnp.float32),
        grid=(slab // rows,),
        in_specs=[
            pl.BlockSpec(memory_space=pltpu.SMEM),
            pl.BlockSpec(both.shape, lambda i: (0, 0)),
            pl.BlockSpec(turn.shape, lambda i: (0, 0)),
        ]
        + [whole] * 4
        + [rim] * 4
        + specs,
        out_specs=pl.BlockSpec((1, comps, rows, pair, width), lambda i: (0, 0, i, 0, 0)),
        compiler_params=grant(58),
        scratch_shapes=[
            pltpu.VMEM((comps, pair, slab + 2 * reach, width), jnp.bfloat16),
            pltpu.VMEM((rows, width + lanes), jnp.bfloat16),
            pltpu.VMEM((pair, comps, slab, width), jnp.int16),
            pltpu.VMEM((pair, comps, slab, width), jnp.int16),
            pltpu.VMEM((comps, pair, rows, width), jnp.float32),
            pltpu.VMEM((comps, pair, rows, width), jnp.float32),
            pltpu.SemaphoreType.DMA((8,)),
        ],
        cost_estimate=pl.CostEstimate(
            flops=0, bytes_accessed=8 * comps * pair * slab * width, transcendentals=0
        ),
    )(core, jnp.asarray(both), jnp.asarray(turn), *pieces, *rims, *terms)


def ring(last, first):
    size = lax.axis_size("gx")
    up = [(i, (i + 1) % size) for i in range(size)]
    down = [(j, i) for i, j in up]
    return lax.ppermute(last, "gx", up), lax.ppermute(first, "gx", down)


def narrowed(rows, near):
    high = lax.reduce_precision(rows, 8, 7)
    low = (rows - high)[:, near]
    return jnp.concatenate([high, low], 1).astype(jnp.bfloat16)


def widened(sent, near):
    rows = sent[:, :reach].astype(jnp.float32)
    low = sent[:, reach:].astype(jnp.float32)
    around = [(0, 0)] * rows.ndim
    around[1] = (near.start, reach - near.stop)
    return rows + jnp.pad(low, around)


def swap(array, bit):
    return lax.ppermute(array, "pert", [(i, i ^ bit) for i in range(lax.axis_size("pert"))])


def exchange(mine, theirs, root, gate, work):
    me = lax.axis_index("pert")
    is_root = me == root
    place = (me // 2) ^ (root // 2)
    at_a, at_b, at_c = place == 0, place == 1, place == 2
    handed = [swap(t, 1) for t in theirs]

    def owned(u, h, k):
        return jnp.where(is_root, mine[u][h, k], handed[u][h, k])

    opening = [owned(u, h, 0) for u in range(2) for h in range(2)]
    opening = gate(*opening)
    source = [
        [[opening[2 * u + h]] + [owned(u, h, k) for k in range(1, phases)] for h in range(2)]
        for u in range(2)
    ]
    X = [[], []]
    Y = [[], []]
    for s in range(phases + 1):
        for u in range(2):
            k = min(s, phases - 1)
            one, two = source[u][0][k], source[u][1][k]
            if s == phases:
                one, two = two, one
            if s > 0:
                one = jnp.where(at_a, one, Y[u][s - 1])
                two = jnp.where(at_a, two, X[u][s - 1])
                one, two, place = gate(one, two, place)
                at_a, at_b, at_c = place == 0, place == 1, place == 2
            X[u].append(swap(one, 2))
            Y[u].append(swap(two, 4))
            if (s, u) in shares:
                place = place + work(shares[s, u])
                at_a, at_b, at_c = place == 0, place == 1, place == 2
    held = []
    for u in range(2):
        parts = []
        for k in range(phases):
            row = []
            for h in range(2):
                P1, P2 = (X[u], Y[u]) if h == 0 else (Y[u], X[u])
                near, far = (at_b, at_c) if h == 0 else (at_c, at_b)
                late = P1[k + 2] if k + 2 <= phases else P2[phases]
                value = jnp.where(near, P1[k], jnp.where(far, late, P2[k + 1]))
                row.append(jnp.where(at_a, source[u][h][k], value))
            parts.append(jnp.stack(row, 0))
        held.append(jnp.stack(parts, 0))
        if u == 0:
            quarter = held[0].shape[3]
            size = lax.axis_size("gx")
            pairs = [
                (c * size + i, c * size + (i + 1) % size)
                for c in range(0, lax.axis_size("pert"), 2)
                for i in range(size)
            ]
            both = ("pert", "gx")
            before = lax.ppermute(held[0][1][:, :, quarter - reach :], both, pairs)
            after = lax.ppermute(held[0][0][:, :, :reach], both, [(j, i) for i, j in pairs])
            before, after, place = lax.optimization_barrier((before, after, place))
            second = [swap(before, 1), swap(after, 1)]
            at_a, at_b, at_c = place == 0, place == 1, place == 2
    other = [swap(h, 1) for h in held]
    return (held[0], other[0], held[1], other[1]), (before, after, *second)


def per_device(pert_field, base_store, section_owner, pert_ids, member_visc):
    _, comps, slab, planes, width = pert_field.shape
    length = slab * lax.axis_size("gx")
    member_pick = pert_ids[0] == jnp.arange(member_visc.shape[0], dtype=jnp.int32)
    viscosity = jnp.sum(jnp.where(member_pick, member_visc, 0.0))[None]
    levels_here = base_store.shape[0]
    owner_slot = section_owner[0] % levels_here
    owner_root = section_owner[0] // levels_here
    tiles = base_store.reshape(levels_here, comps, slab * planes, width)
    tile = tiles[0] if levels_here == 1 else lax.dynamic_index_in_dim(tiles, owner_slot, 0, False)
    me = lax.axis_index("pert")
    in_pairs = lax.axis_size("pert") == 8
    core = (me % 2 if in_pairs else jnp.zeros_like(me)).astype(jnp.int32)[None]
    field = pert_field[0]
    last = narrowed(field[:, slab - reach :, 3:5], slice(reach - 4, reach))
    first = narrowed(field[:, :reach, 3:5], slice(0, 4))
    last, first, tile = lax.optimization_barrier((last, first, tile))
    before, after = ring(last, first)
    before, after = widened(before, slice(reach - 4, reach)), widened(after, slice(0, 4))
    halves = [pack(tile, planes, core, u) for u in range(2)]
    done = {"field": field, "terms": []}

    def gate(*values):
        done["field"], *values = lax.optimization_barrier((done["field"], *values))
        return values

    def work(share):
        terms, token = field_terms(*share, done["field"], before, after, viscosity, length)
        done["terms"].append(terms)
        return token[0]

    if in_pairs:
        mine, theirs = [h[0] for h in halves], [h[1] for h in halves]
        pieces, rims = exchange(mine, theirs, owner_root, gate, work)
    else:
        for share in shares.values():
            work(share)
        pieces = [
            lax.psum(jnp.where(me == owner_root, a, 0).astype(jnp.float32), "pert").astype(a.dtype)
            for h in halves
            for a in h
        ]
        pieces = [a.transpose(1, 0, 2, 3, 4) for a in pieces]
        quarter = slab // 4
        rims = ring(pieces[0][1][:, :, quarter - reach :], pieces[0][0][:, :, :reach]) * 2
    return final(core, pieces, rims, done["terms"], length)


def solution(mesh):
    placed = (
        P("pert", None, "gx", None, None),
        P("pert", None, "gx", None, None),
        P(),
        P("pert"),
        P(),
    )
    return jax.shard_map(
        per_device,
        mesh=mesh,
        in_specs=placed,
        out_specs=P("pert", None, "gx", None, None),
        check_vma=False,
    )
```

```python
import functools

import jax
import jax.numpy as jnp
import numpy as np
from jax import lax
from jax.experimental import pallas as pl
from jax.experimental.pallas import tpu as pltpu
from jax.sharding import PartitionSpec as P

section_step = 0.25
reach = 16
lanes = 128
code_scale = 4096.0
phases = 2
streams = ((0, 3), (1, 2))
shares = {(0, 1): ((0,), 57), (1, 1): ((1, 2), 57)}


def grant(mib):
    return pltpu.CompilerParams(vmem_limit_bytes=mib << 20)


def compact_kernel(length):
    wave = 2.0 * np.pi * np.arange(length) / length
    symbol = 14.0 / 9.0 * np.sin(wave) + 1.0 / 18.0 * np.sin(2.0 * wave)
    symbol = 1j * symbol / (1.0 + 2.0 / 3.0 * np.cos(wave))
    return np.real(np.fft.ifft(symbol))


def along_matrices(rows, length):
    kernel = compact_kernel(length)
    first = np.zeros((rows, rows + 2 * reach))
    second = np.zeros((rows, rows + 2 * reach))
    for i in range(rows):
        for k in range(-reach, reach + 1):
            first[i, i + reach + k] = kernel[-k % length]
        for k, weight in ((0, -980.0), (1, 270.0), (2, -27.0), (3, 2.0)):
            second[i, i + reach + k] = weight
            second[i, i + reach - k] = weight
    high = first.astype(jnp.bfloat16)
    low = (first - high.astype(np.float64)).astype(jnp.bfloat16)
    return high, low, second.astype(jnp.bfloat16)


first_taps = ((1, 45.0), (2, -9.0), (3, 1.0))
second_taps = ((0, -490.0), (1, 270.0), (2, -27.0), (3, 2.0))


def depth_matrix(rows, planes, fields):
    matrix = np.zeros((len(fields) * rows, rows * planes))
    for f, taps in enumerate(fields):
        for i in range(rows):
            for z, weight in taps:
                matrix[f * rows + i, i * planes + z] += weight
    return matrix.astype(jnp.bfloat16)


def first_at(z):
    return [(z + k, w) for k, w in first_taps] + [(z - k, -w) for k, w in first_taps]


def second_at(z):
    taps = [(z + k, w) for k, w in second_taps]
    return taps + [(z - k, w) for k, w in second_taps if k > 0]


def across_matrix(orders):
    matrix = np.zeros((2 * lanes, lanes * len(orders)))
    for o, taps in enumerate(orders):
        for i in range(lanes):
            for k, weight in taps:
                matrix[lanes // 2 + i + k, o * lanes + i] += weight
    return matrix.astype(jnp.bfloat16)


def half_turned(values):
    half = lanes // 2
    return jnp.concatenate([values[:, -half:], values, values[:, :half]], 1)


def product(a, b):
    return jnp.dot(a, b, preferred_element_type=jnp.float32)


def split(values):
    high = values.astype(jnp.bfloat16)
    return high, (values - high.astype(jnp.float32)).astype(jnp.bfloat16)


def pack_kernel(core, weights, tile, mine, theirs):
    rows = weights.shape[0] // 4
    blocks = mine.shape[3] // rows

    def store(kept, sent):
        for b in range(blocks):
            depth = weights.shape[1]
            mixed = product(weights[...], tile[0, b * depth : (b + 1) * depth])
            for f in range(4):
                scale = code_scale if f < 2 else code_scale / 60.0
                part = jnp.round(mixed[f * rows : (f + 1) * rows] * scale)
                target = kept if f < 2 else sent
                code = part.astype(jnp.int32).astype(jnp.int16)
                target[f % 2, 0, 0, b * rows : (b + 1) * rows] = code

    @pl.when(core[0] == 0)
    def _():
        store(mine, theirs)

    @pl.when(core[0] != 0)
    def _():
        store(theirs, mine)


def pack(tile, planes, core, which):
    comps, deep, width = tile.shape
    quarter = deep // planes // 4
    x_rows = min(quarter, 32)
    ghost = [[t for t in first_at(z) if t[0] not in (3, 4)] for z in (3, 4)]
    weights = depth_matrix(x_rows, planes, [[(3, 1.0)], [(4, 1.0)]] + ghost)
    first, second = streams[which]
    shape = jax.ShapeDtypeStruct((2, 2, comps, quarter, width), jnp.int16)
    spec = pl.BlockSpec((2, 1, 1, quarter, width), lambda k, c: (0, k, c, 0, 0))
    return pl.pallas_call(
        pack_kernel,
        out_shape=(shape,) * 2,
        grid=(2, comps),
        in_specs=[
            pl.BlockSpec(memory_space=pltpu.SMEM),
            pl.BlockSpec(weights.shape, lambda k, c: (0, 0)),
            pl.BlockSpec(
                (1, quarter * planes, width), lambda k, c: (c, first + k * (second - first), 0)
            ),
        ],
        out_specs=(spec,) * 2,
        compiler_params=grant(16),
        cost_estimate=pl.CostEstimate(
            flops=0, bytes_accessed=2 * comps * deep * width, transcendentals=0
        ),
    )(core, jnp.asarray(weights), tile)


def field_kernel(comps, viscosity, turn, m_all, m_top, before, after, field, out, token, *scratch):
    terms = scratch[:5]
    columns, high_s, low_s, high_x, low_x, arrived, left = scratch[5:]
    inner, depth, along, across, sums = terms

    def send(i, n, p):
        return pltpu.make_async_copy(terms[n].at[i, p], out.at[i, n, p], left.at[i, n, p])

    slab, width = inner.shape[2:]
    planes = field.shape[1] // slab
    tiles = width // lanes
    gain = viscosity[0] * section_step

    def fetch(c, t):
        source = field.at[c, :, pl.ds(t * lanes, lanes)]
        return pltpu.make_async_copy(source, columns.at[t], arrived.at[t])

    for t in range(tiles):
        fetch(comps[0], t).start()
    for i, c in enumerate(comps):
        for t in range(tiles):
            fetch(c, t).wait()

            def unpack(r, carry):
                start = pl.multiple_of(r * 8, 8)
                plane = [columns[t, pl.ds(start * planes + z, 8, planes), :] for z in range(planes)]
                at = (pl.ds(start, 8), pl.ds(t * lanes, lanes))
                for p in range(2):
                    z = 3 + p
                    centre = plane[z]
                    u1, u2, u3 = plane[z + 1], plane[z + 2], plane[z + 3]
                    d1, d2, d3 = plane[z - 1], plane[z - 2], plane[z - 3]
                    slope = 0.75 * (u1 - d1) - 0.15 * (u2 - d2) + (1.0 / 60.0) * (u3 - d3)
                    curve = 1.5 * (u1 + d1) - 0.15 * (u2 + d2) + (1.0 / 90.0) * (u3 + d3)
                    inner[(i, p) + at] = centre
                    depth[(i, p) + at] = slope
                    sums[(i, p) + at] = centre + gain * (curve - (49.0 / 18.0) * centre)
                return carry

            lax.fori_loop(0, slab // 8, unpack, 0, unroll=4)
            if i + 1 < len(comps):
                fetch(comps[i + 1], t).start()

        for p in range(2):
            send(i, 0, p).start()
            send(i, 1, p).start()
        rows = m_top.shape[0] // 2
        for p in range(2):
            for start, rim in ((0, before), (reach + slab, after)):
                high, low = split(rim[c, :, p])
                high_x[start : start + reach, :] = high
                low_x[start : start + reach, :] = low

            def fill(r, carry):
                start = pl.multiple_of(r * 16, 16)
                at = pl.ds(start, 16)
                to = pl.ds(pl.multiple_of(start + reach, 16), 16)
                high, low = split(inner[i, p, at, :])
                high_x[to, :] = high
                low_x[to, :] = low
                high_s[at, :] = half_turned(high)
                low_s[at, :] = half_turned(low)
                return carry

            lax.fori_loop(0, slab // 16, fill, 0, unroll=8)
            for b in range(slab // rows):
                window = pl.ds(b * rows, rows + 2 * reach)
                at = pl.ds(b * rows, rows)
                one = product(m_all[...], high_x[window, :])
                two = product(m_top[...], low_x[window, :])
                along[i, p, at, :] = one[:rows] + one[2 * rows :] + two[:rows]
                curve = (gain / 180.0) * (one[rows : 2 * rows] + two[rows:])
                sums[i, p, at, :] = sums[i, p, at, :] + curve
            send(i, 2, p).start()
            for t in range(tiles):
                side = pl.ds(t * lanes, lanes)
                window = pl.ds(t * lanes, 2 * lanes)
                both = product(high_s[:, window], turn[...]) + product(low_s[:, window], turn[...])
                across[i, p, :, side] = both[:, :lanes] * (1.0 / 60.0)
                curve = both[:, lanes:] * (gain / 180.0)
                sums[i, p, :, side] = sums[i, p, :, side] + curve
            send(i, 3, p).start()
            send(i, 4, p).start()
    for i in range(len(comps)):
        for n in range(5):
            for p in range(2):
                send(i, n, p).wait()
    token[0] = 0


def field_terms(comps, room, field, before, after, viscosity, length):
    _, slab, planes, width = field.shape
    flat = field.reshape(-1, slab * planes, width)
    rows = min(slab, 128)
    high, low, second = along_matrices(rows, length)
    top = np.concatenate([high, second], 0)
    everything = np.concatenate([high, second, low], 0)
    turn = across_matrix([first_at(0), [t for t in second_at(0) if t[0] != 0]])
    shape = jax.ShapeDtypeStruct((len(comps), 5, 2, slab, width), jnp.float32)
    spec = pl.BlockSpec(memory_space=pltpu.HBM)
    near = pl.BlockSpec(memory_space=pltpu.VMEM)
    return pl.pallas_call(
        functools.partial(field_kernel, comps),
        out_shape=(shape, jax.ShapeDtypeStruct((1,), jnp.int32)),
        in_specs=[pl.BlockSpec(memory_space=pltpu.SMEM)]
        + [near] * 5
        + [pl.BlockSpec(memory_space=pl.ANY)],
        out_specs=(spec, pl.BlockSpec(memory_space=pltpu.SMEM)),
        compiler_params=grant(room),
        scratch_shapes=[pltpu.VMEM((len(comps), 2, slab, width), jnp.float32)] * 5
        + [
            pltpu.VMEM((width // lanes, slab * planes, lanes), jnp.float32),
            pltpu.VMEM((slab, width + lanes), jnp.bfloat16),
            pltpu.VMEM((slab, width + lanes), jnp.bfloat16),
            pltpu.VMEM((slab + 2 * reach, width), jnp.bfloat16),
            pltpu.VMEM((slab + 2 * reach, width), jnp.bfloat16),
            pltpu.SemaphoreType.DMA((width // lanes,)),
            pltpu.SemaphoreType.DMA((len(comps), 5, 2)),
        ],
        cost_estimate=pl.CostEstimate(
            flops=0, bytes_accessed=4 * len(comps) * slab * planes * width * 2, transcendentals=0
        ),
    )(
        viscosity, jnp.asarray(turn), jnp.asarray(everything), jnp.asarray(top), before, after, flat
    )


def final_kernel(
    groups, core, m_both, turn, held0, other0, held1, other1, before, after, before2, after2, *refs
):
    terms, scratch = refs[: len(groups)], refs[len(groups) :]
    kept = {c: (g, i) for g, comps in enumerate(groups) for i, c in enumerate(comps)}
    inner, depth, along, across, sums = [
        [terms[kept[c][0]].at[kept[c][1], n] for c in range(3)] for n in range(5)
    ]
    out, base_s, turned_s, flow_s, ghost_s, slope_s, side_s, arrived = scratch
    step = pl.program_id(0)
    rows = slope_s.shape[2]
    quarter = held0.shape[3]
    slab = 4 * quarter
    inverse = 1.0 / code_scale

    def decoded(values):
        return values.astype(jnp.int32).astype(jnp.float32) * inverse

    def load(flow, ghost, before, after):
        for c in range(3):
            for p in range(2):
                base_s[c, p, 0:reach] = decoded(before[p, c]).astype(jnp.bfloat16)
                base_s[c, p, reach + slab :] = decoded(after[p, c]).astype(jnp.bfloat16)
        copies = []
        for u in range(2):
            for k in range(2):
                at = pl.ds(streams[u][k] * quarter, quarter)
                for n, (source, target) in enumerate(((flow, flow_s), (ghost, ghost_s))):
                    copies.append(
                        pltpu.make_async_copy(
                            source[u].at[k], target.at[:, :, at], arrived.at[4 * n + 2 * u + k]
                        )
                    )
        for copy in copies:
            copy.start()
        for copy in copies:
            copy.wait()

    @pl.when(step == 0)
    def _():
        @pl.when(core[0] == 0)
        def _():
            load((held0, held1), (other0, other1), before, after)

        @pl.when(core[0] != 0)
        def _():
            load((other0, other1), (held0, held1), before2, after2)

        def fill(i, carry):
            start = pl.multiple_of(i * 16, 16)
            to = pl.ds(pl.multiple_of(start + reach, 16), 16)
            for c in range(3):
                for p in range(2):
                    values = decoded(flow_s[p, c, pl.ds(start, 16), :])
                    base_s[c, p, to, :] = values.astype(jnp.bfloat16)
            return carry

        lax.fori_loop(0, slab // 16, fill, 0)

    origin = pl.multiple_of(step * rows, 32)
    def derive(c, carry):
        for p in range(2):
            both = product(m_both[...], base_s[c, p, pl.ds(origin, rows + 2 * reach), :])
            slope_s[c, p] = both[:rows] + both[rows:]
            for r in range(0, rows, 16):
                here = pl.ds(pl.multiple_of(origin + reach + r, 16), 16)
                turned_s[r : r + 16, :] = half_turned(base_s[c, p, here, :])
            for t in range(side_s.shape[3] // lanes):
                window = turned_s[:, pl.ds(t * lanes, 2 * lanes)]
                side_s[c, p, :, pl.ds(t * lanes, lanes)] = product(window, turn[...])
        return carry

    lax.fori_loop(0, 3, derive, 0)

    def body(i, carry):
        start = pl.multiple_of(i * 16, 16)
        at = pl.ds(start, 16)
        there = pl.ds(pl.multiple_of(origin + start, 16), 16)
        inside = pl.ds(pl.multiple_of(origin + reach + start, 16), 16)
        flow = [
            [base_s[c, p, inside, :].astype(jnp.float32) for p in range(2)] for c in range(3)
        ]
        for p in range(2):
            move = [inner[c][p, at, :] for c in range(3)]
            for c in range(3):
                dz = decoded(ghost_s[p, c, there, :])
                if p == 0:
                    dz = dz + 0.75 * flow[c][1]
                else:
                    dz = dz - 0.75 * flow[c][0]
                dy = side_s[c, p, at, :] * (1.0 / 60.0)
                total = flow[0][p] * along[c][p, at, :] + flow[1][p] * across[c][p, at, :]
                total = total + flow[2][p] * depth[c][p, at, :]
                total = total + move[0] * slope_s[c, p, at, :] + move[1] * dy + move[2] * dz
                out[0, c, at, p, :] = sums[c][p, at, :] - section_step * total
        return carry

    lax.fori_loop(0, rows // 16, body, 0)


def final(core, pieces, rims, terms, length):
    _, _, pair, slab, width = terms[0].shape
    comps = sum(t.shape[0] for t in terms)
    groups = tuple(comps_of for comps_of, _ in shares.values())
    rows = min(slab, 64)
    turn = across_matrix([first_at(0)])
    high, low, _ = along_matrices(rows, length)
    both = np.concatenate([high, low], 0)
    whole = pl.BlockSpec(memory_space=pl.ANY)
    rim = pl.BlockSpec(rims[0].shape, lambda i: (0, 0, 0, 0))
    specs = [
        pl.BlockSpec((t.shape[0], 5, pair, rows, width), lambda i: (0, 0, 0, i, 0)) for t in terms
    ]
    return pl.pallas_call(
        functools.partial(final_kernel, groups),
        out_shape=jax.ShapeDtypeStruct((1, comps, slab, pair, width), jnp.float32),
        grid=(slab // rows,),
        in_specs=[
            pl.BlockSpec(memory_space=pltpu.SMEM),
            pl.BlockSpec(both.shape, lambda i: (0, 0)),
            pl.BlockSpec(turn.shape, lambda i: (0, 0)),
        ]
        + [whole] * 4
        + [rim] * 4
        + specs,
        out_specs=pl.BlockSpec((1, comps, rows, pair, width), lambda i: (0, 0, i, 0, 0)),
        compiler_params=grant(58),
        scratch_shapes=[
            pltpu.VMEM((comps, pair, slab + 2 * reach, width), jnp.bfloat16),
            pltpu.VMEM((rows, width + lanes), jnp.bfloat16),
            pltpu.VMEM((pair, comps, slab, width), jnp.int16),
            pltpu.VMEM((pair, comps, slab, width), jnp.int16),
            pltpu.VMEM((comps, pair, rows, width), jnp.float32),
            pltpu.VMEM((comps, pair, rows, width), jnp.float32),
            pltpu.SemaphoreType.DMA((8,)),
        ],
        cost_estimate=pl.CostEstimate(
            flops=0, bytes_accessed=8 * comps * pair * slab * width, transcendentals=0
        ),
    )(core, jnp.asarray(both), jnp.asarray(turn), *pieces, *rims, *terms)


def ring(last, first):
    size = lax.axis_size("gx")
    up = [(i, (i + 1) % size) for i in range(size)]
    down = [(j, i) for i, j in up]
    return lax.ppermute(last, "gx", up), lax.ppermute(first, "gx", down)


def swap(array, bit):
    return lax.ppermute(array, "pert", [(i, i ^ bit) for i in range(lax.axis_size("pert"))])


def exchange(mine, theirs, root, gate, work):
    me = lax.axis_index("pert")
    is_root = me == root
    place = (me // 2) ^ (root // 2)
    at_a, at_b, at_c = place == 0, place == 1, place == 2
    handed = [swap(t, 1) for t in theirs]

    def owned(u, h, k):
        return jnp.where(is_root, mine[u][h, k], handed[u][h, k])

    opening = [owned(u, h, 0) for u in range(2) for h in range(2)]
    opening = gate(*opening)
    source = [
        [[opening[2 * u + h]] + [owned(u, h, k) for k in range(1, phases)] for h in range(2)]
        for u in range(2)
    ]
    X = [[], []]
    Y = [[], []]
    for s in range(phases + 1):
        for u in range(2):
            k = min(s, phases - 1)
            one, two = source[u][0][k], source[u][1][k]
            if s == phases:
                one, two = two, one
            if s > 0:
                one = jnp.where(at_a, one, Y[u][s - 1])
                two = jnp.where(at_a, two, X[u][s - 1])
                one, two, place = gate(one, two, place)
                at_a, at_b, at_c = place == 0, place == 1, place == 2
            X[u].append(swap(one, 2))
            Y[u].append(swap(two, 4))
            if (s, u) in shares:
                place = place + work(shares[s, u])
                at_a, at_b, at_c = place == 0, place == 1, place == 2
    held = []
    for u in range(2):
        parts = []
        for k in range(phases):
            row = []
            for h in range(2):
                P1, P2 = (X[u], Y[u]) if h == 0 else (Y[u], X[u])
                near, far = (at_b, at_c) if h == 0 else (at_c, at_b)
                late = P1[k + 2] if k + 2 <= phases else P2[phases]
                value = jnp.where(near, P1[k], jnp.where(far, late, P2[k + 1]))
                row.append(jnp.where(at_a, source[u][h][k], value))
            parts.append(jnp.stack(row, 0))
        held.append(jnp.stack(parts, 0))
        if u == 0:
            quarter = held[0].shape[3]
            size = lax.axis_size("gx")
            pairs = [
                (c * size + i, c * size + (i + 1) % size)
                for c in range(0, lax.axis_size("pert"), 2)
                for i in range(size)
            ]
            both = ("pert", "gx")
            before = lax.ppermute(held[0][1][:, :, quarter - reach :], both, pairs)
            after = lax.ppermute(held[0][0][:, :, :reach], both, [(j, i) for i, j in pairs])
            before, after, place = lax.optimization_barrier((before, after, place))
            second = [swap(before, 1), swap(after, 1)]
            at_a, at_b, at_c = place == 0, place == 1, place == 2
    other = [swap(h, 1) for h in held]
    return (held[0], other[0], held[1], other[1]), (before, after, *second)


def per_device(pert_field, base_store, section_owner, pert_ids, member_visc):
    _, comps, slab, planes, width = pert_field.shape
    length = slab * lax.axis_size("gx")
    member_pick = pert_ids[0] == jnp.arange(member_visc.shape[0], dtype=jnp.int32)
    viscosity = jnp.sum(jnp.where(member_pick, member_visc, 0.0))[None]
    levels_here = base_store.shape[0]
    owner_slot = section_owner[0] % levels_here
    owner_root = section_owner[0] // levels_here
    tiles = base_store.reshape(levels_here, comps, slab * planes, width)
    tile = tiles[0] if levels_here == 1 else lax.dynamic_index_in_dim(tiles, owner_slot, 0, False)
    me = lax.axis_index("pert")
    in_pairs = lax.axis_size("pert") == 8
    core = (me % 2 if in_pairs else jnp.zeros_like(me)).astype(jnp.int32)[None]
    field = pert_field[0]
    last, first, tile = lax.optimization_barrier(
        (field[:, slab - reach :, 3:5], field[:, :reach, 3:5], tile)
    )
    before, after = ring(last, first)
    halves = [pack(tile, planes, core, u) for u in range(2)]
    done = {"field": field, "terms": []}

    def gate(*values):
        done["field"], *values = lax.optimization_barrier((done["field"], *values))
        return values

    def work(share):
        terms, token = field_terms(*share, done["field"], before, after, viscosity, length)
        done["terms"].append(terms)
        return token[0]

    if in_pairs:
        mine, theirs = [h[0] for h in halves], [h[1] for h in halves]
        pieces, rims = exchange(mine, theirs, owner_root, gate, work)
    else:
        for share in shares.values():
            work(share)
        pieces = [
            lax.psum(jnp.where(me == owner_root, a, 0).astype(jnp.float32), "pert").astype(a.dtype)
            for h in halves
            for a in h
        ]
        pieces = [a.transpose(1, 0, 2, 3, 4) for a in pieces]
        quarter = slab // 4
        rims = ring(pieces[0][1][:, :, quarter - reach :], pieces[0][0][:, :, :reach]) * 2
    return final(core, pieces, rims, done["terms"], length)


def solution(mesh):
    placed = (
        P("pert", None, "gx", None, None),
        P("pert", None, "gx", None, None),
        P(),
        P("pert"),
        P(),
    )
    return jax.shard_map(
        per_device,
        mesh=mesh,
        in_specs=placed,
        out_specs=P("pert", None, "gx", None, None),
        check_vma=False,
    )
```
